32 devices in a mesh: ctx: 8 (over z, y), shard: 4 (over x, core).
Axes of the slice: x: 2, y: 2, z: 4, core: 2. Of those that a mesh axis runs over, the one named last changes fastest.
Arguments:
- inputs: bfloat16 [4, 2048, 1152], P('shard', 'ctx'), may hold values from -6 to 6
- gain_attn: bfloat16 [1152], P('shard'), may hold values from 0.5 to 1.5
- w_query: bfloat16 [1152, 1152], P('shard'), may hold values from -0.1875 to 0.1875
- w_key: bfloat16 [1152, 384], P('shard'), may hold values from -0.1875 to 0.1875
- w_value: bfloat16 [1152, 384], P('shard'), may hold values from -0.1875 to 0.1875
- w_out: bfloat16 [1152, 1152], P('shard'), may hold values from -3 to 3
- gain_mlp: bfloat16 [1152], P('shard'), may hold values from 0.5 to 1.5
- w_gate: bfloat16 [1152, 3072], P('shard'), may hold values from -0.1875 to 0.1875
- w_up: bfloat16 [1152, 3072], P('shard'), may hold values from -0.1875 to 0.1875
- w_down: bfloat16 [3072, 1152], P('shard'), may hold values from -0.109375 to 0.109375
- cotangent: bfloat16 [4, 2048, 1152], P('shard', 'ctx'), may hold values from -6 to 6
Outputs:
- output: bfloat16 [4, 2048, 1152], P('shard', 'ctx')
- grad_inputs: bfloat16 [4, 2048, 1152], P('shard', 'ctx')
- grad_gain_attn: float32 [1152], P('shard')
- grad_w_query: float32 [1152, 1152], P('shard')
- grad_w_key: float32 [1152, 384], P('shard')
- grad_w_value: float32 [1152, 384], P('shard')
- grad_w_out: float32 [1152, 1152], P('shard')
- grad_gain_mlp: float32 [1152], P('shard')
- grad_w_gate: float32 [1152, 3072], P('shard')
- grad_w_up: float32 [1152, 3072], P('shard')
- grad_w_down: float32 [3072, 1152], P('shard')
The draws below stay inside these ranges and needn't reach their ends.
All inputs are finite; a program needn't handle non-finite values.
Results may differ from the reference program's by a relative error of at most 0.018.
Values may be sent and summed in bfloat16 or wider, within the bound.
No kernel may reach another device: no remote copies, remote signals or barrier semaphores. Data moves between devices by JAX's collectives and lax.ppermute only.
A program may use at most 320 MiB of HBM per device.

```python
import math
import jax
import jax.numpy as jnp
from jax import lax

D = 1152
HEADS = 18
KV_HEADS = 6
HEAD = 64
FF = 3072
BLOCK = 256
SEQS = 4
SEQLEN = 2048
QW = 1152
KVW = 384


def levels(rng, shape, cuts, least, top_value):
    level, own = 1.0, jax.random.fold_in(rng, 6)
    for position, shards_of in cuts:
        heights = jnp.exp(jax.random.uniform(jax.random.fold_in(own, position), (shards_of,), jnp.float32, least / len(cuts), top_value / len(cuts)))
        level = level * jnp.repeat(heights, shape[position] // shards_of).reshape([-1 if axis == position else 1 for axis in range(len(shape))])
    return level


def bell_draw(stream_key, dims, spread, bound, shards=(), held_as=jnp.bfloat16):
    drawn = jax.random.normal(stream_key, dims, jnp.float32) * spread
    if len(shards) > 0:
        drawn = levels(stream_key, dims, shards, -0.22, 0.18) * drawn
    return jnp.clip(drawn, min=-bound, max=bound).astype(held_as)


def setup_inputs(seed: int = 0) -> dict:
    seeds = jax.random.split(jax.random.key(seed), 12)
    return {
        "inputs": bell_draw(seeds[0], (SEQS, SEQLEN, D), 1.0, 6.0, ((0, 4), (1, 8))),
        "gain_attn": jnp.clip(1.0 + 0.1 * jax.random.normal(seeds[1], (D,), jnp.float32), 0.5, 1.5).astype(jnp.bfloat16),
        "w_query": bell_draw(seeds[2], (D, QW), D ** -0.5, 0.1875, ((0, 4),)),
        "w_key": bell_draw(seeds[3], (D, KVW), D ** -0.5, 0.1875, ((0, 4),)),
        "w_value": bell_draw(seeds[4], (D, KVW), D ** -0.5, 0.1875, ((0, 4),)),
        "w_out": bell_draw(seeds[5], (QW, D), (max(D // 256, 1)) ** -0.5, 3.0, ((0, 4),)),
        "gain_mlp": jnp.clip(1.0 + 0.1 * jax.random.normal(seeds[6], (D,), jnp.float32), 0.5, 1.5).astype(jnp.bfloat16),
        "w_gate": bell_draw(seeds[7], (D, FF), D ** -0.5, 0.1875, ((0, 4),)),
        "w_up": bell_draw(seeds[8], (D, FF), D ** -0.5, 0.1875, ((0, 4),)),
        "w_down": bell_draw(seeds[9], (FF, D), FF ** -0.5, 0.109375, ((0, 4),)),
        "cotangent": bell_draw(seeds[10], (SEQS, SEQLEN, D), 1.0, 6.0, ((0, 4), (1, 8))),
    }


EPSILON = 1e-05

@jax.custom_vjp
def low(v):
    return lax.optimization_barrier(v.astype(jnp.bfloat16)).astype(jnp.float32)

@jax.custom_vjp
def low_back(v):
    return v

def low_keep(v):
    return (low(v), None)

def low_pass(kept, grad):
    return (grad,)

def back_keep(v):
    return (v, None)

def back_low(kept, grad):
    return (low(grad),)
low.defvjp(low_keep, low_pass)
low_back.defvjp(back_keep, back_low)

def normalize(values, gain):
    scale = lax.rsqrt(lax.optimization_barrier(jnp.mean(values * values, axis=-1, keepdims=True)) + EPSILON)
    return values * scale * gain

def rotate(values, positions, heads):
    count = values.shape[0]
    width = values.shape[1] // heads
    half = width // 2
    frequency = jnp.exp(jnp.arange(half, dtype=jnp.float32) * (-2.0 * math.log(10000.0) / width))
    angles = positions.astype(jnp.float32)[:, None] * frequency[None, :]
    cosine = jnp.cos(angles)[:, None, :]
    sine = jnp.sin(angles)[:, None, :]
    shaped = values.reshape(count, heads, width)
    first = shaped[..., :half]
    second = shaped[..., half:]
    turned = jnp.concatenate([first * cosine - second * sine, second * cosine + first * sine], axis=-1)
    return turned.reshape(count, heads * width)

def project(left_operand, right_operand):
    return jnp.einsum('pwx,xb->pwb', left_operand, right_operand, precision=lax.Precision.HIGHEST)

def apply_attention(queries, keys, values):
    count = queries.shape[0]
    group = HEADS // KV_HEADS
    block_rows = min(512, count)
    key_heads = keys.reshape(count, KV_HEADS, HEAD)
    value_heads = values.reshape(count, KV_HEADS, HEAD)
    key_index = jnp.arange(count, dtype=jnp.int32) // BLOCK

    def one(pair):
        query_block, start = pair
        query_head_count = query_block.reshape(block_rows, KV_HEADS, group, HEAD)
        raw = jnp.einsum('cngd,rnd->ngcr', query_head_count, key_heads, precision=lax.Precision.HIGHEST) * 0.125
        scores = low_back(raw)
        query_index = (start + jnp.arange(block_rows, dtype=jnp.int32)) // BLOCK
        scores = jnp.where(key_index[None, :] <= query_index[:, None], scores, -jnp.inf)
        top = lax.optimization_barrier(jnp.max(scores, axis=-1))
        log_total = top + jnp.log(lax.optimization_barrier(jnp.sum(jnp.exp(scores - top[..., None]), axis=-1)))
        weights = low(jnp.exp(scores - log_total[..., None]))
        gathered = jnp.einsum('ngcr,rnd->cngd', weights, value_heads, precision=lax.Precision.HIGHEST)
        return gathered.reshape(block_rows, HEADS * HEAD)
    blocks = queries.reshape(count // block_rows, block_rows, HEADS * HEAD)
    starts = jnp.arange(count // block_rows, dtype=jnp.int32) * block_rows
    return lax.map(jax.checkpoint(one), (blocks, starts)).reshape(count, HEADS * HEAD)

def forward(inputs, gain_one, query_mat, key_mat, value_mat, output_matrix, gain_two, gate_mat, up_mat, down_mat):
    positions = jnp.arange(SEQLEN, dtype=jnp.int32)
    hidden = low(normalize(inputs, gain_one))
    query_pre = low_back(project(hidden, query_mat))
    key_pre = low_back(project(hidden, key_mat))
    values = low(low_back(project(hidden, value_mat)))
    queries = low(jax.vmap(lambda part: rotate(part, positions, HEADS))(query_pre))
    keys = low(jax.vmap(lambda part: rotate(part, positions, KV_HEADS))(key_pre))
    attended = lax.map(lambda trio: apply_attention(trio[0], trio[1], trio[2]), (queries, keys, values))
    attended = low(low_back(attended))
    mid = inputs + low_back(project(attended, output_matrix))
    normed = low(normalize(mid, gain_two))
    gate = low_back(project(normed, gate_mat))
    up = low_back(project(normed, up_mat))
    activated = low(jax.nn.silu(gate) * up)
    return mid + low_back(project(activated, down_mat))

def reference(inputs, gain_attn, w_query, w_key, w_value, w_out, gain_mlp, w_gate, w_up, w_down, cotangent):
    floats = (inputs.astype(jnp.float32), gain_attn.astype(jnp.float32), w_query.astype(jnp.float32), w_key.astype(jnp.float32), w_value.astype(jnp.float32), w_out.astype(jnp.float32), gain_mlp.astype(jnp.float32), w_gate.astype(jnp.float32), w_up.astype(jnp.float32), w_down.astype(jnp.float32))
    result, pull = jax.vjp(forward, *floats)
    grads = pull(cotangent.astype(jnp.float32))
    return (result.astype(jnp.bfloat16), grads[0].astype(jnp.bfloat16), grads[1], grads[2], grads[3], grads[4], grads[5], grads[6], grads[7], grads[8], grads[9])
```

```python
import functools
import math

import jax
import jax.numpy as jnp
from jax import lax
from jax.experimental import pallas as pl
from jax.experimental.pallas import tpu as pltpu
from jax.sharding import PartitionSpec as P

HEAD = 64
BLOCK = 256
EPSILON = 1e-05
LANES = 128
F32 = jnp.float32
BF16 = jnp.bfloat16
SCORE_SCALE = math.log2(math.e) * 0.125
NEGATIVE = -1e30
VMEM_BYTES = 44 * 1024 * 1024


def nn(left, right):
    return lax.dot_general(left, right, (((1,), (0,)), ((), ())), preferred_element_type=F32)


def nt(left, right):
    return lax.dot_general(left, right, (((1,), (1,)), ((), ())), preferred_element_type=F32)


def tn(left, right):
    return lax.dot_general(left, right, (((0,), (0,)), ((), ())), preferred_element_type=F32)


def ring_order(count):
    if count % 2:
        return list(range(count))
    return list(range(0, count, 2)) + list(range(count - 1, 0, -2))


def params(**kwargs):
    return pltpu.CompilerParams(vmem_limit_bytes=VMEM_BYTES, **kwargs)


def cost(flops, moved, exps=0):
    return pl.CostEstimate(flops=int(flops), bytes_accessed=int(moved), transcendentals=int(exps))


VMEM_SPEC = pl.BlockSpec(memory_space=pltpu.VMEM)
SMEM_SPEC = pl.BlockSpec(memory_space=pltpu.SMEM)


def swap_halves(tile):
    lane = lax.broadcasted_iota(jnp.int32, tile.shape, 1)
    ahead = pltpu.roll(tile, LANES - HEAD // 2, 1)
    behind = pltpu.roll(tile, HEAD // 2, 1)
    return jnp.where(lane % HEAD < HEAD // 2, ahead, behind)


def assemble(shard, pieces, whole, rows):
    for hop, piece in enumerate(pieces):
        start = pl.multiple_of((shard ^ hop) * rows, 16)
        whole[pl.ds(start, rows), :] = piece[:rows, :]


def keys_kernel(shard_ref, x_ref, gain_ref, cos_ref, sin_ref, *rest, rows, kvw):
    pieces, (hidden_ref, kv_ref, whole) = rest[:-3], rest[-3:]
    x = x_ref[...].astype(F32)
    scale = lax.rsqrt(jnp.mean(x * x, axis=-1, keepdims=True) + EPSILON)
    hidden = (x * scale * gain_ref[...]).astype(BF16)
    hidden_ref[...] = hidden
    assemble(shard_ref[0], pieces, whole, rows)
    pre = nn(hidden, whole[...])
    for start in range(0, kvw, LANES):
        tile = pre[:, start : start + LANES]
        turned = tile * cos_ref[...] + swap_halves(tile) * sin_ref[...]
        kv_ref[:, start : start + LANES] = turned.astype(BF16)
    kv_ref[:, kvw:] = pre[:, kvw:].astype(BF16)


def queries_kernel(shard_ref, hidden_ref, cos_ref, sin_ref, *rest, rows):
    pieces, (query_ref, whole) = rest[:-2], rest[-2:]
    assemble(shard_ref[0], pieces, whole, rows)
    pre = nn(hidden_ref[...], whole[...])
    for start in range(0, pre.shape[1], LANES):
        tile = pre[:, start : start + LANES]
        turned = tile * cos_ref[...] + swap_halves(tile) * sin_ref[...]
        query_ref[:, start : start + LANES] = turned.astype(BF16)


def attend_kernel(
    table_ref,
    q_ref,
    kv_ref,
    x_ref,
    gain_ref,
    *rest,
    rows,
    groups,
    per,
    blocks,
):
    pieces = rest[:-10]
    (
        out_ref,
        attended_ref,
        log_ref,
        mid_ref,
        normed_ref,
        turned_q,
        acc,
        top,
        total,
        whole,
    ) = rest[-10:]
    step = pl.program_id(0)
    last = table_ref[blocks]
    shard = table_ref[blocks + 1]
    count = q_ref.shape[0]
    kvw = groups * HEAD

    @pl.when(step == 0)
    def _():
        for group in range(groups):
            for member in range(per):
                head = group * per + member
                part = q_ref[:, head * HEAD : (head + 1) * HEAD]
                turned_q[group, :, member * count : (member + 1) * count] = part.T
        acc[...] = jnp.zeros_like(acc)
        total[...] = jnp.zeros_like(total)
        top[...] = jnp.full_like(top, NEGATIVE)

    @pl.when(step <= last)
    def _():
        for group in range(groups):
            key = kv_ref[:, group * HEAD : (group + 1) * HEAD]
            value = kv_ref[:, kvw + group * HEAD : kvw + (group + 1) * HEAD]
            scores = nn(key, turned_q[group]) * SCORE_SCALE
            old = top[group : group + 1, :]
            new = jnp.maximum(old, jnp.max(scores, axis=0, keepdims=True))
            shrink = jnp.exp2(old - new)
            probs = jnp.exp2(scores - new)
            top[group : group + 1, :] = new
            total[group : group + 1, :] = total[group : group + 1, :] * shrink + jnp.sum(
                probs, axis=0, keepdims=True
            )
            acc[group] = acc[group] * shrink + tn(value, probs.astype(BF16))

    @pl.when(step == blocks - 1)
    def _():
        for group in range(groups):
            sums = total[group : group + 1, :]
            log_ref[group : group + 1, :] = top[group : group + 1, :] + jnp.log2(sums)
            rowed = acc[group] / sums
            for member in range(per):
                head = group * per + member
                out_ref[:, head * HEAD : (head + 1) * HEAD] = rowed[
                    :, member * count : (member + 1) * count
                ].T
        attended = out_ref[...].astype(BF16)
        attended_ref[...] = attended
        assemble(shard, pieces, whole, rows)
        mid = x_ref[...].astype(F32) + nn(attended, whole[...])
        mid_ref[...] = mid
        scale = lax.rsqrt(jnp.mean(mid * mid, axis=-1, keepdims=True) + EPSILON)
        normed_ref[...] = (mid * scale * gain_ref[...]).astype(BF16)


def attend_back_kernel(
    table_ref,
    q_ref,
    kv_ref,
    out_ref,
    log_ref,
    mid_ref,
    gain_ref,
    cot_ref,
    gn_ref,
    cos_ref,
    sin_ref,
    *rest,
    rows,
    groups,
    per,
    blocks,
):
    pieces = rest[:-13]
    (
        gq_ref,
        gkv_ref,
        branch_ref,
        gmid_ref,
        ggain_ref,
        whole,
        q_rows,
        q_cols,
        d_rows,
        d_cols,
        delta,
        acc,
        flat,
    ) = rest[-13:]
    step = pl.program_id(0)
    last = table_ref[blocks]
    shard = table_ref[blocks + 1]
    count = q_ref.shape[0]
    kvw = groups * HEAD

    @pl.when(step == 0)
    def _():
        mid = mid_ref[...]
        incoming = gn_ref[...]
        gain = gain_ref[...]
        scale = lax.rsqrt(jnp.mean(mid * mid, axis=-1, keepdims=True) + EPSILON)
        weighted = incoming * gain
        inner = jnp.mean(weighted * mid, axis=-1, keepdims=True)
        ggain_ref[...] = jnp.sum(incoming * mid * scale, axis=0, keepdims=True)
        grad_mid = (
            cot_ref[...].astype(F32) + scale * weighted - mid * (scale * scale * scale * inner)
        )
        gmid_ref[...] = grad_mid
        branch = grad_mid.astype(BF16)
        branch_ref[...] = branch
        assemble(shard, pieces, whole, rows)
        flat[...] = nt(branch, whole[...])
        for group in range(groups):
            for member in range(per):
                head = group * per + member
                span = slice(head * HEAD, (head + 1) * HEAD)
                cols = slice(member * count, (member + 1) * count)
                part = q_ref[:, span]
                q_rows[group, cols, :] = part
                q_cols[group, :, cols] = part.T
                grad = flat[:, span].astype(BF16)
                d_rows[group, cols, :] = grad
                d_cols[group, :, cols] = grad.T
                product = grad.astype(F32) * out_ref[:, span]
                delta[group : group + 1, cols] = jnp.sum(product.T, axis=0, keepdims=True)
        acc[...] = jnp.zeros_like(acc)

    @pl.when(step > last)
    def _():
        gkv_ref[...] = jnp.zeros_like(gkv_ref)

    @pl.when(step <= last)
    def _():
        for group in range(groups):
            key_span = slice(group * HEAD, (group + 1) * HEAD)
            value_span = slice(kvw + group * HEAD, kvw + (group + 1) * HEAD)
            key = kv_ref[:, key_span]
            value = kv_ref[:, value_span]
            scores = nn(key, q_cols[group]) * SCORE_SCALE
            probs = jnp.exp2(scores - log_ref[group : group + 1, :])
            grad_probs = nn(value, d_cols[group])
            grad_scores = (probs * (grad_probs - delta[group : group + 1, :])).astype(BF16)
            gkv_ref[:, value_span] = nn(probs.astype(BF16), d_rows[group]).astype(BF16)
            gkv_ref[:, key_span] = (nn(grad_scores, q_rows[group]) * 0.125).astype(BF16)
            acc[group] = acc[group] + tn(key, grad_scores)

    @pl.when(step == blocks - 1)
    def _():
        for group in range(groups):
            for member in range(per):
                head = group * per + member
                flat[:, head * HEAD : (head + 1) * HEAD] = (
                    acc[group, :, member * count : (member + 1) * count].T * 0.125
                )
        for start in range(0, flat.shape[1], LANES):
            tile = flat[:, start : start + LANES]
            turned = tile * cos_ref[...] - swap_halves(tile) * sin_ref[...]
            gq_ref[:, start : start + LANES] = turned.astype(BF16)


def unturn_kernel(grad_ref, cos_ref, sin_ref, out_ref, *, kvw):
    for start in range(0, kvw, LANES):
        tile = grad_ref[:, start : start + LANES].astype(F32)
        turned = tile * cos_ref[...] - swap_halves(tile) * sin_ref[...]
        out_ref[:, start : start + LANES] = turned.astype(BF16)
    out_ref[:, kvw:] = grad_ref[:, kvw:]


def inputs_kernel(shard_ref, gq_ref, gkv_ref, x_ref, gain_ref, gmid_ref, *rest, rows, hops):
    q_pieces = rest[:hops]
    kv_pieces = rest[hops : 2 * hops]
    grad_ref, ggain_ref, whole_q, whole_kv = rest[2 * hops :]
    assemble(shard_ref[0], q_pieces, whole_q, rows)
    assemble(shard_ref[0], kv_pieces, whole_kv, rows)
    incoming = nt(gq_ref[...], whole_q[...]) + nt(gkv_ref[...], whole_kv[...])
    x = x_ref[...].astype(F32)
    scale = lax.rsqrt(jnp.mean(x * x, axis=-1, keepdims=True) + EPSILON)
    weighted = incoming * gain_ref[...]
    inner = jnp.mean(weighted * x, axis=-1, keepdims=True)
    ggain_ref[...] = jnp.sum(incoming * x * scale, axis=0, keepdims=True)
    grad = gmid_ref[...] + scale * weighted - x * (scale * scale * scale * inner)
    grad_ref[...] = grad.astype(BF16)


def weight_grad_kernel(shard_ref, left_ref, right_ref, *rest, rows):
    outs, full = rest[:-1], rest[-1]
    full[...] = tn(left_ref[...], right_ref[...])
    for hop, out in enumerate(outs):
        start = pl.multiple_of((shard_ref[0] ^ hop) * rows, 8)
        out[...] = full[pl.ds(start, rows), :].astype(BF16)


def on_device(
    inputs,
    gain_attn,
    w_query,
    w_key,
    w_value,
    w_out,
    gain_mlp,
    w_gate,
    w_up,
    w_down,
    cotangent,
    *,
    n_ctx,
    n_shard,
):
    x = inputs[0]
    cot = cotangent[0]
    count, width = x.shape
    rows = w_query.shape[0]
    qw = w_query.shape[1]
    kvw = w_key.shape[1]
    ff = w_gate.shape[1]
    ff_own = w_down.shape[0]
    groups = kvw // HEAD
    per = qw // kvw
    assert count == BLOCK and n_shard == 4 and ff_own * n_shard == ff
    order = ring_order(n_ctx)
    places = [order.index(index) for index in range(n_ctx)]
    shard = lax.axis_index("shard")
    ctx = lax.axis_index("ctx")
    shard_arr = shard.astype(jnp.int32)[None]
    place = jnp.array(places, jnp.int32)[ctx]
    table = jnp.concatenate(
        [jnp.array(places, jnp.int32), jnp.stack([ctx, shard]).astype(jnp.int32)]
    )

    def hop(value, distance):
        pairs = [(index, index ^ distance) for index in range(n_shard)]
        return lax.ppermute(value, "shard", pairs)

    def gather(value):
        far = hop(value, 2)
        near = hop(value, 1)
        return [value, near, far, hop(far, 1)]

    def reduce(blocks):
        third = hop(blocks[3], 1)
        first = hop(blocks[1], 1)
        across = (blocks[2].astype(F32) + third.astype(F32)).astype(BF16)
        far = hop(across, 2)
        return blocks[0].astype(F32) + first.astype(F32) + far.astype(F32)

    def after(value, done):
        return lax.optimization_barrier((value, done))[0]

    def scatter(value):
        return lax.psum_scatter(
            value, "ctx", scatter_dimension=0, axis_index_groups=[order], tiled=False
        )

    def collect(value):
        return lax.all_gather(value, "ctx", axis=0, axis_index_groups=[order], tiled=True)

    lane = jnp.arange(LANES, dtype=jnp.int32)
    frequency = jnp.exp(
        (lane % (HEAD // 2)).astype(F32) * (-2.0 * math.log(10000.0) / HEAD)
    )
    positions = (ctx * count + jnp.arange(count, dtype=jnp.int32)).astype(F32)
    angles = positions[:, None] * frequency[None, :]
    cosine = jnp.cos(angles)
    sine = jnp.where(lane % HEAD < HEAD // 2, -1.0, 1.0)[None, :] * jnp.sin(angles)

    gains = jnp.concatenate([gain_attn, gain_mlp])
    gain_rows = jnp.zeros((16, 2 * kvw), BF16).at[0, : 2 * rows].set(gains)
    kv_own = jnp.concatenate([jnp.concatenate([w_key, w_value], axis=1), gain_rows], axis=0)
    kv_weights = gather(kv_own)
    q_weights = gather(after(w_query, kv_weights[2]))
    out_weights = gather(after(w_out, q_weights[2]))
    stacked = jnp.stack([piece[rows, : 2 * rows] for piece in kv_weights]).astype(F32)
    owner = jnp.arange(n_shard, dtype=jnp.int32)[:, None] == (
        jnp.arange(n_shard, dtype=jnp.int32)[None, :] ^ shard
    )
    gains_full = jnp.sum(jnp.where(owner[:, :, None], stacked[None], 0.0), axis=1)
    gain_one = gains_full[:, :rows].reshape(1, width)
    gain_two = gains_full[:, rows:].reshape(1, width)

    hidden, kv = pl.pallas_call(
        functools.partial(keys_kernel, rows=rows, kvw=kvw),
        out_shape=(
            jax.ShapeDtypeStruct((count, width), BF16),
            jax.ShapeDtypeStruct((count, 2 * kvw), BF16),
        ),
        in_specs=[SMEM_SPEC] + [VMEM_SPEC] * (4 + n_shard),
        out_specs=(VMEM_SPEC, VMEM_SPEC),
        scratch_shapes=[pltpu.VMEM((width, 2 * kvw), BF16)],
        compiler_params=params(),
        cost_estimate=cost(4 * count * width * kvw, 8e6),
        name="keys",
    )(shard_arr, x, gain_one, cosine, sine, *kv_weights)
    all_kv = collect(kv)

    queries = pl.pallas_call(
        functools.partial(queries_kernel, rows=rows),
        out_shape=jax.ShapeDtypeStruct((count, qw), BF16),
        in_specs=[SMEM_SPEC] + [VMEM_SPEC] * (3 + n_shard),
        out_specs=VMEM_SPEC,
        scratch_shapes=[pltpu.VMEM((width, qw), BF16)],
        compiler_params=params(),
        cost_estimate=cost(2 * count * width * qw, 8e6),
        name="queries",
    )(shard_arr, hidden, cosine, sine, *q_weights)

    def columns(peer):
        start = peer * ff_own
        return jnp.concatenate(
            [
                lax.dynamic_slice_in_dim(w_gate, start, ff_own, 1),
                lax.dynamic_slice_in_dim(w_up, start, ff_own, 1),
            ],
            axis=1,
        )

    parts = [columns(shard)]
    done = out_weights[2]
    for distance in range(1, n_shard):
        parts.append(hop(after(columns(shard ^ distance), done), distance))
    gate_mat = jnp.zeros((width, ff_own), BF16)
    up_mat = jnp.zeros((width, ff_own), BF16)
    for distance, part in enumerate(parts):
        start = (shard ^ distance) * rows
        gate_mat = lax.dynamic_update_slice_in_dim(gate_mat, part[:, :ff_own], start, 0)
        up_mat = lax.dynamic_update_slice_in_dim(up_mat, part[:, ff_own:], start, 0)
    all_cot = jnp.concatenate(gather(after(cot, parts[3])), axis=0)

    blocks = n_ctx
    shared = dict(rows=rows, groups=groups, per=per, blocks=blocks)
    fixed = lambda *shape: pl.BlockSpec(shape, lambda step, table: (0,) * len(shape))
    kv_spec = pl.BlockSpec(
        (count, 2 * kvw), lambda step, table: (table[jnp.minimum(step, table[blocks])], 0)
    )
    once = lambda *shape: pl.BlockSpec(
        shape, lambda step, table: (0,) * len(shape), pipeline_mode=pl.Buffered(1)
    )
    weight_specs = [once(rows, width)] * n_shard
    out32, attended, log_total, mid, normed = pl.pallas_call(
        functools.partial(attend_kernel, **shared),
        out_shape=(
            jax.ShapeDtypeStruct((count, qw), F32),
            jax.ShapeDtypeStruct((count, qw), BF16),
            jax.ShapeDtypeStruct((8, per * count), F32),
            jax.ShapeDtypeStruct((count, width), F32),
            jax.ShapeDtypeStruct((count, width), BF16),
        ),
        grid_spec=pltpu.PrefetchScalarGridSpec(
            num_scalar_prefetch=1,
            grid=(blocks,),
            in_specs=[once(count, qw), kv_spec, once(count, width), once(1, width)]
            + weight_specs,
            out_specs=[
                fixed(count, qw),
                fixed(count, qw),
                fixed(8, per * count),
                fixed(count, width),
                fixed(count, width),
            ],
            scratch_shapes=[
                pltpu.VMEM((groups, HEAD, per * count), BF16),
                pltpu.VMEM((groups, HEAD, per * count), F32),
                pltpu.VMEM((8, per * count), F32),
                pltpu.VMEM((8, per * count), F32),
                pltpu.VMEM((qw, width), BF16),
            ],
        ),
        compiler_params=params(),
        cost_estimate=cost(4 * count * count * blocks * qw, 12e6, count * count * blocks * groups * per),
        name="attend",
    )(table, queries, all_kv, x, gain_two, *out_weights)

    all_normed = jnp.concatenate(gather(normed), axis=0)
    gate = nn(all_normed, gate_mat)
    up = nn(all_normed, up_mat)
    activated = (jax.nn.silu(gate) * up).astype(BF16)
    grad_down = tn(activated, all_cot).astype(BF16)
    grad_activated = nt(all_cot, w_down)
    sigmoid = jax.nn.sigmoid(gate)
    grad_gate = (grad_activated * up * (sigmoid * (1.0 + gate * (1.0 - sigmoid)))).astype(BF16)
    grad_up = (grad_activated * (gate * sigmoid)).astype(BF16)
    part_normed = (nt(grad_gate, gate_mat) + nt(grad_up, up_mat)).astype(BF16)
    grad_normed = reduce([part_normed[k * count : (k + 1) * count] for k in range(n_shard)])
    part_out = nn(activated, w_down).astype(BF16)
    part_out = after(part_out, grad_normed)
    output = (mid + reduce([part_out[k * count : (k + 1) * count] for k in range(n_shard)])).astype(
        BF16
    )[None]

    per_shard = n_ctx // n_shard
    tile = ff_own // per_shard

    def tiles(grad):
        cut = grad.astype(BF16).reshape(n_shard, rows, per_shard, tile).transpose(0, 2, 1, 3)
        return jnp.roll(cut, shard, axis=0).reshape(n_ctx, rows, tile)

    grad_gate_mat = tiles(tn(all_normed, grad_gate))
    grad_up_mat = tiles(tn(all_normed, grad_up))
    down_rows = ff_own // n_ctx
    splits = 3
    down_tiles = (
        grad_down.reshape(n_ctx, down_rows, splits, width // splits)
        .transpose(0, 2, 1, 3)
        .reshape(n_ctx, splits * down_rows, width // splits)
    )
    gate_up = scatter(jnp.concatenate([grad_gate_mat, grad_up_mat], axis=1))
    pairs = []
    for index in range(n_ctx):
        for source in range(n_shard):
            target = (places[index] // per_shard - source) % n_shard
            pairs.append((index * n_shard + source, index * n_shard + target))
    gate_up = lax.ppermute(gate_up, ("ctx", "shard"), pairs)
    down_sum = collect(scatter(down_tiles)[None])
    gate_up = collect(gate_up[None])

    def untile(part):
        back = jnp.roll(part.reshape(n_shard, per_shard, rows, tile), -shard, axis=0)
        return back.reshape(n_ctx, rows, tile).transpose(1, 0, 2).reshape(rows, ff).astype(F32)

    grad_w_gate = untile(gate_up[:, :rows])
    grad_w_up = untile(gate_up[:, rows:])
    grad_w_down = (
        down_sum.reshape(n_ctx, splits, down_rows, width // splits)
        .transpose(0, 2, 1, 3)
        .reshape(ff_own, width)
        .astype(F32)
    )

    place_spec = pl.BlockSpec((count, 2 * kvw), lambda step, table: (table[step], 0))
    grad_query, grad_kv, branch, grad_mid, gain_two_part = pl.pallas_call(
        functools.partial(attend_back_kernel, **shared),
        out_shape=(
            jax.ShapeDtypeStruct((count, qw), BF16),
            jax.ShapeDtypeStruct((blocks * count, 2 * kvw), BF16),
            jax.ShapeDtypeStruct((count, width), BF16),
            jax.ShapeDtypeStruct((count, width), F32),
            jax.ShapeDtypeStruct((1, width), F32),
        ),
        grid_spec=pltpu.PrefetchScalarGridSpec(
            num_scalar_prefetch=1,
            grid=(blocks,),
            in_specs=[
                once(count, qw),
                kv_spec,
                once(count, qw),
                once(8, per * count),
                once(count, width),
                once(1, width),
                once(count, width),
                once(count, width),
                once(count, LANES),
                once(count, LANES),
            ]
            + weight_specs,
            out_specs=[
                fixed(count, qw),
                place_spec,
                fixed(count, width),
                fixed(count, width),
                fixed(1, width),
            ],
            scratch_shapes=[
                pltpu.VMEM((qw, width), BF16),
                pltpu.VMEM((groups, per * count, HEAD), BF16),
                pltpu.VMEM((groups, HEAD, per * count), BF16),
                pltpu.VMEM((groups, per * count, HEAD), BF16),
                pltpu.VMEM((groups, HEAD, per * count), BF16),
                pltpu.VMEM((8, per * count), F32),
                pltpu.VMEM((groups, HEAD, per * count), F32),
                pltpu.VMEM((count, qw), F32),
            ],
        ),
        compiler_params=params(),
        cost_estimate=cost(10 * count * count * blocks * qw, 14e6, count * count * blocks * groups * per),
        name="attend_back",
    )(
        table,
        queries,
        all_kv,
        out32,
        log_total,
        mid,
        gain_two,
        cot,
        grad_normed,
        cosine,
        sine,
        *out_weights,
    )
    own_kv = scatter(grad_kv.reshape(n_ctx, count, 2 * kvw))

    def weight_grad(left, right, name):
        columns_out = right.shape[1]
        return pl.pallas_call(
            functools.partial(weight_grad_kernel, rows=rows),
            out_shape=(jax.ShapeDtypeStruct((rows, columns_out), BF16),) * n_shard,
            in_specs=[SMEM_SPEC, VMEM_SPEC, VMEM_SPEC],
            out_specs=(VMEM_SPEC,) * n_shard,
            scratch_shapes=[pltpu.VMEM((left.shape[1], columns_out), F32)],
            compiler_params=params(),
            cost_estimate=cost(2 * count * left.shape[1] * columns_out, 8e6),
            name=name,
        )(shard_arr, left, right)

    sum_out = reduce(weight_grad(attended, branch, "grad_out"))
    sum_query = reduce(weight_grad(hidden, grad_query, "grad_query"))

    grad_kv_pre = pl.pallas_call(
        functools.partial(unturn_kernel, kvw=kvw),
        out_shape=jax.ShapeDtypeStruct((count, 2 * kvw), BF16),
        in_specs=[VMEM_SPEC] * 3,
        out_specs=VMEM_SPEC,
        compiler_params=params(),
        cost_estimate=cost(4 * count * kvw, 1e6),
        name="unturn",
    )(own_kv, cosine, sine)
    sum_kv = reduce(weight_grad(hidden, grad_kv_pre, "grad_kv"))

    merged = jnp.concatenate([sum_query, sum_out, sum_kv], axis=1).astype(BF16)
    span = merged.shape[1] // n_ctx
    merged = merged.reshape(rows, n_ctx, span).transpose(1, 0, 2)
    merged = collect(scatter(merged)[None])
    merged = merged.transpose(1, 0, 2).reshape(rows, 2 * qw + 2 * kvw)
    grad_w_query = merged[:, :qw].astype(F32)
    grad_w_out = merged[:, qw : 2 * qw].astype(F32)
    grad_w_key = merged[:, 2 * qw : 2 * qw + kvw].astype(F32)
    grad_w_value = merged[:, 2 * qw + kvw :].astype(F32)

    grad_x, gain_one_part = pl.pallas_call(
        functools.partial(inputs_kernel, rows=rows, hops=n_shard),
        out_shape=(
            jax.ShapeDtypeStruct((count, width), BF16),
            jax.ShapeDtypeStruct((1, width), F32),
        ),
        in_specs=[SMEM_SPEC] + [VMEM_SPEC] * (5 + 2 * n_shard),
        out_specs=(VMEM_SPEC, VMEM_SPEC),
        scratch_shapes=[pltpu.VMEM((width, qw), BF16), pltpu.VMEM((width, 2 * kvw), BF16)],
        compiler_params=params(),
        cost_estimate=cost(2 * count * width * (qw + 2 * kvw), 12e6),
        name="grad_inputs",
    )(shard_arr, grad_query, grad_kv_pre, x, gain_one, grad_mid, *q_weights, *kv_weights)

    gain_parts = jnp.concatenate([gain_one_part, gain_two_part], axis=0)
    distance = 1
    while distance < n_shard:
        gain_parts = gain_parts + hop(gain_parts, distance)
        distance *= 2
    distance = 1
    while distance < n_ctx:
        gain_parts = gain_parts + lax.ppermute(
            gain_parts, "ctx", [(index, index ^ distance) for index in range(n_ctx)]
        )
        distance *= 2
    own_gains = lax.dynamic_slice_in_dim(gain_parts, shard * rows, rows, 1)

    return (
        output,
        grad_x[None],
        own_gains[0],
        grad_w_query,
        grad_w_key,
        grad_w_value,
        grad_w_out,
        own_gains[1],
        grad_w_gate,
        grad_w_up,
        grad_w_down,
    )


def solution(mesh):
    tokens = P("shard", "ctx", None)
    split = P("shard", None)
    gain = P("shard")
    placed = (tokens, gain, split, split, split, split, gain, split, split, split, tokens)
    return jax.shard_map(
        functools.partial(on_device, n_ctx=mesh.shape["ctx"], n_shard=mesh.shape["shard"]),
        mesh=mesh,
        in_specs=placed,
        out_specs=(tokens, tokens, gain, split, split, split, split, gain, split, split, split),
        check_vma=False,
    )
```

```python
import functools
import math

import jax
import jax.numpy as jnp
from jax import lax
from jax.experimental import pallas as pl
from jax.experimental.pallas import tpu as pltpu
from jax.sharding import PartitionSpec as P

HEAD = 64
BLOCK = 256
EPSILON = 1e-05
LANES = 128
F32 = jnp.float32
BF16 = jnp.bfloat16
SCORE_SCALE = math.log2(math.e) * 0.125
NEGATIVE = -1e30
VMEM_BYTES = 30 * 1024 * 1024


def nn(left, right):
    return lax.dot_general(left, right, (((1,), (0,)), ((), ())), preferred_element_type=F32)


def nt(left, right):
    return lax.dot_general(left, right, (((1,), (1,)), ((), ())), preferred_element_type=F32)


def tn(left, right):
    return lax.dot_general(left, right, (((0,), (0,)), ((), ())), preferred_element_type=F32)


def ring_order(count):
    if count % 2:
        return list(range(count))
    return list(range(0, count, 2)) + list(range(count - 1, 0, -2))


def params(limit=VMEM_BYTES):
    return pltpu.CompilerParams(vmem_limit_bytes=limit)


def cost(flops, moved, exps=0):
    return pl.CostEstimate(flops=int(flops), bytes_accessed=int(moved), transcendentals=int(exps))


VMEM_SPEC = pl.BlockSpec(memory_space=pltpu.VMEM)
HBM_SPEC = pl.BlockSpec(memory_space=pltpu.HBM)
SMEM_SPEC = pl.BlockSpec(memory_space=pltpu.SMEM)


def swap_halves(tile):
    lane = lax.broadcasted_iota(jnp.int32, tile.shape, 1)
    ahead = pltpu.roll(tile, LANES - HEAD // 2, 1)
    behind = pltpu.roll(tile, HEAD // 2, 1)
    return jnp.where(lane % HEAD < HEAD // 2, ahead, behind)


def fetches(starts, pieces, whole, sems, sizes):
    copies = []
    for index, (piece, size) in enumerate(zip(pieces, sizes)):
        start = pl.multiple_of(starts[index], 16)
        copies.append(
            pltpu.make_async_copy(
                piece.at[pl.ds(0, size), :], whole.at[pl.ds(start, size), :], sems.at[index]
            )
        )
    return copies


def keys_kernel(starts_ref, x_ref, cos_ref, sin_ref, *rest, sizes, kvw):
    pieces = rest[: len(sizes)]
    hidden_ref, kv_ref, one_ref, two_ref, whole, bands, sems, band_sems = rest[len(sizes) :]
    copies = fetches(starts_ref, pieces, whole, sems, sizes)
    rows = sizes[0]
    for index, piece in enumerate(pieces):
        band = pltpu.make_async_copy(
            piece.at[pl.ds(rows, 16), :], bands.at[index], band_sems.at[index]
        )
        band.start()
        copies[index].start()
    x = x_ref[...].astype(F32)
    scale = lax.rsqrt(jnp.mean(x * x, axis=-1, keepdims=True) + EPSILON)
    width = x.shape[1]
    ones = jnp.zeros((8, width), F32)
    twos = jnp.zeros((8, width), F32)
    for index, piece in enumerate(pieces):
        pltpu.make_async_copy(
            piece.at[pl.ds(rows, 16), :], bands.at[index], band_sems.at[index]
        ).wait()
        band = bands[index].astype(F32)[:8, :]
        blank = jnp.zeros((8, width - rows), F32)
        first = jnp.concatenate([band[:, :rows], blank], axis=1)
        second = jnp.concatenate([band[:, rows : 2 * rows], blank], axis=1)
        ones = ones + pltpu.roll(first, starts_ref[index], 1)
        twos = twos + pltpu.roll(second, starts_ref[index], 1)
    one_ref[...] = ones[:1, :]
    two_ref[...] = twos[:1, :]
    hidden = (x * scale * ones[:1, :]).astype(BF16)
    hidden_ref[...] = hidden
    for copy in copies:
        copy.wait()
    pre = nn(hidden, whole[...])
    for start in range(0, kvw, LANES):
        tile = pre[:, start : start + LANES]
        turned = tile * cos_ref[...] + swap_halves(tile) * sin_ref[...]
        kv_ref[:, start : start + LANES] = turned.astype(BF16)
    kv_ref[:, kvw:] = pre[:, kvw:].astype(BF16)


def queries_kernel(starts_ref, hidden_ref, cos_ref, sin_ref, *rest, sizes):
    pieces = rest[: len(sizes)]
    query_ref, whole, sems = rest[len(sizes) :]
    copies = fetches(starts_ref, pieces, whole, sems, sizes)
    for copy in copies:
        copy.start()
    for copy in copies:
        copy.wait()
    pre = nn(hidden_ref[...], whole[...])
    for start in range(0, pre.shape[1], LANES):
        tile = pre[:, start : start + LANES]
        turned = tile * cos_ref[...] + swap_halves(tile) * sin_ref[...]
        query_ref[:, start : start + LANES] = turned.astype(BF16)


def attend_kernel(
    table_ref,
    q_ref,
    kv_ref,
    x_ref,
    gain_ref,
    *rest,
    sizes,
    groups,
    per,
    blocks,
):
    pieces = rest[:-13]
    (
        out_ref,
        attended_ref,
        log_ref,
        mid_ref,
        normed_ref,
        cols_ref,
        acc,
        top,
        total,
        whole,
        scores,
        tall,
        sems,
    ) = rest[-13:]
    step = pl.program_id(0)
    last = table_ref[blocks]
    starts = [table_ref[blocks + 1 + index] for index in range(len(sizes))]
    count = q_ref.shape[0]
    kvw = groups * HEAD

    @pl.when(step == 0)
    def _():
        for copy in fetches(starts, pieces, whole, sems, sizes):
            copy.start()
        turned = q_ref[...].T
        for group in range(groups):
            for member in range(per):
                head = group * per + member
                cols_ref[group, :, member * count : (member + 1) * count] = turned[
                    head * HEAD : (head + 1) * HEAD, :
                ]
        acc[...] = jnp.zeros_like(acc)
        total[...] = jnp.zeros_like(total)
        top[...] = jnp.full_like(top, NEGATIVE)

    @pl.when(step <= last)
    def _():
        def score(group):
            key = kv_ref[:, group * HEAD : (group + 1) * HEAD]
            scores[group % 2] = nn(key, cols_ref[group])

        score(0)
        for group in range(groups):
            if group + 1 < groups:
                score(group + 1)
            value = kv_ref[:, kvw + group * HEAD : kvw + (group + 1) * HEAD]
            raw = scores[group % 2]
            old = top[group : group + 1, :]
            new = jnp.maximum(old, jnp.max(raw, axis=0, keepdims=True))
            shrink = jnp.exp2((old - new) * SCORE_SCALE)
            probs = jnp.exp2((raw - new) * SCORE_SCALE)
            top[group : group + 1, :] = new
            total[group : group + 1, :] = total[group : group + 1, :] * shrink + jnp.sum(
                probs, axis=0, keepdims=True
            )
            acc[group] = acc[group] * shrink + tn(value, probs.astype(BF16))

    @pl.when(step == blocks - 1)
    def _():
        for group in range(groups):
            sums = total[group : group + 1, :]
            log_ref[group : group + 1, :] = top[
                group : group + 1, :
            ] * SCORE_SCALE + jnp.log2(sums)
            rowed = acc[group] / sums
            for member in range(per):
                head = group * per + member
                tall[head * HEAD : (head + 1) * HEAD, :] = rowed[
                    :, member * count : (member + 1) * count
                ]
        out_ref[...] = tall[...]
        attended = tall[...].astype(BF16).T
        attended_ref[...] = attended
        for copy in fetches(starts, pieces, whole, sems, sizes):
            copy.wait()
        mid = x_ref[...].astype(F32) + nn(attended, whole[...])
        mid_ref[...] = mid
        scale = lax.rsqrt(jnp.mean(mid * mid, axis=-1, keepdims=True) + EPSILON)
        normed_ref[...] = (mid * scale * gain_ref[...]).astype(BF16)


def attend_back_kernel(
    table_ref,
    q_ref,
    kv_ref,
    cols_ref,
    out_ref,
    log_ref,
    mid_ref,
    gain_ref,
    cot_ref,
    gn_ref,
    cos_ref,
    sin_ref,
    *rest,
    sizes,
    groups,
    per,
    blocks,
):
    pieces = rest[:-14]
    (
        gq_ref,
        gkv_ref,
        branch_ref,
        gmid_ref,
        ggain_ref,
        whole,
        q_rows,
        d_rows,
        d_cols,
        delta,
        acc,
        probs_all,
        tall,
        sems,
    ) = rest[-14:]
    step = pl.program_id(0)
    last = table_ref[blocks]
    starts = [table_ref[blocks + 1 + index] for index in range(len(sizes))]
    count = q_ref.shape[0]
    kvw = groups * HEAD

    @pl.when(step == 0)
    def _():
        copies = fetches(starts, pieces, whole, sems, sizes)
        for copy in copies:
            copy.start()
        mid = mid_ref[...]
        incoming = gn_ref[...]
        gain = gain_ref[...]
        scale = lax.rsqrt(jnp.mean(mid * mid, axis=-1, keepdims=True) + EPSILON)
        weighted = incoming * gain
        inner = jnp.mean(weighted * mid, axis=-1, keepdims=True)
        ggain_ref[...] = jnp.sum(incoming * mid * scale, axis=0, keepdims=True)
        grad_mid = (
            cot_ref[...].astype(F32) + scale * weighted - mid * (scale * scale * scale * inner)
        )
        gmid_ref[...] = grad_mid
        branch = grad_mid.astype(BF16)
        branch_ref[...] = branch
        for copy in copies:
            copy.wait()
        grads = nt(branch, whole[...]).astype(BF16)
        turned = grads.T
        tall[...] = turned.astype(F32) * out_ref[...]
        for group in range(groups):
            for member in range(per):
                head = group * per + member
                span = slice(head * HEAD, (head + 1) * HEAD)
                cols = slice(member * count, (member + 1) * count)
                q_rows[group, cols, :] = q_ref[:, span]
                d_rows[group, cols, :] = grads[:, span]
                d_cols[group, :, cols] = turned[span, :]
                delta[group : group + 1, cols] = jnp.sum(tall[span, :], axis=0, keepdims=True)
        acc[...] = jnp.zeros_like(acc)

    @pl.when(step > last)
    def _():
        gkv_ref[...] = jnp.zeros_like(gkv_ref)

    @pl.when(step <= last)
    def _():
        def spans(group):
            return (
                slice(group * HEAD, (group + 1) * HEAD),
                slice(kvw + group * HEAD, kvw + (group + 1) * HEAD),
            )

        def score(group):
            key_span, value_span = spans(group)
            probs_all[group % 2, 0] = nn(kv_ref[:, key_span], cols_ref[group])
            probs_all[group % 2, 1] = nn(kv_ref[:, value_span], d_cols[group])

        score(0)
        for group in range(groups):
            if group + 1 < groups:
                score(group + 1)
            key_span, value_span = spans(group)
            probs = jnp.exp2(
                probs_all[group % 2, 0] * SCORE_SCALE - log_ref[group : group + 1, :]
            )
            grad_scores = (
                probs * (probs_all[group % 2, 1] - delta[group : group + 1, :])
            ).astype(BF16)
            gkv_ref[:, value_span] = nn(probs.astype(BF16), d_rows[group]).astype(BF16)
            gkv_ref[:, key_span] = (nn(grad_scores, q_rows[group]) * 0.125).astype(BF16)
            acc[group] = acc[group] + tn(kv_ref[:, key_span], grad_scores)

    @pl.when(step == blocks - 1)
    def _():
        for group in range(groups):
            for member in range(per):
                head = group * per + member
                tall[head * HEAD : (head + 1) * HEAD, :] = (
                    acc[group, :, member * count : (member + 1) * count] * 0.125
                )
        for start in range(0, tall.shape[0], LANES):
            tile = tall[start : start + LANES, :].T
            turned = tile * cos_ref[...] - swap_halves(tile) * sin_ref[...]
            gq_ref[:, start : start + LANES] = turned.astype(BF16)


def kv_back_kernel(starts_ref, grad_ref, cos_ref, sin_ref, hidden_ref, out_ref, *rest, kvw):
    outs, full = rest[:-1], rest[-1]
    for start in range(0, kvw, LANES):
        tile = grad_ref[:, start : start + LANES].astype(F32)
        turned = tile * cos_ref[...] - swap_halves(tile) * sin_ref[...]
        out_ref[:, start : start + LANES] = turned.astype(BF16)
    out_ref[:, kvw:] = grad_ref[:, kvw:]
    full[...] = tn(hidden_ref[...], out_ref[...])
    for index, out in enumerate(outs):
        start = pl.multiple_of(starts_ref[index], 8)
        out[...] = full[pl.ds(start, out.shape[0]), :].astype(BF16)


def stack_kernel(*refs):
    parts, out_ref = refs[:-1], refs[-1]
    tile = out_ref.shape[1]
    row = 0
    for index in range(0, len(parts), 3):
        first, second, third = parts[index : index + 3]
        rows, columns = first.shape
        for start in range(0, columns, tile):
            span = slice(start, start + tile)
            total = (
                first[:, span].astype(F32) + second[:, span].astype(F32)
            ) + third[:, span].astype(F32)
            out_ref[row : row + rows, :] = total.astype(BF16)
            row += rows


def build_kernel(starts_ref, own_ref, near_ref, far_ref, gate_ref, up_ref, sems, *, half, lanes):
    rows = own_ref.shape[0]
    width = gate_ref.shape[1]
    copies = []

    def place(source, row, column, height, breadth):
        target = gate_ref if column < width else up_ref
        column = column % width
        copies.append(
            pltpu.make_async_copy(
                source,
                target.at[pl.ds(pl.multiple_of(row, 16), height), pl.ds(column, breadth)],
                sems.at[len(copies)],
            )
        )

    for index, piece in enumerate((own_ref, near_ref)):
        for column in (0, width):
            place(piece.at[:, pl.ds(column, width)], starts_ref[index], column, rows, width)
    for spot in range(far_ref.shape[0]):
        for index in range(2):
            place(
                far_ref.at[spot, pl.ds(index * half, half), :],
                starts_ref[2 + index] + (spot % 2) * half,
                (spot // 2) * lanes,
                half,
                lanes,
            )
    for copy in copies:
        copy.start()
    for copy in copies:
        copy.wait()


def inputs_kernel(
    q_starts, kv_starts, gq_ref, gkv_ref, x_ref, gain_ref, gmid_ref, *rest, q_sizes, kv_sizes
):
    q_pieces = rest[: len(q_sizes)]
    kv_pieces = rest[len(q_sizes) : len(q_sizes) + len(kv_sizes)]
    grad_ref, ggain_ref, whole_q, whole_kv, q_sems, kv_sems = rest[
        len(q_sizes) + len(kv_sizes) :
    ]
    copies = fetches(q_starts, q_pieces, whole_q, q_sems, q_sizes)
    copies += fetches(kv_starts, kv_pieces, whole_kv, kv_sems, kv_sizes)
    for copy in copies:
        copy.start()
    for copy in copies:
        copy.wait()
    incoming = nt(gq_ref[...], whole_q[...]) + nt(gkv_ref[...], whole_kv[...])
    x = x_ref[...].astype(F32)
    scale = lax.rsqrt(jnp.mean(x * x, axis=-1, keepdims=True) + EPSILON)
    weighted = incoming * gain_ref[...]
    inner = jnp.mean(weighted * x, axis=-1, keepdims=True)
    ggain_ref[...] = jnp.sum(incoming * x * scale, axis=0, keepdims=True)
    grad = gmid_ref[...] + scale * weighted - x * (scale * scale * scale * inner)
    grad_ref[...] = grad.astype(BF16)


def weight_grad_kernel(starts_ref, left_ref, right_ref, *rest):
    outs, (left, right, full, sems) = rest[:-4], rest[-4:]
    copies = [
        pltpu.make_async_copy(left_ref, left, sems.at[0]),
        pltpu.make_async_copy(right_ref, right, sems.at[1]),
    ]
    for copy in copies:
        copy.start()
    for copy in copies:
        copy.wait()
    full[...] = tn(left[...], right[...])
    for index, out in enumerate(outs):
        start = pl.multiple_of(starts_ref[index], 8)
        out[...] = full[pl.ds(start, out.shape[0]), :].astype(BF16)


def feed_grads_kernel(
    shard_ref, normed_ref, gate_ref, up_ref, act_ref, cot_ref, out_ref, turned, *, rows, per_shard
):
    shards = turned.shape[0] // rows
    tile = out_ref.shape[2]
    turned[...] = normed_ref[...].T

    def row_block(index, carry):
        left = turned[pl.ds(pl.multiple_of(index * rows, 16), rows), :]
        place = lax.rem(index + shard_ref[0], shards) * per_shard
        for slot, ref in ((0, gate_ref), (1, up_ref)):
            grad = nn(left, ref[...])
            for half in range(per_shard):
                out_ref[place + half, slot * rows : (slot + 1) * rows, :] = grad[
                    :, half * tile : (half + 1) * tile
                ].astype(BF16)
        return carry

    lax.fori_loop(0, shards, row_block, 0)
    own = act_ref.shape[1]
    places = out_ref.shape[0]
    band = own // places
    turned[:own, :] = act_ref[...].T

    def down_block(index, carry):
        left = turned[pl.ds(pl.multiple_of(index * 2 * band, 16), 2 * band), :]
        grad = nn(left, cot_ref[...])
        for part in range(2):
            for split in range(grad.shape[1] // tile):
                start = 2 * rows + split * band
                out_ref[2 * index + part, start : start + band, :] = grad[
                    part * band : (part + 1) * band, split * tile : (split + 1) * tile
                ].astype(BF16)
        return carry

    lax.fori_loop(0, places // 2, down_block, 0)


def widen_kernel(
    shard_ref,
    gate_up_ref,
    down_in_ref,
    mixed_ref,
    gate_ref,
    up_ref,
    down_ref,
    query_ref,
    out_ref,
    stack,
    *,
    rows,
):
    step = pl.program_id(0)
    tile = gate_ref.shape[1]
    band = down_ref.shape[0]
    share = mixed_ref.shape[1]
    gate_ref[...] = gate_up_ref[0, :rows, :].astype(F32)
    up_ref[...] = gate_up_ref[0, rows:, :].astype(F32)
    for split in range(down_ref.shape[1] // tile):
        down_ref[:, split * tile : (split + 1) * tile] = down_in_ref[
            0, split * band : (split + 1) * band, :
        ].astype(F32)
    stack[pl.ds(pl.multiple_of(step * share, 8), share), :] = mixed_ref[0].astype(F32)

    @pl.when(step == pl.num_programs(0) - 1)
    def _():
        cuts = query_ref.shape[1] // tile
        for cut in range(cuts):
            span = slice(cut * tile, (cut + 1) * tile)
            query_ref[:, span] = stack[cut * rows : (cut + 1) * rows, :]
            out_ref[:, span] = stack[(cuts + cut) * rows : (cuts + cut + 1) * rows, :]


def on_device(
    inputs,
    gain_attn,
    w_query,
    w_key,
    w_value,
    w_out,
    gain_mlp,
    w_gate,
    w_up,
    w_down,
    cotangent,
    *,
    n_ctx,
    n_shard,
):
    x = inputs[0]
    cot = cotangent[0]
    count, width = x.shape
    rows, qw = w_query.shape
    kvw = w_key.shape[1]
    ff_own = w_down.shape[0]
    ff = w_gate.shape[1]
    groups = kvw // HEAD
    per = qw // kvw
    blocks = n_ctx
    per_shard = n_ctx // n_shard
    tile = ff_own // per_shard
    assert count == BLOCK and n_shard == 4 and ff_own * n_shard == ff
    aligned = tile % LANES == 0
    order = ring_order(n_ctx)
    places = [order.index(index) for index in range(n_ctx)]
    shard = lax.axis_index("shard")
    ctx = lax.axis_index("ctx")
    shard_arr = shard.astype(jnp.int32)[None]

    def after(value, done):
        return lax.optimization_barrier((value, done))[0]

    def hop(value, distance):
        pairs = [(index, index ^ distance) for index in range(n_shard)]
        return lax.ppermute(value, "shard", pairs)

    def ctx_hop(value, distance):
        pairs = [(index, index ^ distance) for index in range(n_ctx)]
        return lax.ppermute(value, "ctx", pairs)

    def gather(value, done):
        far = hop(after(value, done), 2)
        return [value, hop(value, 1), far, hop(far, 1)]

    def halves(parts):
        third = hop(parts[3], 1)
        first = hop(parts[1], 1)
        across = (parts[2].astype(F32) + third.astype(F32)).astype(BF16)
        return parts[0], first, across

    def reduce(parts):
        own, first, across = halves(parts)
        return [own, first, hop(across, 2)]

    def add(parts):
        return sum(part.astype(F32) for part in parts)

    def scatter(value):
        return lax.psum_scatter(
            value, "ctx", scatter_dimension=0, axis_index_groups=[order], tiled=False
        )

    def collect(value):
        return lax.all_gather(value, "ctx", axis=0, axis_index_groups=[order], tiled=True)

    lane = jnp.arange(LANES, dtype=jnp.int32)
    frequency = jnp.exp((lane % (HEAD // 2)).astype(F32) * (-2.0 * math.log(10000.0) / HEAD))
    positions = (ctx * count + jnp.arange(count, dtype=jnp.int32)).astype(F32)
    angles = positions[:, None] * frequency[None, :]
    cosine = jnp.cos(angles)
    sine = jnp.where(lane % HEAD < HEAD // 2, -1.0, 1.0)[None, :] * jnp.sin(angles)

    gains = jnp.concatenate([gain_attn, gain_mlp])
    gain_rows = jnp.zeros((16, 2 * kvw), BF16).at[0, : 2 * rows].set(gains)
    kv_own = jnp.concatenate([jnp.concatenate([w_key, w_value], axis=1), gain_rows], axis=0)
    far = hop(kv_own, 2)
    kv_weights = [kv_own, hop(kv_own, 1), far, hop(far, 1)]
    starts = jnp.stack([(shard ^ k) * rows for k in range(n_shard)]).astype(jnp.int32)
    sizes = (rows,) * n_shard
    table = jnp.concatenate(
        [jnp.array(places, jnp.int32), ctx.astype(jnp.int32)[None], starts]
    )

    def columns(peer):
        start = peer * ff_own
        return jnp.concatenate(
            [
                lax.dynamic_slice_in_dim(w_gate, start, ff_own, 1),
                lax.dynamic_slice_in_dim(w_up, start, ff_own, 1),
            ],
            axis=1,
        )

    half = rows // 2
    lanes = 4 * ff_own // n_ctx
    spot = jnp.array(places, jnp.int32)[ctx]
    chosen = []
    for distance in (2, 3):
        peer = (shard ^ distance) * ff_own
        column = peer + lax.rem(spot // 2 * lanes, ff_own)
        cuts = [
            lax.dynamic_slice(mat, (spot % 2 * half, column), (half, lanes))
            for mat in (w_gate, w_up)
        ]
        chosen.append(jnp.where(spot // 2 * lanes < ff_own, cuts[0], cuts[1]))
    near_columns = columns(shard ^ 1)
    cosine, sine, near_columns, table, starts, *chosen = lax.optimization_barrier(
        (cosine, sine, near_columns, table, starts, *chosen)
    )
    far_tiles = [hop(after(part, far), k) for part, k in zip(chosen, (2, 3))]
    q_weights = gather(w_query, far_tiles[1])
    out_weights = gather(w_out, q_weights[2])
    far_tile = jnp.concatenate(far_tiles, axis=0)

    hidden, kv, gain_one, gain_two = pl.pallas_call(
        functools.partial(keys_kernel, sizes=sizes, kvw=kvw),
        out_shape=(
            jax.ShapeDtypeStruct((count, width), BF16),
            jax.ShapeDtypeStruct((count, 2 * kvw), BF16),
            jax.ShapeDtypeStruct((1, width), F32),
            jax.ShapeDtypeStruct((1, width), F32),
        ),
        in_specs=[SMEM_SPEC] + [VMEM_SPEC] * 3 + [HBM_SPEC] * n_shard,
        out_specs=(VMEM_SPEC,) * 4,
        scratch_shapes=[
            pltpu.VMEM((width, 2 * kvw), BF16),
            pltpu.VMEM((n_shard, 16, 2 * kvw), BF16),
            pltpu.SemaphoreType.DMA((n_shard,)),
            pltpu.SemaphoreType.DMA((n_shard,)),
        ],
        compiler_params=params(),
        cost_estimate=cost(4 * count * width * kvw, 8e6),
        name="keys",
    )(starts, x, cosine, sine, *kv_weights)
    all_kv = collect(kv)

    queries = pl.pallas_call(
        functools.partial(queries_kernel, sizes=sizes),
        out_shape=jax.ShapeDtypeStruct((count, qw), BF16),
        in_specs=[SMEM_SPEC] + [VMEM_SPEC] * 3 + [HBM_SPEC] * len(sizes),
        out_specs=VMEM_SPEC,
        scratch_shapes=[pltpu.VMEM((width, qw), BF16), pltpu.SemaphoreType.DMA((len(sizes),))],
        compiler_params=params(),
        cost_estimate=cost(2 * count * width * qw, 8e6),
        name="queries",
    )(starts, hidden, cosine, sine, *q_weights)

    far_rows = collect(after(far_tile, kv)[None])
    near_part = hop(near_columns, 1)
    cot_near = hop(cot, 1)
    cot_far = hop(after(cot, (out_weights[2], queries)), 2)

    shared = dict(sizes=sizes, groups=groups, per=per, blocks=blocks)
    fixed = lambda *shape: pl.BlockSpec(shape, lambda step, table: (0,) * len(shape))
    kv_spec = pl.BlockSpec(
        (count, 2 * kvw), lambda step, table: (table[jnp.minimum(step, table[blocks])], 0)
    )
    once = lambda *shape: pl.BlockSpec(
        shape, lambda step, table: (0,) * len(shape), pipeline_mode=pl.Buffered(1)
    )
    weight_specs = [HBM_SPEC] * len(sizes)
    span = per * count
    out_tall, attended, log_total, mid, normed, q_cols = pl.pallas_call(
        functools.partial(attend_kernel, **shared),
        out_shape=(
            jax.ShapeDtypeStruct((qw, count), F32),
            jax.ShapeDtypeStruct((count, qw), BF16),
            jax.ShapeDtypeStruct((8, span), F32),
            jax.ShapeDtypeStruct((count, width), F32),
            jax.ShapeDtypeStruct((count, width), BF16),
            jax.ShapeDtypeStruct((groups, HEAD, span), BF16),
        ),
        grid_spec=pltpu.PrefetchScalarGridSpec(
            num_scalar_prefetch=1,
            grid=(blocks,),
            in_specs=[once(count, qw), kv_spec, once(count, width), once(1, width)]
            + weight_specs,
            out_specs=[
                fixed(qw, count),
                fixed(count, qw),
                fixed(8, span),
                fixed(count, width),
                fixed(count, width),
                fixed(groups, HEAD, span),
            ],
            scratch_shapes=[
                pltpu.VMEM((groups, HEAD, span), F32),
                pltpu.VMEM((8, span), F32),
                pltpu.VMEM((8, span), F32),
                pltpu.VMEM((qw, width), BF16),
                pltpu.VMEM((2, count, span), F32),
                pltpu.VMEM((qw, count), F32),
                pltpu.SemaphoreType.DMA((len(sizes),)),
            ],
        ),
        compiler_params=params(),
        cost_estimate=cost(
            4 * count * count * blocks * qw, 12e6, count * count * blocks * groups * per
        ),
        name="attend",
    )(table, queries, all_kv, x, gain_two, *out_weights)

    if ff_own % lanes == 0 and lanes % LANES == 0:
        gate_mat, up_mat = pl.pallas_call(
            functools.partial(build_kernel, half=half, lanes=lanes),
            out_shape=(jax.ShapeDtypeStruct((width, ff_own), BF16),) * 2,
            in_specs=[SMEM_SPEC] + [HBM_SPEC] * 3,
            out_specs=(HBM_SPEC,) * 2,
            scratch_shapes=[pltpu.SemaphoreType.DMA((4 + 2 * n_ctx,))],
            compiler_params=params(),
            cost_estimate=cost(1e5, 8e6),
            name="build",
        )(starts, columns(shard), near_part, after(far_rows, normed))
    else:
        tiles_of = after(far_rows, normed).reshape(n_ctx // 2, 2, 2, half, lanes)
        tiles_of = tiles_of.transpose(2, 1, 3, 0, 4).reshape(2, rows, 2 * ff_own)
        gate_mat = jnp.zeros((width, ff_own), BF16)
        up_mat = jnp.zeros((width, ff_own), BF16)
        for part, start in zip((columns(shard), near_part, tiles_of[0], tiles_of[1]), starts):
            gate_mat = lax.dynamic_update_slice_in_dim(gate_mat, part[:, :ff_own], start, 0)
            up_mat = lax.dynamic_update_slice_in_dim(up_mat, part[:, ff_own:], start, 0)
    normed_far = hop(normed, 2)
    normed_pieces = [normed, hop(normed, 1), normed_far, hop(normed_far, 1)]
    cot_far = after(cot_far, normed)
    all_cot = jnp.concatenate([cot, cot_near, cot_far, hop(cot_far, 1)], axis=0)
    all_normed = jnp.concatenate(normed_pieces, axis=0)
    gate = nn(all_normed, gate_mat)
    up = nn(all_normed, up_mat)
    grad_activated = nt(all_cot, w_down)
    sigmoid = jax.nn.sigmoid(gate)
    activated = (gate * sigmoid * up).astype(BF16)
    grad_gate = (grad_activated * up * (sigmoid * (1.0 + gate * (1.0 - sigmoid)))).astype(BF16)
    grad_up = (grad_activated * (gate * sigmoid)).astype(BF16)
    cut = lambda whole: [whole[k * count : (k + 1) * count] for k in range(n_shard)]
    if aligned:
        feed_tiles = pl.pallas_call(
            functools.partial(feed_grads_kernel, rows=rows, per_shard=per_shard),
            out_shape=jax.ShapeDtypeStruct((n_ctx, 3 * rows, tile), BF16),
            in_specs=[SMEM_SPEC] + [VMEM_SPEC] * 5,
            out_specs=VMEM_SPEC,
            scratch_shapes=[pltpu.VMEM((width, n_shard * count), BF16)],
            compiler_params=params(),
            cost_estimate=cost(6 * n_shard * count * width * ff_own, 15e6),
            name="feed_grads",
        )(shard_arr, all_normed, grad_gate, grad_up, activated, all_cot)
    else:

        def tiles(grad):
            pieces = grad.astype(BF16).reshape(n_shard, rows, per_shard, tile)
            pieces = pieces.transpose(0, 2, 1, 3)
            return jnp.roll(pieces, shard, axis=0).reshape(n_ctx, rows, tile)

        down = tn(activated, all_cot).astype(BF16)
        down = down.reshape(n_ctx, ff_own // n_ctx, width // tile, tile).transpose(0, 2, 1, 3)
        feed_tiles = jnp.concatenate(
            [
                tiles(tn(all_normed, grad_gate)),
                tiles(tn(all_normed, grad_up)),
                down.reshape(n_ctx, rows, tile),
            ],
            axis=1,
        )
    feed_sum = scatter(feed_tiles)
    down_sum = feed_sum[2 * rows :]
    grad_gate, grad_up = lax.optimization_barrier((grad_gate, grad_up, feed_tiles))[:2]
    part_normed = (nt(grad_gate, gate_mat) + nt(grad_up, up_mat)).astype(BF16)
    grad_normed = add(reduce(cut(part_normed)))
    pairs = []
    for index in range(n_ctx):
        for source in range(n_shard):
            target = (places[index] // per_shard - source) % n_shard
            pairs.append((index * n_shard + source, index * n_shard + target))
    gate_up_sum = lax.ppermute(feed_sum[: 2 * rows], ("ctx", "shard"), pairs)

    part_out = nn(activated, w_down).astype(BF16)
    part_out = after(part_out, grad_normed)
    output = (mid + add(reduce(cut(part_out)))).astype(BF16)[None]

    place_spec = pl.BlockSpec((count, 2 * kvw), lambda step, table: (table[step], 0))
    grad_query, grad_kv, branch, grad_mid, gain_two_part = pl.pallas_call(
        functools.partial(attend_back_kernel, **shared),
        out_shape=(
            jax.ShapeDtypeStruct((count, qw), BF16),
            jax.ShapeDtypeStruct((blocks * count, 2 * kvw), BF16),
            jax.ShapeDtypeStruct((count, width), BF16),
            jax.ShapeDtypeStruct((count, width), F32),
            jax.ShapeDtypeStruct((1, width), F32),
        ),
        grid_spec=pltpu.PrefetchScalarGridSpec(
            num_scalar_prefetch=1,
            grid=(blocks,),
            in_specs=[
                once(count, qw),
                kv_spec,
                once(groups, HEAD, span),
                once(qw, count),
                once(8, span),
                once(count, width),
                once(1, width),
                once(count, width),
                once(count, width),
                once(count, LANES),
                once(count, LANES),
            ]
            + weight_specs,
            out_specs=[
                fixed(count, qw),
                place_spec,
                fixed(count, width),
                fixed(count, width),
                fixed(1, width),
            ],
            scratch_shapes=[
                pltpu.VMEM((qw, width), BF16),
                pltpu.VMEM((groups, span, HEAD), BF16),
                pltpu.VMEM((groups, span, HEAD), BF16),
                pltpu.VMEM((groups, HEAD, span), BF16),
                pltpu.VMEM((8, span), F32),
                pltpu.VMEM((groups, HEAD, span), F32),
                pltpu.VMEM((2, 2, count, span), F32),
                pltpu.VMEM((qw, count), F32),
                pltpu.SemaphoreType.DMA((len(sizes),)),
            ],
        ),
        compiler_params=params(),
        cost_estimate=cost(
            10 * count * count * blocks * qw, 14e6, count * count * blocks * groups * per
        ),
        name="attend_back",
    )(
        table,
        queries,
        all_kv,
        q_cols,
        out_tall,
        log_total,
        mid,
        gain_two,
        cot,
        grad_normed,
        cosine,
        sine,
        *out_weights,
    )
    own_kv = scatter(after(grad_kv, down_sum).reshape(n_ctx, count, 2 * kvw))

    def weight_grad(left, right, name):
        columns_out = right.shape[1]
        return pl.pallas_call(
            weight_grad_kernel,
            out_shape=(jax.ShapeDtypeStruct((rows, columns_out), BF16),) * n_shard,
            in_specs=[SMEM_SPEC, HBM_SPEC, HBM_SPEC],
            out_specs=(VMEM_SPEC,) * n_shard,
            scratch_shapes=[
                pltpu.VMEM(left.shape, BF16),
                pltpu.VMEM(right.shape, BF16),
                pltpu.VMEM((left.shape[1], columns_out), F32),
                pltpu.SemaphoreType.DMA((2,)),
            ],
            compiler_params=params(),
            cost_estimate=cost(2 * count * left.shape[1] * columns_out, 8e6),
            name=name,
        )(starts, left, right)

    def stack(parts, breadth, name):
        height = sum(part.shape[0] * part.shape[1] for part in parts[::3]) // breadth
        if breadth % LANES:
            wide = jnp.concatenate(
                [add(parts[index : index + 3]) for index in range(0, len(parts), 3)], axis=1
            )
            wide = wide.astype(BF16).reshape(rows, -1, breadth)
            return wide.transpose(1, 0, 2).reshape(height, breadth)
        return pl.pallas_call(
            stack_kernel,
            out_shape=jax.ShapeDtypeStruct((height, breadth), BF16),
            in_specs=[VMEM_SPEC] * len(parts),
            out_specs=VMEM_SPEC,
            compiler_params=params(),
            cost_estimate=cost(1e6, 6e6),
            name=name,
        )(*parts)

    parts_query = reduce(weight_grad(hidden, grad_query, "grad_query"))
    parts_out = reduce(weight_grad(attended, branch, "grad_out"))
    mixed = stack(parts_query + parts_out, tile, "stack_mixed")
    mixed_sum = scatter(after(mixed, own_kv).reshape(n_ctx, -1, tile))
    gathered = collect(jnp.concatenate([gate_up_sum, down_sum, mixed_sum])[None])

    grad_kv_pre, *kv_blocks = pl.pallas_call(
        functools.partial(kv_back_kernel, kvw=kvw),
        out_shape=(jax.ShapeDtypeStruct((count, 2 * kvw), BF16),)
        + (jax.ShapeDtypeStruct((rows, 2 * kvw), BF16),) * n_shard,
        in_specs=[SMEM_SPEC] + [VMEM_SPEC] * 4,
        out_specs=(VMEM_SPEC,) * (1 + n_shard),
        scratch_shapes=[pltpu.VMEM((width, 2 * kvw), F32)],
        compiler_params=params(),
        cost_estimate=cost(4 * count * width * kvw, 5e6),
        name="kv_back",
    )(starts, own_kv, cosine, sine, hidden)
    sum_kv = stack(reduce(kv_blocks), LANES, "stack_kv").reshape(n_ctx, -1, LANES)

    def exchange(value):
        return lax.all_to_all(value, "ctx", split_axis=0, concat_axis=0, tiled=True)

    own_sum = jnp.sum(exchange(sum_kv).astype(F32), axis=0, keepdims=True).astype(BF16)
    both = exchange(jnp.broadcast_to(own_sum, sum_kv.shape))
    both = both.reshape(2 * kvw // LANES, rows, LANES).transpose(1, 0, 2).reshape(rows, 2 * kvw)
    grad_w_key = both[:, :kvw].astype(F32)
    grad_w_value = both[:, kvw:].astype(F32)

    grad_x, gain_one_part = pl.pallas_call(
        functools.partial(inputs_kernel, q_sizes=sizes, kv_sizes=sizes),
        out_shape=(
            jax.ShapeDtypeStruct((count, width), BF16),
            jax.ShapeDtypeStruct((1, width), F32),
        ),
        in_specs=[SMEM_SPEC] * 2
        + [VMEM_SPEC] * 5
        + [HBM_SPEC] * (2 * len(sizes)),
        out_specs=(VMEM_SPEC, VMEM_SPEC),
        scratch_shapes=[
            pltpu.VMEM((width, qw), BF16),
            pltpu.VMEM((width, 2 * kvw), BF16),
            pltpu.SemaphoreType.DMA((len(sizes),)),
            pltpu.SemaphoreType.DMA((len(sizes),)),
        ],
        compiler_params=params(),
        cost_estimate=cost(2 * count * width * (qw + 2 * kvw), 12e6),
        name="grad_inputs",
    )(
        starts,
        starts,
        grad_query,
        grad_kv_pre,
        x,
        gain_one,
        grad_mid,
        *q_weights,
        *kv_weights,
    )

    gain_parts = jnp.concatenate([gain_one_part, gain_two_part], axis=0)
    for distance in [1 << bit for bit in range(n_shard.bit_length() - 1)]:
        gain_parts = gain_parts + hop(gain_parts, distance)
    for distance in [1 << bit for bit in range(n_ctx.bit_length() - 1)]:
        gain_parts = gain_parts + ctx_hop(gain_parts, distance)
    own_gains = lax.dynamic_slice_in_dim(gain_parts, shard * rows, rows, 1)

    if aligned:
        share = mixed_sum.shape[0]
        rolled = lambda step, where: (lax.rem(step + where[0] * per_shard, n_ctx), 0, 0)
        band = ff_own // n_ctx
        grad_w_gate, grad_w_up, grad_w_down, grad_w_query, grad_w_out = pl.pallas_call(
            functools.partial(widen_kernel, rows=rows),
            out_shape=(
                jax.ShapeDtypeStruct((rows, ff), F32),
                jax.ShapeDtypeStruct((rows, ff), F32),
                jax.ShapeDtypeStruct((ff_own, width), F32),
                jax.ShapeDtypeStruct((rows, qw), F32),
                jax.ShapeDtypeStruct((rows, width), F32),
            ),
            grid_spec=pltpu.PrefetchScalarGridSpec(
                num_scalar_prefetch=1,
                grid=(n_ctx,),
                in_specs=[
                    pl.BlockSpec((1, 2 * rows, tile), rolled),
                    pl.BlockSpec((1, rows, tile), lambda step, where: (step, 2, 0)),
                    pl.BlockSpec((1, share, tile), lambda step, where: (step, 3 * rows // share, 0)),
                ],
                out_specs=[
                    pl.BlockSpec((rows, tile), lambda step, where: (0, step)),
                    pl.BlockSpec((rows, tile), lambda step, where: (0, step)),
                    pl.BlockSpec((band, width), lambda step, where: (step, 0)),
                    pl.BlockSpec((rows, qw), lambda step, where: (0, 0)),
                    pl.BlockSpec((rows, width), lambda step, where: (0, 0)),
                ],
                scratch_shapes=[pltpu.VMEM((n_ctx * share, tile), F32)],
            ),
            compiler_params=params(56 * 1024 * 1024),
            cost_estimate=cost(1e6, 20e6),
            name="widen",
        )(shard_arr, gathered, gathered, gathered)
    else:

        def untile(part):
            back = jnp.roll(part.reshape(n_shard, per_shard, rows, tile), -shard, axis=0)
            back = back.reshape(n_ctx, rows, tile).transpose(1, 0, 2)
            return back.reshape(rows, ff).astype(F32)

        grad_w_gate = untile(gathered[:, :rows])
        grad_w_up = untile(gathered[:, rows : 2 * rows])
        down = gathered[:, 2 * rows : 3 * rows].reshape(n_ctx, width // tile, -1, tile)
        grad_w_down = down.transpose(0, 2, 1, 3).reshape(ff_own, width).astype(F32)
        wide = gathered[:, 3 * rows :].reshape(2 * qw // tile, rows, tile).transpose(1, 0, 2)
        wide = wide.reshape(rows, 2 * qw).astype(F32)
        grad_w_query, grad_w_out = wide[:, :qw], wide[:, qw:]

    return (
        output,
        grad_x[None],
        own_gains[0],
        grad_w_query,
        grad_w_key,
        grad_w_value,
        grad_w_out,
        own_gains[1],
        grad_w_gate,
        grad_w_up,
        grad_w_down,
    )


def solution(mesh):
    tokens = P("shard", "ctx", None)
    split = P("shard", None)
    gain = P("shard")
    placed = (tokens, gain, split, split, split, split, gain, split, split, split, tokens)
    return jax.shard_map(
        functools.partial(on_device, n_ctx=mesh.shape["ctx"], n_shard=mesh.shape["shard"]),
        mesh=mesh,
        in_specs=placed,
        out_specs=(tokens, tokens, gain, split, split, split, split, gain, split, split, split),
        check_vma=False,
    )
```

```python
import functools
import math

import jax
import jax.numpy as jnp
from jax import lax
from jax.experimental import pallas as pl
from jax.experimental.pallas import tpu as pltpu
from jax.sharding import PartitionSpec as P

HEAD = 64
BLOCK = 256
EPSILON = 1e-05
LANES = 128
F32 = jnp.float32
BF16 = jnp.bfloat16
SCORE_SCALE = math.log2(math.e) * 0.125
NEGATIVE = -1e30
ALL_VMEM = 60 * 1024 * 1024
PART_VMEM = 32 * 1024 * 1024


def nn(left, right):
    return lax.dot_general(left, right, (((1,), (0,)), ((), ())), preferred_element_type=F32)


def nt(left, right):
    return lax.dot_general(left, right, (((1,), (1,)), ((), ())), preferred_element_type=F32)


def tn(left, right):
    return lax.dot_general(left, right, (((0,), (0,)), ((), ())), preferred_element_type=F32)


def ring_order(count):
    if count % 2:
        return list(range(count))
    return list(range(0, count, 2)) + list(range(count - 1, 0, -2))


def params(limit=ALL_VMEM):
    return pltpu.CompilerParams(vmem_limit_bytes=limit)


def cost(flops, moved, exps=0):
    return pl.CostEstimate(flops=int(flops), bytes_accessed=int(moved), transcendentals=int(exps))


HBM_SPEC = pl.BlockSpec(memory_space=pltpu.HBM)
SMEM_SPEC = pl.BlockSpec(memory_space=pltpu.SMEM)


def block(shape):
    return pl.BlockSpec(shape, lambda *_: (0,) * len(shape), pipeline_mode=pl.Buffered(1))


def call_once(
    kernel, outs, ins, held=(), moved=(), scratch=(), flops=0, limit=PART_VMEM, name=None
):
    return pl.pallas_call(
        kernel,
        out_shape=tuple(jax.ShapeDtypeStruct(shape, dtype) for shape, dtype in outs),
        grid=(1,),
        in_specs=[SMEM_SPEC] * len(held)
        + [block(array.shape) for array in ins]
        + [HBM_SPEC] * len(moved),
        out_specs=tuple(pl.BlockSpec(shape, lambda *_: (0,) * len(shape)) for shape, _ in outs),
        scratch_shapes=list(scratch),
        compiler_params=params(limit),
        cost_estimate=cost(flops, sum(2 * math.prod(shape) for shape, _ in outs) + 4e6),
        name=name,
    )(*held, *ins, *moved)


def swap_halves(tile):
    lane = lax.broadcasted_iota(jnp.int32, tile.shape, 1)
    ahead = pltpu.roll(tile, LANES - HEAD // 2, 1)
    behind = pltpu.roll(tile, HEAD // 2, 1)
    return jnp.where(lane % HEAD < HEAD // 2, ahead, behind)


def fetches(starts, pieces, whole, sems, sizes):
    copies = []
    for index, (piece, size) in enumerate(zip(pieces, sizes)):
        start = pl.multiple_of(starts[index], 16)
        copies.append(
            pltpu.make_async_copy(
                piece.at[pl.ds(0, size), :], whole.at[pl.ds(start, size), :], sems.at[index]
            )
        )
    return copies


def keys_kernel(starts_ref, x_ref, cos_ref, sin_ref, *rest, sizes, kvw):
    pieces = rest[: len(sizes)]
    hidden_ref, kv_ref, one_ref, two_ref, whole, bands, sems, band_sems = rest[len(sizes) :]
    copies = fetches(starts_ref, pieces, whole, sems, sizes)
    rows = sizes[0]
    for index, piece in enumerate(pieces):
        band = pltpu.make_async_copy(
            piece.at[pl.ds(rows, 16), :], bands.at[index], band_sems.at[index]
        )
        band.start()
        copies[index].start()
    x = x_ref[...].astype(F32)
    scale = lax.rsqrt(jnp.mean(x * x, axis=-1, keepdims=True) + EPSILON)
    width = x.shape[1]
    ones = jnp.zeros((8, width), F32)
    twos = jnp.zeros((8, width), F32)
    for index, piece in enumerate(pieces):
        pltpu.make_async_copy(
            piece.at[pl.ds(rows, 16), :], bands.at[index], band_sems.at[index]
        ).wait()
        band = bands[index].astype(F32)[:8, :]
        blank = jnp.zeros((8, width - rows), F32)
        first = jnp.concatenate([band[:, :rows], blank], axis=1)
        second = jnp.concatenate([band[:, rows : 2 * rows], blank], axis=1)
        ones = ones + pltpu.roll(first, starts_ref[index], 1)
        twos = twos + pltpu.roll(second, starts_ref[index], 1)
    one_ref[...] = ones[:1, :]
    two_ref[...] = twos[:1, :]
    hidden = (x * scale * ones[:1, :]).astype(BF16)
    hidden_ref[...] = hidden
    for copy in copies:
        copy.wait()
    pre = nn(hidden, whole[...])
    for start in range(0, kvw, LANES):
        tile = pre[:, start : start + LANES]
        turned = tile * cos_ref[...] + swap_halves(tile) * sin_ref[...]
        kv_ref[:, start : start + LANES] = turned.astype(BF16)
    kv_ref[:, kvw:] = pre[:, kvw:].astype(BF16)


def queries_kernel(starts_ref, hidden_ref, cos_ref, sin_ref, *rest, sizes):
    pieces = rest[: len(sizes)]
    query_ref, whole, sems = rest[len(sizes) :]
    copies = fetches(starts_ref, pieces, whole, sems, sizes)
    for copy in copies:
        copy.start()
    for copy in copies:
        copy.wait()
    pre = nn(hidden_ref[...], whole[...])
    for start in range(0, pre.shape[1], LANES):
        tile = pre[:, start : start + LANES]
        turned = tile * cos_ref[...] + swap_halves(tile) * sin_ref[...]
        query_ref[:, start : start + LANES] = turned.astype(BF16)


def attend_kernel(
    table_ref,
    q_ref,
    kv_ref,
    x_ref,
    gain_ref,
    *rest,
    sizes,
    groups,
    per,
    blocks,
):
    pieces = rest[:-13]
    (
        out_ref,
        attended_ref,
        log_ref,
        mid_ref,
        normed_ref,
        cols_ref,
        acc,
        top,
        total,
        whole,
        scores,
        tall,
        sems,
    ) = rest[-13:]
    step = pl.program_id(0)
    last = table_ref[blocks]
    starts = [table_ref[blocks + 1 + index] for index in range(len(sizes))]
    count = q_ref.shape[0]
    kvw = groups * HEAD

    @pl.when(step == 0)
    def _():
        for copy in fetches(starts, pieces, whole, sems, sizes):
            copy.start()
        turned = q_ref[...].T
        for group in range(groups):
            for member in range(per):
                head = group * per + member
                cols_ref[group, :, member * count : (member + 1) * count] = turned[
                    head * HEAD : (head + 1) * HEAD, :
                ]
        acc[...] = jnp.zeros_like(acc)
        total[...] = jnp.zeros_like(total)
        top[...] = jnp.full_like(top, NEGATIVE)

    @pl.when(step <= last)
    def _():
        def score(group):
            key = kv_ref[:, group * HEAD : (group + 1) * HEAD]
            scores[group % 2] = nn(key, cols_ref[group])

        score(0)
        for group in range(groups):
            if group + 1 < groups:
                score(group + 1)
            value = kv_ref[:, kvw + group * HEAD : kvw + (group + 1) * HEAD]
            raw = scores[group % 2]
            old = top[group : group + 1, :]
            new = jnp.maximum(old, jnp.max(raw, axis=0, keepdims=True))
            shrink = jnp.exp2((old - new) * SCORE_SCALE)
            probs = jnp.exp2((raw - new) * SCORE_SCALE)
            top[group : group + 1, :] = new
            total[group : group + 1, :] = total[group : group + 1, :] * shrink + jnp.sum(
                probs, axis=0, keepdims=True
            )
            acc[group] = acc[group] * shrink + tn(value, probs.astype(BF16))

    @pl.when(step == blocks - 1)
    def _():
        for group in range(groups):
            sums = total[group : group + 1, :]
            log_ref[group : group + 1, :] = top[
                group : group + 1, :
            ] * SCORE_SCALE + jnp.log2(sums)
            rowed = acc[group] / sums
            for member in range(per):
                head = group * per + member
                tall[head * HEAD : (head + 1) * HEAD, :] = rowed[
                    :, member * count : (member + 1) * count
                ]
        out_ref[...] = tall[...]
        attended = tall[...].astype(BF16).T
        attended_ref[...] = attended
        for copy in fetches(starts, pieces, whole, sems, sizes):
            copy.wait()
        mid = x_ref[...].astype(F32) + nn(attended, whole[...])
        mid_ref[...] = mid
        scale = lax.rsqrt(jnp.mean(mid * mid, axis=-1, keepdims=True) + EPSILON)
        normed_ref[...] = (mid * scale * gain_ref[...]).astype(BF16)


def attend_back_kernel(
    table_ref,
    kv_ref,
    cols_ref,
    out_ref,
    log_ref,
    mid_ref,
    gain_ref,
    cot_ref,
    gn_own_ref,
    gn_near_ref,
    gn_far_ref,
    cos_ref,
    sin_ref,
    *rest,
    sizes,
    groups,
    per,
    blocks,
):
    pieces = rest[: len(sizes)]
    (
        gq_ref,
        gkv_ref,
        branch_ref,
        gmid_ref,
        ggain_ref,
        whole,
        d_cols,
        delta,
        acc,
        probs_all,
        tall,
        sems,
    ) = rest[len(sizes) :]
    step = pl.program_id(0)
    last = table_ref[blocks]
    starts = [table_ref[blocks + 1 + index] for index in range(len(sizes))]
    count = kv_ref.shape[0]
    kvw = groups * HEAD

    @pl.when(step == 0)
    def _():
        copies = fetches(starts, pieces, whole, sems, sizes)
        for copy in copies:
            copy.start()
        mid = mid_ref[...]
        incoming = (
            gn_own_ref[...].astype(F32) + gn_near_ref[...].astype(F32)
        ) + gn_far_ref[...].astype(F32)
        gain = gain_ref[...]
        scale = lax.rsqrt(jnp.mean(mid * mid, axis=-1, keepdims=True) + EPSILON)
        weighted = incoming * gain
        inner = jnp.mean(weighted * mid, axis=-1, keepdims=True)
        ggain_ref[...] = jnp.sum(incoming * mid * scale, axis=0, keepdims=True)
        grad_mid = (
            cot_ref[...].astype(F32) + scale * weighted - mid * (scale * scale * scale * inner)
        )
        gmid_ref[...] = grad_mid
        branch = grad_mid.astype(BF16)
        branch_ref[...] = branch
        for copy in copies:
            copy.wait()
        grads = nt(branch, whole[...]).astype(BF16)
        turned = grads.T
        tall[...] = turned.astype(F32) * out_ref[...]
        for group in range(groups):
            for member in range(per):
                head = group * per + member
                span = slice(head * HEAD, (head + 1) * HEAD)
                cols = slice(member * count, (member + 1) * count)
                d_cols[group, :, cols] = turned[span, :]
                delta[group : group + 1, cols] = jnp.sum(tall[span, :], axis=0, keepdims=True)
        acc[...] = jnp.zeros_like(acc)

    @pl.when(step > last)
    def _():
        gkv_ref[...] = jnp.zeros_like(gkv_ref)

    @pl.when(step <= last)
    def _():
        def spans(group):
            return (
                slice(group * HEAD, (group + 1) * HEAD),
                slice(kvw + group * HEAD, kvw + (group + 1) * HEAD),
            )

        def score(group):
            key_span, value_span = spans(group)
            probs_all[group % 2, 0] = nn(kv_ref[:, key_span], cols_ref[group])
            probs_all[group % 2, 1] = nn(kv_ref[:, value_span], d_cols[group])

        score(0)
        for group in range(groups):
            if group + 1 < groups:
                score(group + 1)
            key_span, value_span = spans(group)
            probs = jnp.exp2(
                probs_all[group % 2, 0] * SCORE_SCALE - log_ref[group : group + 1, :]
            )
            grad_scores = (
                probs * (probs_all[group % 2, 1] - delta[group : group + 1, :])
            ).astype(BF16)
            gkv_ref[:, value_span] = nt(probs.astype(BF16), d_cols[group]).astype(BF16)
            gkv_ref[:, key_span] = (nt(grad_scores, cols_ref[group]) * 0.125).astype(BF16)
            acc[group] = acc[group] + tn(kv_ref[:, key_span], grad_scores)

    @pl.when(step == blocks - 1)
    def _():
        for group in range(groups):
            for member in range(per):
                head = group * per + member
                tall[head * HEAD : (head + 1) * HEAD, :] = (
                    acc[group, :, member * count : (member + 1) * count] * 0.125
                )
        for start in range(0, tall.shape[0], LANES):
            tile = tall[start : start + LANES, :].T
            turned = tile * cos_ref[...] - swap_halves(tile) * sin_ref[...]
            gq_ref[:, start : start + LANES] = turned.astype(BF16)


def kv_back_kernel(starts_ref, grad_ref, cos_ref, sin_ref, hidden_ref, out_ref, *rest, kvw):
    outs, full = rest[:-1], rest[-1]
    for start in range(0, kvw, LANES):
        tile = grad_ref[:, start : start + LANES].astype(F32)
        turned = tile * cos_ref[...] - swap_halves(tile) * sin_ref[...]
        out_ref[:, start : start + LANES] = turned.astype(BF16)
    out_ref[:, kvw:] = grad_ref[:, kvw:]
    full[...] = tn(hidden_ref[...], out_ref[...])
    for index, out in enumerate(outs):
        start = pl.multiple_of(starts_ref[index], 8)
        out[...] = full[pl.ds(start, out.shape[0]), :].astype(BF16)


def stack_kernel(*refs):
    parts, out_ref = refs[:-1], refs[-1]
    tile = out_ref.shape[1]
    row = 0
    for index in range(0, len(parts), 3):
        first, second, third = parts[index : index + 3]
        rows, columns = first.shape
        for start in range(0, columns, tile):
            span = slice(start, start + tile)
            total = (
                first[:, span].astype(F32) + second[:, span].astype(F32)
            ) + third[:, span].astype(F32)
            out_ref[row : row + rows, :] = total.astype(BF16)
            row += rows


def inputs_kernel(starts_ref, gq_ref, gkv_ref, x_ref, gain_ref, gmid_ref, *rest, sizes):
    hops = len(sizes)
    grad_ref, ggain_ref, whole_q, whole_kv, q_sems, kv_sems = rest[2 * hops :]
    copies = fetches(starts_ref, rest[:hops], whole_q, q_sems, sizes)
    copies += fetches(starts_ref, rest[hops : 2 * hops], whole_kv, kv_sems, sizes)
    for copy in copies:
        copy.start()
    for copy in copies:
        copy.wait()
    incoming = nt(gq_ref[...], whole_q[...]) + nt(gkv_ref[...], whole_kv[...])
    x = x_ref[...].astype(F32)
    scale = lax.rsqrt(jnp.mean(x * x, axis=-1, keepdims=True) + EPSILON)
    weighted = incoming * gain_ref[...]
    inner = jnp.mean(weighted * x, axis=-1, keepdims=True)
    ggain_ref[...] = jnp.sum(incoming * x * scale, axis=0, keepdims=True)
    grad = gmid_ref[...] + scale * weighted - x * (scale * scale * scale * inner)
    grad_ref[...] = grad.astype(BF16)


def weight_grads_kernel(starts_ref, hidden_ref, query_ref, attended_ref, branch_ref, *rest):
    outs, full = rest[:-1], rest[-1]
    hops = len(outs) // 2
    for index, (left, right) in enumerate(((hidden_ref, query_ref), (attended_ref, branch_ref))):
        full[...] = tn(left[...], right[...])
        for hop, out in enumerate(outs[index * hops : (index + 1) * hops]):
            start = pl.multiple_of(starts_ref[hop], 8)
            out[...] = full[pl.ds(start, out.shape[0]), :].astype(BF16)


def units(normed, cot, gate_mat, up_mat, down_mat):
    gate = nn(normed, gate_mat)
    up = nn(normed, up_mat)
    grad = nt(cot, down_mat)
    sigmoid = 1.0 / (1.0 + jnp.exp(-gate))
    silu = gate * sigmoid
    return (
        (silu * up).astype(BF16),
        (grad * up * (sigmoid * (1.0 + gate * (1.0 - sigmoid)))).astype(BF16),
        (grad * silu).astype(BF16),
    )


def feed_near_kernel(
    starts_ref, own_gate_ref, own_up_ref, near_ref, far_ref, down_ref, *rest, half, lanes
):
    normed_refs, cot_refs = rest[:2], rest[2:4]
    gate_mat_out, up_mat_out, act_out, gate_out, up_out, back_out = rest[4:10]
    gate_mat, up_mat, down_mat, tokens, cots, act, grad_gate, grad_up, back = rest[10:19]
    mat_sems, token_sems, out_sems = rest[19:]
    rows = near_ref.shape[0]
    own = gate_mat.shape[1]
    mats = []

    def place(source, row, column, height, breadth):
        target = gate_mat if column < own else up_mat
        mats.append(
            pltpu.make_async_copy(
                source,
                target.at[pl.ds(pl.multiple_of(row, 16), height), pl.ds(column % own, breadth)],
                mat_sems.at[len(mats)],
            )
        )

    mine = pl.ds(pl.multiple_of(starts_ref[4] * own, LANES), own)
    for index, ref in enumerate((own_gate_ref, own_up_ref)):
        place(ref.at[:, mine], starts_ref[0], index * own, rows, own)
        place(near_ref.at[:, pl.ds(index * own, own)], starts_ref[1], index * own, rows, own)
    for spot in range(far_ref.shape[0]):
        for index in range(2):
            place(
                far_ref.at[spot, pl.ds(index * half, half), :],
                starts_ref[2 + index] + (spot % 2) * half,
                (spot // 2) * lanes,
                half,
                lanes,
            )
    loads = [
        pltpu.make_async_copy(ref, target.at[index], token_sems.at[slot, index])
        for slot, (refs, target) in enumerate(((normed_refs, tokens), (cot_refs, cots)))
        for index, ref in enumerate(refs)
    ]
    loads.append(pltpu.make_async_copy(down_ref, down_mat, token_sems.at[2, 0]))
    for copy in mats + loads:
        copy.start()
    for copy in mats:
        copy.wait()
    outs = [
        pltpu.make_async_copy(source, target, out_sems.at[index])
        for index, (source, target) in enumerate(
            (
                (gate_mat, gate_mat_out),
                (up_mat, up_mat_out),
                (act, act_out),
                (grad_gate, gate_out),
                (grad_up, up_out),
                (back, back_out),
            )
        )
    ]
    for copy in outs[:2]:
        copy.start()
    for copy in loads:
        copy.wait()

    def token_block(index, carry):
        act[index], grad_gate[index], grad_up[index] = units(
            tokens[index], cots[index], gate_mat[...], up_mat[...], down_mat[...]
        )
        back[index] = (
            nt(grad_gate[index], gate_mat[...]) + nt(grad_up[index], up_mat[...])
        ).astype(BF16)
        return carry

    lax.fori_loop(0, 2, token_block, 0)
    for copy in outs[2:]:
        copy.start()
    for copy in outs:
        copy.wait()


def feed_far_kernel(
    starts_ref, gate_mat_ref, up_mat_ref, down_ref, act_in, gate_in, up_in, *rest, per_shard
):
    hops = 4
    normed_refs, cot_refs = rest[:hops], rest[hops : 2 * hops]
    tiles_out, act_out, gate_out, up_out = rest[2 * hops : 2 * hops + 4]
    gate_mat, up_mat, down_mat, tokens, cots, turned, act, grad_gate, grad_up, tiles = rest[
        2 * hops + 4 : 2 * hops + 14
    ]
    mat_sems, token_sems, cot_sems, unit_sems, out_sems, tile_sems = rest[2 * hops + 14 :]
    width, own = gate_mat.shape
    count = tokens.shape[1]
    places, height, tile = tiles.shape
    rows = height // 3
    mats = [
        pltpu.make_async_copy(source, target, mat_sems.at[index])
        for index, (source, target) in enumerate(
            ((gate_mat_ref, gate_mat), (up_mat_ref, up_mat), (down_ref, down_mat))
        )
    ]
    token_copies = [
        pltpu.make_async_copy(ref, tokens.at[index], token_sems.at[index])
        for index, ref in enumerate(normed_refs)
    ]
    cot_copies = [
        pltpu.make_async_copy(ref, cots.at[pl.ds(index * count, count), :], cot_sems.at[index])
        for index, ref in enumerate(cot_refs)
    ]
    unit_copies = [
        pltpu.make_async_copy(source.at[index], target.at[pl.ds(index * count, count), :],
                              unit_sems.at[slot, index])
        for slot, (source, target) in enumerate(
            ((act_in, act), (gate_in, grad_gate), (up_in, grad_up))
        )
        for index in range(2)
    ]
    for copy in mats + token_copies[2:] + cot_copies[2:]:
        copy.start()
    for copy in token_copies[:2] + cot_copies[:2] + unit_copies:
        copy.start()
    for copy in token_copies[:2]:
        copy.wait()
    for index in range(2):
        turned[:, index * count : (index + 1) * count] = tokens[index].T
    for copy in mats + token_copies[2:] + cot_copies[2:]:
        copy.wait()

    def token_block(index, carry):
        span = pl.ds(pl.multiple_of(index * count, count), count)
        normed = tokens[index]
        act[span, :], grad_gate[span, :], grad_up[span, :] = units(
            normed, cots[span, :], gate_mat[...], up_mat[...], down_mat[...]
        )
        turned[:, span] = normed.T
        return carry

    lax.fori_loop(2, hops, token_block, 0)
    late = pl.ds(2 * count, 2 * count)
    outs = [
        pltpu.make_async_copy(source.at[late, :], target, out_sems.at[index])
        for index, (source, target) in enumerate(
            ((act, act_out), (grad_gate, gate_out), (grad_up, up_out))
        )
    ]
    for copy in outs:
        copy.start()
    for copy in cot_copies[:2] + unit_copies:
        copy.wait()

    def tile_copy(spot, slot):
        low, high = ((0, 2 * rows), (2 * rows, 3 * rows))[slot]
        return pltpu.make_async_copy(
            tiles.at[spot, pl.ds(low, high - low), :],
            tiles_out.at[spot, pl.ds(low, high - low), :],
            tile_sems.at[slot, spot],
        )

    def row_block(index, carry):
        left = turned[pl.ds(pl.multiple_of(index * rows, 16), rows), :]
        spot = lax.rem(index + starts_ref[hops], hops) * per_shard
        for slot, ref in ((0, grad_gate), (1, grad_up)):
            grad = nn(left, ref[...])
            for part in range(per_shard):
                tiles[spot + part, slot * rows : (slot + 1) * rows, :] = grad[
                    :, part * tile : (part + 1) * tile
                ].astype(BF16)
        for part in range(per_shard):
            tile_copy(spot + part, 0).start()
        return carry

    lax.fori_loop(0, hops, row_block, 0)
    band = own // places
    turned[:own, :] = act[...].T

    def down_block(index, carry):
        left = turned[pl.ds(pl.multiple_of(index * 2 * band, 16), 2 * band), :]
        grad = nn(left, cots[...])
        for part in range(2):
            for split in range(width // tile):
                start = 2 * rows + split * band
                tiles[2 * index + part, start : start + band, :] = grad[
                    part * band : (part + 1) * band, split * tile : (split + 1) * tile
                ].astype(BF16)
            tile_copy(2 * index + part, 1).start()
        return carry

    lax.fori_loop(0, places // 2, down_block, 0)
    for copy in outs:
        copy.wait()
    for spot in range(places):
        for slot in range(2):
            tile_copy(spot, slot).wait()


def normed_back_kernel(gate_ref, up_ref, gate_mat_ref, up_mat_ref, *outs):
    count = outs[0].shape[0]
    for index, out in enumerate(outs):
        span = slice(index * count, (index + 1) * count)
        out[...] = (
            nt(gate_ref[span, :], gate_mat_ref[...]) + nt(up_ref[span, :], up_mat_ref[...])
        ).astype(BF16)


def widen_kernel(
    shard_ref,
    gate_up_ref,
    down_in_ref,
    mixed_ref,
    gate_ref,
    up_ref,
    down_ref,
    query_ref,
    out_ref,
    stack,
    *,
    rows,
):
    step = pl.program_id(0)
    tile = gate_ref.shape[1]
    band = down_ref.shape[0]
    share = mixed_ref.shape[1]
    gate_ref[...] = gate_up_ref[0, :rows, :].astype(F32)
    up_ref[...] = gate_up_ref[0, rows:, :].astype(F32)
    for split in range(down_ref.shape[1] // tile):
        down_ref[:, split * tile : (split + 1) * tile] = down_in_ref[
            0, split * band : (split + 1) * band, :
        ].astype(F32)
    stack[pl.ds(pl.multiple_of(step * share, 8), share), :] = mixed_ref[0].astype(F32)

    @pl.when(step == pl.num_programs(0) - 1)
    def _():
        cuts = query_ref.shape[1] // tile
        for cut in range(cuts):
            span = slice(cut * tile, (cut + 1) * tile)
            query_ref[:, span] = stack[cut * rows : (cut + 1) * rows, :]
            out_ref[:, span] = stack[(cuts + cut) * rows : (cuts + cut + 1) * rows, :]


def on_device(
    inputs,
    gain_attn,
    w_query,
    w_key,
    w_value,
    w_out,
    gain_mlp,
    w_gate,
    w_up,
    w_down,
    cotangent,
    *,
    n_ctx,
    n_shard,
):
    x = inputs[0]
    cot = cotangent[0]
    count, width = x.shape
    rows, qw = w_query.shape
    kvw = w_key.shape[1]
    ff_own = w_down.shape[0]
    ff = w_gate.shape[1]
    groups = kvw // HEAD
    per = qw // kvw
    blocks = n_ctx
    per_shard = n_ctx // n_shard
    tile = ff_own // per_shard
    assert count == BLOCK and n_shard == 4 and ff_own * n_shard == ff
    aligned = tile % LANES == 0
    order = ring_order(n_ctx)
    places = [order.index(index) for index in range(n_ctx)]
    shard = lax.axis_index("shard")
    ctx = lax.axis_index("ctx")
    shard_arr = shard.astype(jnp.int32)[None]

    def after(value, done):
        return lax.optimization_barrier((value, done))[0]

    def hop(value, distance):
        pairs = [(index, index ^ distance) for index in range(n_shard)]
        return lax.ppermute(value, "shard", pairs)

    def ctx_hop(value, distance):
        pairs = [(index, index ^ distance) for index in range(n_ctx)]
        return lax.ppermute(value, "ctx", pairs)

    def gather(value, done):
        far = hop(after(value, done), 2)
        return [value, hop(value, 1), far, hop(far, 1)]

    def halves(parts):
        third = hop(parts[3], 1)
        first = hop(parts[1], 1)
        across = (parts[2].astype(F32) + third.astype(F32)).astype(BF16)
        return parts[0], first, across

    def reduce(parts):
        own, first, across = halves(parts)
        return [own, first, hop(across, 2)]

    def add(parts):
        return sum(part.astype(F32) for part in parts)

    def scatter(value):
        return lax.psum_scatter(
            value, "ctx", scatter_dimension=0, axis_index_groups=[order], tiled=False
        )

    def collect(value):
        return lax.all_gather(value, "ctx", axis=0, axis_index_groups=[order], tiled=True)

    lane = jnp.arange(LANES, dtype=jnp.int32)
    frequency = jnp.exp((lane % (HEAD // 2)).astype(F32) * (-2.0 * math.log(10000.0) / HEAD))
    positions = (ctx * count + jnp.arange(count, dtype=jnp.int32)).astype(F32)
    angles = positions[:, None] * frequency[None, :]
    cosine = jnp.cos(angles)
    sine = jnp.where(lane % HEAD < HEAD // 2, -1.0, 1.0)[None, :] * jnp.sin(angles)

    gains = jnp.concatenate([gain_attn, gain_mlp])
    gain_rows = jnp.zeros((16, 2 * kvw), BF16).at[0, : 2 * rows].set(gains)
    kv_own = jnp.concatenate([jnp.concatenate([w_key, w_value], axis=1), gain_rows], axis=0)
    far = hop(kv_own, 2)
    kv_weights = [kv_own, hop(kv_own, 1), far, hop(far, 1)]
    starts = jnp.stack(
        [(shard ^ k) * rows for k in range(n_shard)] + [shard]
    ).astype(jnp.int32)
    sizes = (rows,) * n_shard
    table = jnp.concatenate(
        [jnp.array(places, jnp.int32), ctx.astype(jnp.int32)[None], starts]
    )

    def columns(peer):
        start = peer * ff_own
        return jnp.concatenate(
            [
                lax.dynamic_slice_in_dim(w_gate, start, ff_own, 1),
                lax.dynamic_slice_in_dim(w_up, start, ff_own, 1),
            ],
            axis=1,
        )

    half = rows // 2
    lanes = 4 * ff_own // n_ctx
    spot = jnp.array(places, jnp.int32)[ctx]
    chosen = []
    for distance in (2, 3):
        peer = (shard ^ distance) * ff_own
        column = peer + lax.rem(spot // 2 * lanes, ff_own)
        cuts = [
            lax.dynamic_slice(mat, (spot % 2 * half, column), (half, lanes))
            for mat in (w_gate, w_up)
        ]
        chosen.append(jnp.where(spot // 2 * lanes < ff_own, cuts[0], cuts[1]))
    near_columns = columns(shard ^ 1)
    cosine, sine, near_columns, table, starts, *chosen = lax.optimization_barrier(
        (cosine, sine, near_columns, table, starts, *chosen)
    )
    q_weights = gather(w_query, far)
    out_weights = gather(w_out, q_weights[2])

    fetch_sems = pltpu.SemaphoreType.DMA((n_shard,))
    hidden, kv, gain_one, gain_two = call_once(
        functools.partial(keys_kernel, sizes=sizes, kvw=kvw),
        [((count, width), BF16), ((count, 2 * kvw), BF16), ((1, width), F32), ((1, width), F32)],
        [x, cosine, sine],
        held=[starts],
        moved=kv_weights,
        scratch=[
            pltpu.VMEM((width, 2 * kvw), BF16),
            pltpu.VMEM((n_shard, 16, 2 * kvw), BF16),
            fetch_sems,
            fetch_sems,
        ],
        flops=4 * count * width * kvw,
        limit=ALL_VMEM,
        name="keys",
    )
    all_kv = collect(kv)

    (queries,) = call_once(
        functools.partial(queries_kernel, sizes=sizes),
        [((count, qw), BF16)],
        [hidden, cosine, sine],
        held=[starts],
        moved=q_weights,
        scratch=[pltpu.VMEM((width, qw), BF16), fetch_sems],
        flops=2 * count * width * qw,
        name="queries",
    )

    far_tiles = [
        hop(after(part, (out_weights[2], queries)), k) for part, k in zip(chosen, (2, 3))
    ]
    far_tile = jnp.concatenate(far_tiles, axis=0)
    far_rows = collect(after(far_tile, kv)[None])
    near_part = hop(near_columns, 1)
    cot_near = hop(cot, 1)
    cot_far = hop(after(cot, far_tile), 2)

    shared = dict(sizes=sizes, groups=groups, per=per, blocks=blocks)
    fixed = lambda *shape: pl.BlockSpec(shape, lambda step, table: (0,) * len(shape))
    kv_spec = pl.BlockSpec(
        (count, 2 * kvw), lambda step, table: (table[jnp.minimum(step, table[blocks])], 0)
    )
    once = lambda *shape: block(shape)
    weight_specs = [HBM_SPEC] * len(sizes)
    span = per * count
    out_tall, attended, log_total, mid, normed, q_cols = pl.pallas_call(
        functools.partial(attend_kernel, **shared),
        out_shape=(
            jax.ShapeDtypeStruct((qw, count), F32),
            jax.ShapeDtypeStruct((count, qw), BF16),
            jax.ShapeDtypeStruct((8, span), F32),
            jax.ShapeDtypeStruct((count, width), F32),
            jax.ShapeDtypeStruct((count, width), BF16),
            jax.ShapeDtypeStruct((groups, HEAD, span), BF16),
        ),
        grid_spec=pltpu.PrefetchScalarGridSpec(
            num_scalar_prefetch=1,
            grid=(blocks,),
            in_specs=[once(count, qw), kv_spec, once(count, width), once(1, width)]
            + weight_specs,
            out_specs=[
                fixed(qw, count),
                fixed(count, qw),
                fixed(8, span),
                fixed(count, width),
                fixed(count, width),
                fixed(groups, HEAD, span),
            ],
            scratch_shapes=[
                pltpu.VMEM((groups, HEAD, span), F32),
                pltpu.VMEM((8, span), F32),
                pltpu.VMEM((8, span), F32),
                pltpu.VMEM((qw, width), BF16),
                pltpu.VMEM((2, count, span), F32),
                pltpu.VMEM((qw, count), F32),
                pltpu.SemaphoreType.DMA((len(sizes),)),
            ],
        ),
        compiler_params=params(),
        cost_estimate=cost(
            4 * count * count * blocks * qw, 12e6, count * count * blocks * groups * per
        ),
        name="attend",
    )(table, queries, all_kv, x, gain_two, *out_weights)

    normed_far = hop(normed, 2)
    normed_near = hop(normed, 1)
    cot_far = after(cot_far, normed)
    far_rows = after(far_rows, normed)
    all_count = n_shard * count
    if aligned:
        two = ((2, count, ff_own), BF16)
        mats = [((width, ff_own), BF16)] * 2
        pair = (2, count, width)
        gate_mat, up_mat, *near_units, back = pl.pallas_call(
            functools.partial(feed_near_kernel, half=half, lanes=lanes),
            out_shape=tuple(
                jax.ShapeDtypeStruct(*out) for out in [*mats, two, two, two, (pair, BF16)]
            ),
            in_specs=[SMEM_SPEC] + [HBM_SPEC] * 9,
            out_specs=(HBM_SPEC,) * 6,
            scratch_shapes=[
                pltpu.VMEM((width, ff_own), BF16),
                pltpu.VMEM((width, ff_own), BF16),
                pltpu.VMEM((ff_own, width), BF16),
                pltpu.VMEM(pair, BF16),
                pltpu.VMEM(pair, BF16),
                pltpu.VMEM(*two),
                pltpu.VMEM(*two),
                pltpu.VMEM(*two),
                pltpu.VMEM(pair, BF16),
                pltpu.SemaphoreType.DMA((4 + 2 * n_ctx,)),
                pltpu.SemaphoreType.DMA((3, 2)),
                pltpu.SemaphoreType.DMA((6,)),
            ],
            compiler_params=params(),
            cost_estimate=cost(10 * 2 * count * width * ff_own, 12e6),
            name="feed_near",
        )(
            starts,
            w_gate,
            w_up,
            near_part,
            far_rows,
            w_down,
            normed,
            normed_near,
            cot,
            cot_near,
        )
        normed_far, cot_far = lax.optimization_barrier((normed_far, cot_far, back))[:2]
        normed_pieces = [normed, normed_near, normed_far, hop(normed_far, 1)]
        cot_pieces = [cot, cot_near, cot_far, hop(cot_far, 1)]
        late = ((2 * count, ff_own), BF16)
        feed_tiles, *far_units = pl.pallas_call(
            functools.partial(feed_far_kernel, per_shard=per_shard),
            out_shape=tuple(
                jax.ShapeDtypeStruct(*out)
                for out in [((n_ctx, 3 * rows, tile), BF16), late, late, late]
            ),
            in_specs=[SMEM_SPEC] + [HBM_SPEC] * (6 + 2 * n_shard),
            out_specs=(HBM_SPEC,) * 4,
            scratch_shapes=[
                pltpu.VMEM((width, ff_own), BF16),
                pltpu.VMEM((width, ff_own), BF16),
                pltpu.VMEM((ff_own, width), BF16),
                pltpu.VMEM((n_shard, count, width), BF16),
                pltpu.VMEM((all_count, width), BF16),
                pltpu.VMEM((width, all_count), BF16),
                pltpu.VMEM((all_count, ff_own), BF16),
                pltpu.VMEM((all_count, ff_own), BF16),
                pltpu.VMEM((all_count, ff_own), BF16),
                pltpu.VMEM((n_ctx, 3 * rows, tile), BF16),
                pltpu.SemaphoreType.DMA((3,)),
                pltpu.SemaphoreType.DMA((n_shard,)),
                pltpu.SemaphoreType.DMA((n_shard,)),
                pltpu.SemaphoreType.DMA((3, 2)),
                pltpu.SemaphoreType.DMA((3,)),
                pltpu.SemaphoreType.DMA((2, n_ctx)),
            ],
            compiler_params=params(),
            cost_estimate=cost(9 * all_count * width * ff_own, 25e6),
            name="feed_far",
        )(
            starts, gate_mat, up_mat, w_down, *near_units, *normed_pieces, *cot_pieces
        )
        to_own, to_near = back[0], back[1]
        act_parts = [near_units[0].reshape(2 * count, ff_own), far_units[0]]
        grad_gate_far, grad_up_far = far_units[1:]
    else:
        normed_pieces = [normed, normed_near, normed_far, hop(normed_far, 1)]
        cot_pieces = [cot, cot_near, cot_far, hop(cot_far, 1)]
        tiles_of = far_rows.reshape(n_ctx // 2, 2, 2, half, lanes)
        tiles_of = tiles_of.transpose(2, 1, 3, 0, 4).reshape(2, rows, 2 * ff_own)
        gate_mat = jnp.zeros((width, ff_own), BF16)
        up_mat = jnp.zeros((width, ff_own), BF16)
        for part, start in zip((columns(shard), near_part, tiles_of[0], tiles_of[1]), starts):
            gate_mat = lax.dynamic_update_slice_in_dim(gate_mat, part[:, :ff_own], start, 0)
            up_mat = lax.dynamic_update_slice_in_dim(up_mat, part[:, ff_own:], start, 0)
        all_cot = jnp.concatenate(cot_pieces, axis=0)
        all_normed = jnp.concatenate(normed_pieces, axis=0)
        gate = nn(all_normed, gate_mat)
        up = nn(all_normed, up_mat)
        grad_activated = nt(all_cot, w_down)
        sigmoid = jax.nn.sigmoid(gate)
        activated = (gate * sigmoid * up).astype(BF16)
        grad_gate = (grad_activated * up * (sigmoid * (1.0 + gate * (1.0 - sigmoid)))).astype(BF16)
        grad_up = (grad_activated * (gate * sigmoid)).astype(BF16)

        def tiles(grad):
            pieces = grad.astype(BF16).reshape(n_shard, rows, per_shard, tile)
            pieces = pieces.transpose(0, 2, 1, 3)
            return jnp.roll(pieces, shard, axis=0).reshape(n_ctx, rows, tile)

        down = tn(activated, all_cot).astype(BF16)
        down = down.reshape(n_ctx, ff_own // n_ctx, width // tile, tile).transpose(0, 2, 1, 3)
        feed_tiles = jnp.concatenate(
            [
                tiles(tn(all_normed, grad_gate)),
                tiles(tn(all_normed, grad_up)),
                down.reshape(n_ctx, rows, tile),
            ],
            axis=1,
        )
        grad_gate_far, grad_up_far = grad_gate[2 * count :], grad_up[2 * count :]
        back = nt(grad_gate[: 2 * count], gate_mat) + nt(grad_up[: 2 * count], up_mat)
        to_own, to_near = back[:count].astype(BF16), back[count:].astype(BF16)
        act_parts = [activated[: 2 * count], activated[2 * count :]]
    from_near = hop(to_near, 1)
    feed_sum = scatter(feed_tiles)
    down_sum = feed_sum[2 * rows :]
    pairs = []
    for index in range(n_ctx):
        for source in range(n_shard):
            target = (places[index] // per_shard - source) % n_shard
            pairs.append((index * n_shard + source, index * n_shard + target))
    gate_up_sum = lax.ppermute(feed_sum[: 2 * rows], ("ctx", "shard"), pairs)

    to_far, to_third = call_once(
        normed_back_kernel,
        [((count, width), BF16)] * 2,
        [grad_gate_far, grad_up_far, gate_mat, up_mat],
        flops=8 * count * width * ff_own,
        limit=ALL_VMEM,
        name="normed_back",
    )
    third = hop(to_third, 1)
    across = (to_far.astype(F32) + third.astype(F32)).astype(BF16)
    from_far = hop(across, 2)

    part_out = [after(nn(part, w_down).astype(BF16), from_far) for part in act_parts]
    part_out = [part[k * count : (k + 1) * count] for part in part_out for k in range(2)]
    output = (mid + add(reduce(part_out))).astype(BF16)[None]

    place_spec = pl.BlockSpec((count, 2 * kvw), lambda step, table: (table[step], 0))
    grad_query, grad_kv, branch, grad_mid, gain_two_part = pl.pallas_call(
        functools.partial(attend_back_kernel, **shared),
        out_shape=(
            jax.ShapeDtypeStruct((count, qw), BF16),
            jax.ShapeDtypeStruct((blocks * count, 2 * kvw), BF16),
            jax.ShapeDtypeStruct((count, width), BF16),
            jax.ShapeDtypeStruct((count, width), F32),
            jax.ShapeDtypeStruct((1, width), F32),
        ),
        grid_spec=pltpu.PrefetchScalarGridSpec(
            num_scalar_prefetch=1,
            grid=(blocks,),
            in_specs=[
                kv_spec,
                once(groups, HEAD, span),
                once(qw, count),
                once(8, span),
                once(count, width),
                once(1, width),
                once(count, width),
                once(count, width),
                once(count, width),
                once(count, width),
                once(count, LANES),
                once(count, LANES),
            ]
            + weight_specs,
            out_specs=[
                fixed(count, qw),
                place_spec,
                fixed(count, width),
                fixed(count, width),
                fixed(1, width),
            ],
            scratch_shapes=[
                pltpu.VMEM((qw, width), BF16),
                pltpu.VMEM((groups, HEAD, span), BF16),
                pltpu.VMEM((8, span), F32),
                pltpu.VMEM((groups, HEAD, span), F32),
                pltpu.VMEM((2, 2, count, span), F32),
                pltpu.VMEM((qw, count), F32),
                pltpu.SemaphoreType.DMA((len(sizes),)),
            ],
        ),
        compiler_params=params(),
        cost_estimate=cost(
            10 * count * count * blocks * qw, 14e6, count * count * blocks * groups * per
        ),
        name="attend_back",
    )(
        table,
        all_kv,
        q_cols,
        out_tall,
        log_total,
        mid,
        gain_two,
        cot,
        to_own,
        from_near,
        from_far,
        cosine,
        sine,
        *out_weights,
    )
    own_kv = scatter(after(grad_kv, down_sum).reshape(n_ctx, count, 2 * kvw))

    def stack(parts, breadth, name):
        height = sum(part.shape[0] * part.shape[1] for part in parts[::3]) // breadth
        if breadth % LANES:
            wide = jnp.concatenate(
                [add(parts[index : index + 3]) for index in range(0, len(parts), 3)], axis=1
            )
            wide = wide.astype(BF16).reshape(rows, -1, breadth)
            return wide.transpose(1, 0, 2).reshape(height, breadth)
        return call_once(stack_kernel, [((height, breadth), BF16)], parts, flops=1e6, name=name)[0]

    grad_blocks = call_once(
        weight_grads_kernel,
        [((rows, qw), BF16)] * n_shard + [((rows, width), BF16)] * n_shard,
        [hidden, grad_query, attended, branch],
        held=[starts],
        scratch=[pltpu.VMEM((width, qw), F32)],
        flops=4 * count * width * qw,
        limit=ALL_VMEM,
        name="weight_grads",
    )
    parts_query = reduce(grad_blocks[:n_shard])
    parts_out = reduce(grad_blocks[n_shard:])
    mixed = stack(parts_query + parts_out, tile, "stack_mixed")
    mixed_sum = scatter(after(mixed, own_kv).reshape(n_ctx, -1, tile))

    grad_kv_pre, *kv_blocks = call_once(
        functools.partial(kv_back_kernel, kvw=kvw),
        [((count, 2 * kvw), BF16)] + [((rows, 2 * kvw), BF16)] * n_shard,
        [own_kv, cosine, sine, hidden],
        held=[starts],
        scratch=[pltpu.VMEM((width, 2 * kvw), F32)],
        flops=4 * count * width * kvw,
        name="kv_back",
    )
    sum_kv = stack(reduce(kv_blocks), LANES, "stack_kv").reshape(n_ctx, -1, LANES)
    shares = jnp.concatenate([gate_up_sum, down_sum, mixed_sum])
    gathered = collect(after(shares, sum_kv)[None])

    def exchange(value):
        return lax.all_to_all(value, "ctx", split_axis=0, concat_axis=0, tiled=True)

    own_sum = jnp.sum(exchange(sum_kv).astype(F32), axis=0, keepdims=True).astype(BF16)
    both = exchange(jnp.broadcast_to(own_sum, sum_kv.shape))
    both = both.reshape(2 * kvw // LANES, rows, LANES).transpose(1, 0, 2).reshape(rows, 2 * kvw)
    grad_w_key = both[:, :kvw].astype(F32)
    grad_w_value = both[:, kvw:].astype(F32)

    grad_x, gain_one_part = call_once(
        functools.partial(inputs_kernel, sizes=sizes),
        [((count, width), BF16), ((1, width), F32)],
        [grad_query, grad_kv_pre, x, gain_one, grad_mid],
        held=[starts],
        moved=[*q_weights, *kv_weights],
        scratch=[
            pltpu.VMEM((width, qw), BF16),
            pltpu.VMEM((width, 2 * kvw), BF16),
            fetch_sems,
            fetch_sems,
        ],
        flops=2 * count * width * (qw + 2 * kvw),
        name="grad_inputs",
    )

    gain_parts = jnp.concatenate([gain_one_part, gain_two_part], axis=0)
    for distance in [1 << bit for bit in range(n_shard.bit_length() - 1)]:
        gain_parts = gain_parts + hop(gain_parts, distance)
    for distance in [1 << bit for bit in range(n_ctx.bit_length() - 1)]:
        gain_parts = gain_parts + ctx_hop(gain_parts, distance)
    own_gains = lax.dynamic_slice_in_dim(gain_parts, shard * rows, rows, 1)

    if aligned:
        share = mixed_sum.shape[0]
        rolled = lambda step, where: (lax.rem(step + where[0] * per_shard, n_ctx), 0, 0)
        band = ff_own // n_ctx
        grad_w_gate, grad_w_up, grad_w_down, grad_w_query, grad_w_out = pl.pallas_call(
            functools.partial(widen_kernel, rows=rows),
            out_shape=(
                jax.ShapeDtypeStruct((rows, ff), F32),
                jax.ShapeDtypeStruct((rows, ff), F32),
                jax.ShapeDtypeStruct((ff_own, width), F32),
                jax.ShapeDtypeStruct((rows, qw), F32),
                jax.ShapeDtypeStruct((rows, width), F32),
            ),
            grid_spec=pltpu.PrefetchScalarGridSpec(
                num_scalar_prefetch=1,
                grid=(n_ctx,),
                in_specs=[
                    pl.BlockSpec((1, 2 * rows, tile), rolled),
                    pl.BlockSpec((1, rows, tile), lambda step, where: (step, 2, 0)),
                    pl.BlockSpec((1, share, tile), lambda step, where: (step, 3 * rows // share, 0)),
                ],
                out_specs=[
                    pl.BlockSpec((rows, tile), lambda step, where: (0, step)),
                    pl.BlockSpec((rows, tile), lambda step, where: (0, step)),
                    pl.BlockSpec((band, width), lambda step, where: (step, 0)),
                    pl.BlockSpec((rows, qw), lambda step, where: (0, 0)),
                    pl.BlockSpec((rows, width), lambda step, where: (0, 0)),
                ],
                scratch_shapes=[pltpu.VMEM((n_ctx * share, tile), F32)],
            ),
            compiler_params=params(),
            cost_estimate=cost(1e6, 20e6),
            name="widen",
        )(shard_arr, gathered, gathered, gathered)
    else:

        def untile(part):
            back = jnp.roll(part.reshape(n_shard, per_shard, rows, tile), -shard, axis=0)
            back = back.reshape(n_ctx, rows, tile).transpose(1, 0, 2)
            return back.reshape(rows, ff).astype(F32)

        grad_w_gate = untile(gathered[:, :rows])
        grad_w_up = untile(gathered[:, rows : 2 * rows])
        down = gathered[:, 2 * rows : 3 * rows].reshape(n_ctx, width // tile, -1, tile)
        grad_w_down = down.transpose(0, 2, 1, 3).reshape(ff_own, width).astype(F32)
        wide = gathered[:, 3 * rows :].reshape(2 * qw // tile, rows, tile).transpose(1, 0, 2)
        wide = wide.reshape(rows, 2 * qw).astype(F32)
        grad_w_query, grad_w_out = wide[:, :qw], wide[:, qw:]

    return (
        output,
        grad_x[None],
        own_gains[0],
        grad_w_query,
        grad_w_key,
        grad_w_value,
        grad_w_out,
        own_gains[1],
        grad_w_gate,
        grad_w_up,
        grad_w_down,
    )


def solution(mesh):
    tokens = P("shard", "ctx", None)
    split = P("shard", None)
    gain = P("shard")
    placed = (tokens, gain, split, split, split, split, gain, split, split, split, tokens)
    return jax.shard_map(
        functools.partial(on_device, n_ctx=mesh.shape["ctx"], n_shard=mesh.shape["shard"]),
        mesh=mesh,
        in_specs=placed,
        out_specs=(tokens, tokens, gain, split, split, split, split, gain, split, split, split),
        check_vma=False,
    )
```

```python
import functools
import math

import jax
import jax.numpy as jnp
from jax import lax
from jax.experimental import pallas as pl
from jax.experimental.pallas import tpu as pltpu
from jax.sharding import PartitionSpec as P

HEAD = 64
BLOCK = 256
EPSILON = 1e-05
LANES = 128
F32 = jnp.float32
BF16 = jnp.bfloat16
SCORE_SCALE = math.log2(math.e) * 0.125
NEGATIVE = -1e30
ALL_VMEM = 60 * 1024 * 1024
PART_VMEM = 32 * 1024 * 1024


def nn(left, right):
    return lax.dot_general(left, right, (((1,), (0,)), ((), ())), preferred_element_type=F32)


def nt(left, right):
    return lax.dot_general(left, right, (((1,), (1,)), ((), ())), preferred_element_type=F32)


def tn(left, right):
    return lax.dot_general(left, right, (((0,), (0,)), ((), ())), preferred_element_type=F32)


def ring_order(count):
    return list(range(0, count, 2)) + list(range(count - 1, 0, -2))


def ring_place(index, count):
    return jnp.where(index % 2 == 0, index // 2, count - 1 - index // 2)


def params(limit=ALL_VMEM):
    return pltpu.CompilerParams(vmem_limit_bytes=limit)


def cost(flops, moved, exps=0):
    return pl.CostEstimate(flops=int(flops), bytes_accessed=int(moved), transcendentals=int(exps))


HBM_SPEC = pl.BlockSpec(memory_space=pltpu.HBM)
SMEM_SPEC = pl.BlockSpec(memory_space=pltpu.SMEM)


def block(shape):
    return pl.BlockSpec(shape, lambda *_: (0,) * len(shape), pipeline_mode=pl.Buffered(1))


def call_once(
    kernel, outs, ins, held=(), moved=(), scratch=(), flops=0, limit=PART_VMEM, name=None
):
    return pl.pallas_call(
        kernel,
        out_shape=tuple(jax.ShapeDtypeStruct(shape, dtype) for shape, dtype in outs),
        grid=(1,),
        in_specs=[SMEM_SPEC] * len(held)
        + [block(array.shape) for array in ins]
        + [HBM_SPEC] * len(moved),
        out_specs=tuple(pl.BlockSpec(shape, lambda *_: (0,) * len(shape)) for shape, _ in outs),
        scratch_shapes=list(scratch),
        compiler_params=params(limit),
        cost_estimate=cost(flops, sum(2 * math.prod(shape) for shape, _ in outs) + 4e6),
        name=name,
    )(*held, *ins, *moved)


def swap_halves(tile):
    lane = lax.broadcasted_iota(jnp.int32, tile.shape, 1)
    ahead = pltpu.roll(tile, LANES - HEAD // 2, 1)
    behind = pltpu.roll(tile, HEAD // 2, 1)
    return jnp.where(lane % HEAD < HEAD // 2, ahead, behind)


def row_start(ids_ref, hop, rows):
    return pl.multiple_of((ids_ref[0] ^ hop) * rows, 16)


def fetches(ids_ref, pieces, whole, sems, sizes, column=0):
    copies = []
    for index, (piece, size) in enumerate(zip(pieces, sizes)):
        start = row_start(ids_ref, index, size)
        copies.append(
            pltpu.make_async_copy(
                piece.at[pl.ds(0, size), pl.ds(column, whole.shape[1])],
                whole.at[pl.ds(start, size), :],
                sems.at[index],
            )
        )
    return copies


def keys_kernel(ids_ref, x_ref, cos_ref, sin_ref, *rest, sizes, kvw):
    pieces = rest[: len(sizes)]
    hidden_ref, kv_ref, one_ref, two_ref, whole, bands, sems, band_sems = rest[len(sizes) :]
    copies = fetches(ids_ref, pieces, whole, sems, sizes)
    rows = sizes[0]
    for index, piece in enumerate(pieces):
        band = pltpu.make_async_copy(
            piece.at[pl.ds(rows, 16), :], bands.at[index], band_sems.at[index]
        )
        band.start()
        copies[index].start()
    x = x_ref[...].astype(F32)
    scale = lax.rsqrt(jnp.mean(x * x, axis=-1, keepdims=True) + EPSILON)
    width = x.shape[1]
    ones = jnp.zeros((8, width), F32)
    twos = jnp.zeros((8, width), F32)
    for index, piece in enumerate(pieces):
        pltpu.make_async_copy(
            piece.at[pl.ds(rows, 16), :], bands.at[index], band_sems.at[index]
        ).wait()
        band = bands[index].astype(F32)[:8, :]
        blank = jnp.zeros((8, width - rows), F32)
        first = jnp.concatenate([band[:, :rows], blank], axis=1)
        second = jnp.concatenate([band[:, rows : 2 * rows], blank], axis=1)
        ones = ones + pltpu.roll(first, (ids_ref[0] ^ index) * rows, 1)
        twos = twos + pltpu.roll(second, (ids_ref[0] ^ index) * rows, 1)
    one_ref[...] = ones[:1, :]
    two_ref[...] = twos[:1, :]
    hidden = (x * scale * ones[:1, :]).astype(BF16)
    hidden_ref[...] = hidden
    for copy in copies:
        copy.wait()
    pre = nn(hidden, whole[...])
    for start in range(0, kvw, LANES):
        tile = pre[:, start : start + LANES]
        turned = tile * cos_ref[...] + swap_halves(tile) * sin_ref[...]
        kv_ref[:, start : start + LANES] = turned.astype(BF16)
    kv_ref[:, kvw:] = pre[:, kvw:].astype(BF16)


def queries_kernel(ids_ref, hidden_ref, cos_ref, sin_ref, *rest, sizes):
    pieces = rest[: len(sizes)]
    query_ref, whole, sems = rest[len(sizes) :]
    copies = fetches(ids_ref, pieces, whole, sems, sizes)
    for copy in copies:
        copy.start()
    for copy in copies:
        copy.wait()
    pre = nn(hidden_ref[...], whole[...])
    for start in range(0, pre.shape[1], LANES):
        tile = pre[:, start : start + LANES]
        turned = tile * cos_ref[...] + swap_halves(tile) * sin_ref[...]
        query_ref[:, start : start + LANES] = turned.astype(BF16)


def attend_kernel(
    table_ref,
    q_ref,
    kv_ref,
    x_ref,
    gain_ref,
    *rest,
    sizes,
    column,
    groups,
    per,
    blocks,
):
    pieces = rest[:-13]
    (
        out_ref,
        attended_ref,
        log_ref,
        mid_ref,
        normed_ref,
        cols_ref,
        acc,
        top,
        total,
        whole,
        scores,
        tall,
        sems,
    ) = rest[-13:]
    step = pl.program_id(0)
    last = table_ref[1]
    count = q_ref.shape[0]
    kvw = groups * HEAD

    @pl.when(step == 0)
    def _():
        for copy in fetches(table_ref, pieces, whole, sems, sizes, column):
            copy.start()
        turned = q_ref[...].T
        for group in range(groups):
            for member in range(per):
                head = group * per + member
                cols_ref[group, :, member * count : (member + 1) * count] = turned[
                    head * HEAD : (head + 1) * HEAD, :
                ]
        acc[...] = jnp.zeros_like(acc)
        total[...] = jnp.zeros_like(total)
        top[...] = jnp.full_like(top, NEGATIVE)

    @pl.when(step <= last)
    def _():
        def score(group):
            key = kv_ref[:, group * HEAD : (group + 1) * HEAD]
            scores[group % 2] = nn(key, cols_ref[group])

        score(0)
        for group in range(groups):
            if group + 1 < groups:
                score(group + 1)
            value = kv_ref[:, kvw + group * HEAD : kvw + (group + 1) * HEAD]
            raw = scores[group % 2]
            old = top[group : group + 1, :]
            new = jnp.maximum(old, jnp.max(raw, axis=0, keepdims=True))
            shrink = jnp.exp2((old - new) * SCORE_SCALE)
            probs = jnp.exp2((raw - new) * SCORE_SCALE)
            top[group : group + 1, :] = new
            total[group : group + 1, :] = total[group : group + 1, :] * shrink + jnp.sum(
                probs, axis=0, keepdims=True
            )
            acc[group] = acc[group] * shrink + tn(value, probs.astype(BF16))

    @pl.when(step == blocks - 1)
    def _():
        for group in range(groups):
            sums = total[group : group + 1, :]
            log_ref[group : group + 1, :] = top[
                group : group + 1, :
            ] * SCORE_SCALE + jnp.log2(sums)
            rowed = acc[group] / sums
            for member in range(per):
                head = group * per + member
                tall[head * HEAD : (head + 1) * HEAD, :] = rowed[
                    :, member * count : (member + 1) * count
                ]
        out_ref[...] = tall[...]
        attended = tall[...].astype(BF16).T
        attended_ref[...] = attended
        for copy in fetches(table_ref, pieces, whole, sems, sizes, column):
            copy.wait()
        mid = x_ref[...].astype(F32) + nn(attended, whole[...])
        mid_ref[...] = mid
        scale = lax.rsqrt(jnp.mean(mid * mid, axis=-1, keepdims=True) + EPSILON)
        normed_ref[...] = (mid * scale * gain_ref[...]).astype(BF16)


def attend_back_kernel(
    table_ref,
    kv_ref,
    cols_ref,
    out_ref,
    log_ref,
    mid_ref,
    gain_ref,
    cot_ref,
    gn_own_ref,
    gn_near_ref,
    gn_far_ref,
    cos_ref,
    sin_ref,
    *rest,
    sizes,
    column,
    groups,
    per,
    blocks,
):
    pieces = rest[: len(sizes)]
    (
        gq_ref,
        gkv_ref,
        branch_ref,
        gmid_ref,
        ggain_ref,
        whole,
        d_cols,
        delta,
        acc,
        probs_all,
        tall,
        sems,
    ) = rest[len(sizes) :]
    step = pl.program_id(0)
    last = table_ref[1]
    count = kv_ref.shape[0]
    kvw = groups * HEAD

    @pl.when(step == 0)
    def _():
        copies = fetches(table_ref, pieces, whole, sems, sizes, column)
        for copy in copies:
            copy.start()
        mid = mid_ref[...]
        incoming = (
            gn_own_ref[...].astype(F32) + gn_near_ref[...].astype(F32)
        ) + gn_far_ref[...].astype(F32)
        gain = gain_ref[...]
        scale = lax.rsqrt(jnp.mean(mid * mid, axis=-1, keepdims=True) + EPSILON)
        weighted = incoming * gain
        inner = jnp.mean(weighted * mid, axis=-1, keepdims=True)
        ggain_ref[...] = jnp.sum(incoming * mid * scale, axis=0, keepdims=True)
        grad_mid = (
            cot_ref[...].astype(F32) + scale * weighted - mid * (scale * scale * scale * inner)
        )
        gmid_ref[...] = grad_mid
        branch = grad_mid.astype(BF16)
        branch_ref[...] = branch
        for copy in copies:
            copy.wait()
        grads = nt(branch, whole[...]).astype(BF16)
        turned = grads.T
        tall[...] = turned.astype(F32) * out_ref[...]
        for group in range(groups):
            for member in range(per):
                head = group * per + member
                span = slice(head * HEAD, (head + 1) * HEAD)
                cols = slice(member * count, (member + 1) * count)
                d_cols[group, :, cols] = turned[span, :]
                delta[group : group + 1, cols] = jnp.sum(tall[span, :], axis=0, keepdims=True)
        acc[...] = jnp.zeros_like(acc)

    @pl.when(step > last)
    def _():
        gkv_ref[...] = jnp.zeros_like(gkv_ref)

    @pl.when(step <= last)
    def _():
        def spans(group):
            return (
                slice(group * HEAD, (group + 1) * HEAD),
                slice(kvw + group * HEAD, kvw + (group + 1) * HEAD),
            )

        def score(group):
            key_span, value_span = spans(group)
            probs_all[group % 2, 0] = nn(kv_ref[:, key_span], cols_ref[group])
            probs_all[group % 2, 1] = nn(kv_ref[:, value_span], d_cols[group])

        score(0)
        for group in range(groups):
            if group + 1 < groups:
                score(group + 1)
            key_span, value_span = spans(group)
            probs = jnp.exp2(
                probs_all[group % 2, 0] * SCORE_SCALE - log_ref[group : group + 1, :]
            )
            grad_scores = (
                probs * (probs_all[group % 2, 1] - delta[group : group + 1, :])
            ).astype(BF16)
            gkv_ref[:, value_span] = nt(probs.astype(BF16), d_cols[group]).astype(BF16)
            gkv_ref[:, key_span] = (nt(grad_scores, cols_ref[group]) * 0.125).astype(BF16)
            acc[group] = acc[group] + tn(kv_ref[:, key_span], grad_scores)

    @pl.when(step == blocks - 1)
    def _():
        for group in range(groups):
            for member in range(per):
                head = group * per + member
                tall[head * HEAD : (head + 1) * HEAD, :] = (
                    acc[group, :, member * count : (member + 1) * count] * 0.125
                )
        for start in range(0, tall.shape[0], LANES):
            tile = tall[start : start + LANES, :].T
            turned = tile * cos_ref[...] - swap_halves(tile) * sin_ref[...]
            gq_ref[:, start : start + LANES] = turned.astype(BF16)


def kv_back_kernel(ids_ref, grad_ref, cos_ref, sin_ref, hidden_ref, out_ref, *rest, kvw):
    outs, full = rest[:-1], rest[-1]
    for start in range(0, kvw, LANES):
        tile = grad_ref[:, start : start + LANES].astype(F32)
        turned = tile * cos_ref[...] - swap_halves(tile) * sin_ref[...]
        out_ref[:, start : start + LANES] = turned.astype(BF16)
    out_ref[:, kvw:] = grad_ref[:, kvw:]
    full[...] = tn(hidden_ref[...], out_ref[...])
    for index, out in enumerate(outs):
        start = row_start(ids_ref, index, out.shape[0])
        out[...] = full[pl.ds(start, out.shape[0]), :].astype(BF16)


def stack_kernel(*refs):
    parts, out_ref = refs[:-1], refs[-1]
    tile = out_ref.shape[1]
    row = 0
    for index in range(0, len(parts), 3):
        first, second, third = parts[index : index + 3]
        rows, columns = first.shape
        for start in range(0, columns, tile):
            span = slice(start, start + tile)
            total = (
                first[:, span].astype(F32) + second[:, span].astype(F32)
            ) + third[:, span].astype(F32)
            out_ref[row : row + rows, :] = total.astype(BF16)
            row += rows


def inputs_kernel(ids_ref, gq_ref, gkv_ref, x_ref, gain_ref, gmid_ref, *rest, sizes):
    hops = len(sizes)
    grad_ref, ggain_ref, whole_q, whole_kv, q_sems, kv_sems = rest[2 * hops :]
    copies = fetches(ids_ref, rest[:hops], whole_q, q_sems, sizes)
    copies += fetches(ids_ref, rest[hops : 2 * hops], whole_kv, kv_sems, sizes)
    for copy in copies:
        copy.start()
    for copy in copies:
        copy.wait()
    incoming = nt(gq_ref[...], whole_q[...]) + nt(gkv_ref[...], whole_kv[...])
    x = x_ref[...].astype(F32)
    scale = lax.rsqrt(jnp.mean(x * x, axis=-1, keepdims=True) + EPSILON)
    weighted = incoming * gain_ref[...]
    inner = jnp.mean(weighted * x, axis=-1, keepdims=True)
    ggain_ref[...] = jnp.sum(incoming * x * scale, axis=0, keepdims=True)
    grad = gmid_ref[...] + scale * weighted - x * (scale * scale * scale * inner)
    grad_ref[...] = grad.astype(BF16)


def weight_grads_kernel(ids_ref, hidden_ref, query_ref, attended_ref, branch_ref, *rest):
    outs, full = rest[:-1], rest[-1]
    hops = len(outs) // 2
    for index, (left, right) in enumerate(((hidden_ref, query_ref), (attended_ref, branch_ref))):
        full[...] = tn(left[...], right[...])
        for hop, out in enumerate(outs[index * hops : (index + 1) * hops]):
            start = row_start(ids_ref, hop, out.shape[0])
            out[...] = full[pl.ds(start, out.shape[0]), :].astype(BF16)


def units(normed, cot, gate_mat, up_mat, down_mat):
    gate = nn(normed, gate_mat)
    up = nn(normed, up_mat)
    grad = nt(cot, down_mat)
    sigmoid = 1.0 / (1.0 + jnp.exp(-gate))
    silu = gate * sigmoid
    return (
        (silu * up).astype(BF16),
        (grad * up * (sigmoid * (1.0 + gate * (1.0 - sigmoid)))).astype(BF16),
        (grad * silu).astype(BF16),
    )


def feed_near_kernel(
    ids_ref, own_gate_ref, own_up_ref, near_ref, far_ref, down_ref, *rest, half, lanes
):
    normed_refs, cot_refs = rest[:2], rest[2:4]
    gate_mat_out, up_mat_out, act_out, gate_out, up_out, back_out = rest[4:10]
    gate_mat, up_mat, down_mat, tokens, cots, act, grad_gate, grad_up, back = rest[10:19]
    mat_sems, token_sems, out_sems = rest[19:]
    rows = near_ref.shape[0]
    own = gate_mat.shape[1]
    mats = []

    def place(source, row, column, height, breadth):
        target = gate_mat if column < own else up_mat
        mats.append(
            pltpu.make_async_copy(
                source,
                target.at[pl.ds(row, height), pl.ds(column % own, breadth)],
                mat_sems.at[len(mats)],
            )
        )

    mine = pl.ds(pl.multiple_of(ids_ref[0] * own, LANES), own)
    for index, ref in enumerate((own_gate_ref, own_up_ref)):
        place(ref.at[:, mine], row_start(ids_ref, 0, rows), index * own, rows, own)
        place(
            near_ref.at[:, pl.ds(index * own, own)],
            row_start(ids_ref, 1, rows),
            index * own,
            rows,
            own,
        )
    for spot in range(far_ref.shape[0]):
        for index in range(2):
            place(
                far_ref.at[spot, pl.ds(index * half, half), :],
                pl.multiple_of(row_start(ids_ref, 2 + index, rows) + (spot % 2) * half, 16),
                (spot // 2) * lanes,
                half,
                lanes,
            )
    count = tokens.shape[0] // 2
    loads = [
        pltpu.make_async_copy(
            ref, target.at[pl.ds(index * count, count), :], token_sems.at[slot, index]
        )
        for slot, (refs, target) in enumerate(((normed_refs, tokens), (cot_refs, cots)))
        for index, ref in enumerate(refs)
    ]
    loads.append(pltpu.make_async_copy(down_ref, down_mat, token_sems.at[2, 0]))
    for copy in mats + loads:
        copy.start()
    for copy in mats:
        copy.wait()
    outs = [
        pltpu.make_async_copy(source, target, out_sems.at[index])
        for index, (source, target) in enumerate(
            (
                (gate_mat, gate_mat_out),
                (up_mat, up_mat_out),
                (act, act_out),
                (grad_gate, gate_out),
                (grad_up, up_out),
                (back, back_out),
            )
        )
    ]
    for copy in outs[:2]:
        copy.start()
    for copy in loads:
        copy.wait()

    act[...], grad_gate[...], grad_up[...] = units(
        tokens[...], cots[...], gate_mat[...], up_mat[...], down_mat[...]
    )
    back[...] = (
        nt(grad_gate[...], gate_mat[...]) + nt(grad_up[...], up_mat[...])
    ).astype(BF16)
    for copy in outs[2:]:
        copy.start()
    for copy in outs:
        copy.wait()


def feed_far_kernel(
    ids_ref, gate_mat_ref, up_mat_ref, down_ref, act_in, gate_in, up_in, *rest, per_shard
):
    hops = 4
    normed_refs, cot_refs = rest[:hops], rest[hops : 2 * hops]
    tiles_out, act_out, gate_out, up_out = rest[2 * hops : 2 * hops + 4]
    gate_mat, up_mat, down_mat, tokens, cots, turned, act, grad_gate, grad_up, tiles = rest[
        2 * hops + 4 : 2 * hops + 14
    ]
    mat_sems, token_sems, cot_sems, unit_sems, out_sems, tile_sems = rest[2 * hops + 14 :]
    width, own = gate_mat.shape
    count = tokens.shape[0] // hops
    places, height, tile = tiles.shape
    rows = height // 3
    mats = [
        pltpu.make_async_copy(source, target, mat_sems.at[index])
        for index, (source, target) in enumerate(
            ((gate_mat_ref, gate_mat), (up_mat_ref, up_mat), (down_ref, down_mat))
        )
    ]
    token_copies = [
        pltpu.make_async_copy(ref, tokens.at[pl.ds(index * count, count), :], token_sems.at[index])
        for index, ref in enumerate(normed_refs)
    ]
    cot_copies = [
        pltpu.make_async_copy(ref, cots.at[pl.ds(index * count, count), :], cot_sems.at[index])
        for index, ref in enumerate(cot_refs)
    ]
    unit_copies = [
        pltpu.make_async_copy(source, target.at[pl.ds(0, 2 * count), :], unit_sems.at[slot])
        for slot, (source, target) in enumerate(
            ((act_in, act), (gate_in, grad_gate), (up_in, grad_up))
        )
    ]
    for copy in mats + token_copies[2:] + cot_copies[2:]:
        copy.start()
    for copy in token_copies[:2] + cot_copies[:2] + unit_copies:
        copy.start()
    for copy in token_copies[:2]:
        copy.wait()
    turned[:, : 2 * count] = tokens[: 2 * count, :].T
    for copy in mats + token_copies[2:] + cot_copies[2:]:
        copy.wait()

    late = pl.ds(2 * count, 2 * count)
    act[late, :], grad_gate[late, :], grad_up[late, :] = units(
        tokens[late, :], cots[late, :], gate_mat[...], up_mat[...], down_mat[...]
    )
    turned[:, 2 * count :] = tokens[late, :].T
    outs = [
        pltpu.make_async_copy(source.at[late, :], target, out_sems.at[index])
        for index, (source, target) in enumerate(
            ((act, act_out), (grad_gate, gate_out), (grad_up, up_out))
        )
    ]
    for copy in outs:
        copy.start()
    for copy in cot_copies[:2] + unit_copies:
        copy.wait()

    def tile_copy(spot, slot):
        low, high = ((0, 2 * rows), (2 * rows, 3 * rows))[slot]
        return pltpu.make_async_copy(
            tiles.at[spot, pl.ds(low, high - low), :],
            tiles_out.at[spot, pl.ds(low, high - low), :],
            tile_sems.at[slot, spot],
        )

    def row_block(index, carry):
        left = turned[pl.ds(pl.multiple_of(index * 2 * rows, 16), 2 * rows), :]
        spots = [
            lax.rem(2 * index + block + ids_ref[0], hops) * per_shard for block in range(2)
        ]
        for slot, ref in ((0, grad_gate), (1, grad_up)):
            grad = nn(left, ref[...])
            for block, spot in enumerate(spots):
                for part in range(per_shard):
                    tiles[spot + part, slot * rows : (slot + 1) * rows, :] = grad[
                        block * rows : (block + 1) * rows, part * tile : (part + 1) * tile
                    ].astype(BF16)
        for spot in spots:
            for part in range(per_shard):
                tile_copy(spot + part, 0).start()
        return carry

    lax.fori_loop(0, hops // 2, row_block, 0)
    band = own // places
    turned[:own, :] = act[...].T

    def down_block(index, carry):
        left = turned[pl.ds(pl.multiple_of(index * 4 * band, 16), 4 * band), :]
        grad = nn(left, cots[...])
        for part in range(4):
            for split in range(width // tile):
                start = 2 * rows + split * band
                tiles[4 * index + part, start : start + band, :] = grad[
                    part * band : (part + 1) * band, split * tile : (split + 1) * tile
                ].astype(BF16)
            tile_copy(4 * index + part, 1).start()
        return carry

    lax.fori_loop(0, places // 4, down_block, 0)
    for copy in outs:
        copy.wait()
    for spot in range(places):
        for slot in range(2):
            tile_copy(spot, slot).wait()


def normed_back_kernel(gate_ref, up_ref, gate_mat_ref, up_mat_ref, *outs):
    count = outs[0].shape[0]
    for index, out in enumerate(outs):
        span = slice(index * count, (index + 1) * count)
        out[...] = (
            nt(gate_ref[span, :], gate_mat_ref[...]) + nt(up_ref[span, :], up_mat_ref[...])
        ).astype(BF16)


def widen_kernel(
    ids_ref,
    gate_up_ref,
    down_in_ref,
    mixed_ref,
    gate_ref,
    up_ref,
    down_ref,
    query_ref,
    out_ref,
    stack,
    *,
    rows,
):
    step = pl.program_id(0)
    several, _, tile = gate_up_ref.shape
    band = down_ref.shape[0] // several
    share = mixed_ref.shape[1]
    for part in range(several):
        span = slice(part * tile, (part + 1) * tile)
        gate_ref[:, span] = gate_up_ref[part, :rows, :].astype(F32)
        up_ref[:, span] = gate_up_ref[part, rows:, :].astype(F32)
        for split in range(down_ref.shape[1] // tile):
            down_ref[part * band : (part + 1) * band, split * tile : (split + 1) * tile] = (
                down_in_ref[part, split * band : (split + 1) * band, :].astype(F32)
            )
        start = pl.multiple_of((step * several + part) * share, 8)
        stack[pl.ds(start, share), :] = mixed_ref[part].astype(F32)

    @pl.when(step == pl.num_programs(0) - 1)
    def _():
        cuts = query_ref.shape[1] // tile
        for cut in range(cuts):
            span = slice(cut * tile, (cut + 1) * tile)
            query_ref[:, span] = stack[cut * rows : (cut + 1) * rows, :]
            out_ref[:, span] = stack[(cuts + cut) * rows : (cuts + cut + 1) * rows, :]


def on_device(
    inputs,
    gain_attn,
    w_query,
    w_key,
    w_value,
    w_out,
    gain_mlp,
    w_gate,
    w_up,
    w_down,
    cotangent,
    *,
    n_ctx,
    n_shard,
):
    x = inputs[0]
    cot = cotangent[0]
    count, width = x.shape
    rows, qw = w_query.shape
    kvw = w_key.shape[1]
    ff_own = w_down.shape[0]
    ff = w_gate.shape[1]
    groups = kvw // HEAD
    per = qw // kvw
    blocks = n_ctx
    per_shard = n_ctx // n_shard
    tile = ff_own // per_shard
    assert count == BLOCK and n_shard == 4 and n_ctx % 2 == 0 and ff_own * n_shard == ff
    aligned = tile % LANES == 0
    order = ring_order(n_ctx)
    places = [order.index(index) for index in range(n_ctx)]
    shard = lax.axis_index("shard")
    ctx = lax.axis_index("ctx")

    def after(value, done):
        return lax.optimization_barrier((value, done))[0]

    def hop(value, distance):
        pairs = [(index, index ^ distance) for index in range(n_shard)]
        return lax.ppermute(value, "shard", pairs)

    def ctx_hop(value, distance):
        pairs = [(index, index ^ distance) for index in range(n_ctx)]
        return lax.ppermute(value, "ctx", pairs)

    def gather(value, done):
        far = hop(after(value, done), 2)
        return [value, hop(value, 1), far, hop(far, 1)]

    def halves(parts):
        third = hop(parts[3], 1)
        first = hop(parts[1], 1)
        across = (parts[2].astype(F32) + third.astype(F32)).astype(BF16)
        return parts[0], first, across

    def reduce(parts):
        own, first, across = halves(parts)
        return [own, first, hop(across, 2)]

    def add(parts):
        return sum(part.astype(F32) for part in parts)

    def scatter(value):
        return lax.psum_scatter(
            value, "ctx", scatter_dimension=0, axis_index_groups=[order], tiled=False
        )

    def collect(value):
        return lax.all_gather(value, "ctx", axis=0, axis_index_groups=[order], tiled=True)

    lane = jnp.arange(LANES, dtype=jnp.int32)
    frequency = jnp.exp((lane % (HEAD // 2)).astype(F32) * (-2.0 * math.log(10000.0) / HEAD))
    positions = (ctx * count + jnp.arange(count, dtype=jnp.int32)).astype(F32)
    angles = positions[:, None] * frequency[None, :]
    cosine = jnp.cos(angles)
    sine = jnp.where(lane % HEAD < HEAD // 2, -1.0, 1.0)[None, :] * jnp.sin(angles)

    gains = jnp.concatenate([gain_attn, gain_mlp])
    gain_rows = jnp.zeros((16, 2 * kvw), BF16).at[0, : 2 * rows].set(gains)
    kv_own = jnp.concatenate([jnp.concatenate([w_key, w_value], axis=1), gain_rows], axis=0)
    far = hop(kv_own, 2)
    kv_weights = [kv_own, hop(kv_own, 1), far, hop(far, 1)]
    ids = jnp.stack([shard, ctx]).astype(jnp.int32)
    sizes = (rows,) * n_shard


    half = rows // 2
    lanes = 4 * ff_own // n_ctx
    spot = ring_place(ctx, n_ctx)

    def columns(peer):
        start = peer * ff_own
        return jnp.concatenate(
            [
                lax.dynamic_slice_in_dim(w_gate, start, ff_own, 1),
                lax.dynamic_slice_in_dim(w_up, start, ff_own, 1),
            ],
            axis=1,
        )

    def far_columns(peer):
        column = peer * ff_own + lax.rem(spot // 2 * lanes, ff_own)
        cuts = [
            lax.dynamic_slice(mat, (spot % 2 * half, column), (half, lanes))
            for mat in (w_gate, w_up)
        ]
        return jnp.where(spot // 2 * lanes < ff_own, cuts[0], cuts[1])

    near_columns = columns(shard ^ 1)
    far_cut = jnp.concatenate([far_columns(shard ^ distance) for distance in (2, 3)], axis=0)
    query_own = jnp.concatenate([w_query, far_cut], axis=1)
    cosine, sine, ids, near_columns, query_own = lax.optimization_barrier(
        (cosine, sine, ids, near_columns, query_own)
    )
    query_weights = gather(query_own, far)
    out_far = hop(after(w_out, query_weights[2]), 2)
    fetch_sems = pltpu.SemaphoreType.DMA((n_shard,))
    hidden, kv, gain_one, gain_two = call_once(
        functools.partial(keys_kernel, sizes=sizes, kvw=kvw),
        [((count, width), BF16), ((count, 2 * kvw), BF16), ((1, width), F32), ((1, width), F32)],
        [x, cosine, sine],
        held=[ids],
        moved=kv_weights,
        scratch=[
            pltpu.VMEM((width, 2 * kvw), BF16),
            pltpu.VMEM((n_shard, 16, 2 * kvw), BF16),
            fetch_sems,
            fetch_sems,
        ],
        flops=4 * count * width * kvw,
        limit=ALL_VMEM,
        name="keys",
    )
    all_kv = collect(kv)

    (queries,) = call_once(
        functools.partial(queries_kernel, sizes=sizes),
        [((count, qw), BF16)],
        [hidden, cosine, sine],
        held=[ids],
        moved=query_weights,
        scratch=[pltpu.VMEM((width, qw), BF16), fetch_sems],
        flops=2 * count * width * qw,
        name="queries",
    )
    out_weights = [w_out, hop(w_out, 1), out_far, hop(after(out_far, queries), 1)]
    far_tile = jnp.concatenate(
        [query_weights[2][:half, qw:], query_weights[3][half:, qw:]], axis=0
    )
    far_rows = collect(after(far_tile, kv)[None])
    near_part = hop(near_columns, 1)
    cot_near = hop(cot, 1)
    cot_far = hop(after(cot, (out_weights[2], queries)), 2)

    shared = dict(sizes=sizes, column=0, groups=groups, per=per, blocks=blocks)
    fixed = lambda *shape: pl.BlockSpec(shape, lambda step, table: (0,) * len(shape))
    kv_spec = pl.BlockSpec(
        (count, 2 * kvw), lambda step, table: (ring_place(jnp.minimum(step, table[1]), blocks), 0)
    )
    once = lambda *shape: block(shape)
    weight_specs = [HBM_SPEC] * len(sizes)
    span = per * count
    out_tall, attended, log_total, mid, normed, q_cols = pl.pallas_call(
        functools.partial(attend_kernel, **shared),
        out_shape=(
            jax.ShapeDtypeStruct((qw, count), F32),
            jax.ShapeDtypeStruct((count, qw), BF16),
            jax.ShapeDtypeStruct((8, span), F32),
            jax.ShapeDtypeStruct((count, width), F32),
            jax.ShapeDtypeStruct((count, width), BF16),
            jax.ShapeDtypeStruct((groups, HEAD, span), BF16),
        ),
        grid_spec=pltpu.PrefetchScalarGridSpec(
            num_scalar_prefetch=1,
            grid=(blocks,),
            in_specs=[once(count, qw), kv_spec, once(count, width), once(1, width)]
            + weight_specs,
            out_specs=[
                fixed(qw, count),
                fixed(count, qw),
                fixed(8, span),
                fixed(count, width),
                fixed(count, width),
                fixed(groups, HEAD, span),
            ],
            scratch_shapes=[
                pltpu.VMEM((groups, HEAD, span), F32),
                pltpu.VMEM((8, span), F32),
                pltpu.VMEM((8, span), F32),
                pltpu.VMEM((qw, width), BF16),
                pltpu.VMEM((2, count, span), F32),
                pltpu.VMEM((qw, count), F32),
                pltpu.SemaphoreType.DMA((len(sizes),)),
            ],
        ),
        compiler_params=params(),
        cost_estimate=cost(
            4 * count * count * blocks * qw, 12e6, count * count * blocks * groups * per
        ),
        name="attend",
    )(ids, queries, all_kv, x, gain_two, *out_weights)

    normed_far = hop(normed, 2)
    normed_near = hop(normed, 1)
    cot_far = after(cot_far, normed)
    far_rows = after(far_rows, normed)
    all_count = n_shard * count
    if aligned:
        two = ((2 * count, ff_own), BF16)
        mats = [((width, ff_own), BF16)] * 2
        pair = (2 * count, width)
        gate_mat, up_mat, *near_units, back = pl.pallas_call(
            functools.partial(feed_near_kernel, half=half, lanes=lanes),
            out_shape=tuple(
                jax.ShapeDtypeStruct(*out) for out in [*mats, two, two, two, (pair, BF16)]
            ),
            in_specs=[SMEM_SPEC] + [HBM_SPEC] * 9,
            out_specs=(HBM_SPEC,) * 6,
            scratch_shapes=[
                pltpu.VMEM((width, ff_own), BF16),
                pltpu.VMEM((width, ff_own), BF16),
                pltpu.VMEM((ff_own, width), BF16),
                pltpu.VMEM(pair, BF16),
                pltpu.VMEM(pair, BF16),
                pltpu.VMEM(*two),
                pltpu.VMEM(*two),
                pltpu.VMEM(*two),
                pltpu.VMEM(pair, BF16),
                pltpu.SemaphoreType.DMA((4 + 2 * n_ctx,)),
                pltpu.SemaphoreType.DMA((3, 2)),
                pltpu.SemaphoreType.DMA((6,)),
            ],
            compiler_params=params(),
            cost_estimate=cost(10 * 2 * count * width * ff_own, 12e6),
            name="feed_near",
        )(
            ids,
            w_gate,
            w_up,
            near_part,
            far_rows,
            w_down,
            normed,
            normed_near,
            cot,
            cot_near,
        )
        normed_far, cot_far = lax.optimization_barrier((normed_far, cot_far, back))[:2]
        normed_pieces = [normed, normed_near, normed_far, hop(normed_far, 1)]
        cot_pieces = [cot, cot_near, cot_far, hop(cot_far, 1)]
        late = ((2 * count, ff_own), BF16)
        feed_tiles, *far_units = pl.pallas_call(
            functools.partial(feed_far_kernel, per_shard=per_shard),
            out_shape=tuple(
                jax.ShapeDtypeStruct(*out)
                for out in [((n_ctx, 3 * rows, tile), BF16), late, late, late]
            ),
            in_specs=[SMEM_SPEC] + [HBM_SPEC] * (6 + 2 * n_shard),
            out_specs=(HBM_SPEC,) * 4,
            scratch_shapes=[
                pltpu.VMEM((width, ff_own), BF16),
                pltpu.VMEM((width, ff_own), BF16),
                pltpu.VMEM((ff_own, width), BF16),
                pltpu.VMEM((all_count, width), BF16),
                pltpu.VMEM((all_count, width), BF16),
                pltpu.VMEM((width, all_count), BF16),
                pltpu.VMEM((all_count, ff_own), BF16),
                pltpu.VMEM((all_count, ff_own), BF16),
                pltpu.VMEM((all_count, ff_own), BF16),
                pltpu.VMEM((n_ctx, 3 * rows, tile), BF16),
                pltpu.SemaphoreType.DMA((3,)),
                pltpu.SemaphoreType.DMA((n_shard,)),
                pltpu.SemaphoreType.DMA((n_shard,)),
                pltpu.SemaphoreType.DMA((3,)),
                pltpu.SemaphoreType.DMA((3,)),
                pltpu.SemaphoreType.DMA((2, n_ctx)),
            ],
            compiler_params=params(),
            cost_estimate=cost(9 * all_count * width * ff_own, 25e6),
            name="feed_far",
        )(
            ids, gate_mat, up_mat, w_down, *near_units, *normed_pieces, *cot_pieces
        )
        to_own, to_near = back[:count], back[count:]
        act_parts = [near_units[0], far_units[0]]
        grad_gate_far, grad_up_far = far_units[1:]
    else:
        normed_pieces = [normed, normed_near, normed_far, hop(normed_far, 1)]
        cot_pieces = [cot, cot_near, cot_far, hop(cot_far, 1)]
        tiles_of = far_rows.reshape(n_ctx // 2, 2, 2, half, lanes)
        tiles_of = tiles_of.transpose(2, 1, 3, 0, 4).reshape(2, rows, 2 * ff_own)
        gate_mat = jnp.zeros((width, ff_own), BF16)
        up_mat = jnp.zeros((width, ff_own), BF16)
        for part, start in zip(
            (columns(shard), near_part, tiles_of[0], tiles_of[1]),
            [(shard ^ k) * rows for k in range(n_shard)],
        ):
            gate_mat = lax.dynamic_update_slice_in_dim(gate_mat, part[:, :ff_own], start, 0)
            up_mat = lax.dynamic_update_slice_in_dim(up_mat, part[:, ff_own:], start, 0)
        all_cot = jnp.concatenate(cot_pieces, axis=0)
        all_normed = jnp.concatenate(normed_pieces, axis=0)
        gate = nn(all_normed, gate_mat)
        up = nn(all_normed, up_mat)
        grad_activated = nt(all_cot, w_down)
        sigmoid = jax.nn.sigmoid(gate)
        activated = (gate * sigmoid * up).astype(BF16)
        grad_gate = (grad_activated * up * (sigmoid * (1.0 + gate * (1.0 - sigmoid)))).astype(BF16)
        grad_up = (grad_activated * (gate * sigmoid)).astype(BF16)

        def tiles(grad):
            pieces = grad.astype(BF16).reshape(n_shard, rows, per_shard, tile)
            pieces = pieces.transpose(0, 2, 1, 3)
            return jnp.roll(pieces, shard, axis=0).reshape(n_ctx, rows, tile)

        down = tn(activated, all_cot).astype(BF16)
        down = down.reshape(n_ctx, ff_own // n_ctx, width // tile, tile).transpose(0, 2, 1, 3)
        feed_tiles = jnp.concatenate(
            [
                tiles(tn(all_normed, grad_gate)),
                tiles(tn(all_normed, grad_up)),
                down.reshape(n_ctx, rows, tile),
            ],
            axis=1,
        )
        grad_gate_far, grad_up_far = grad_gate[2 * count :], grad_up[2 * count :]
        back = nt(grad_gate[: 2 * count], gate_mat) + nt(grad_up[: 2 * count], up_mat)
        to_own, to_near = back[:count].astype(BF16), back[count:].astype(BF16)
        act_parts = [activated[: 2 * count], activated[2 * count :]]
    from_near = hop(to_near, 1)
    feed_sum = scatter(feed_tiles)
    down_sum = feed_sum[2 * rows :]
    pairs = []
    for index in range(n_ctx):
        for source in range(n_shard):
            target = (places[index] // per_shard - source) % n_shard
            pairs.append((index * n_shard + source, index * n_shard + target))
    gate_up_sum = lax.ppermute(feed_sum[: 2 * rows], ("ctx", "shard"), pairs)

    to_far, to_third = call_once(
        normed_back_kernel,
        [((count, width), BF16)] * 2,
        [grad_gate_far, grad_up_far, gate_mat, up_mat],
        flops=8 * count * width * ff_own,
        limit=ALL_VMEM,
        name="normed_back",
    )
    third = hop(to_third, 1)
    across = (to_far.astype(F32) + third.astype(F32)).astype(BF16)
    from_far = hop(across, 2)

    part_out = [after(nn(part, w_down).astype(BF16), from_far) for part in act_parts]
    part_out = [part[k * count : (k + 1) * count] for part in part_out for k in range(2)]
    output = (mid + add(reduce(part_out))).astype(BF16)[None]

    place_spec = pl.BlockSpec(
        (count, 2 * kvw), lambda step, table: (ring_place(step, blocks), 0)
    )
    grad_query, grad_kv, branch, grad_mid, gain_two_part = pl.pallas_call(
        functools.partial(attend_back_kernel, **shared),
        out_shape=(
            jax.ShapeDtypeStruct((count, qw), BF16),
            jax.ShapeDtypeStruct((blocks * count, 2 * kvw), BF16),
            jax.ShapeDtypeStruct((count, width), BF16),
            jax.ShapeDtypeStruct((count, width), F32),
            jax.ShapeDtypeStruct((1, width), F32),
        ),
        grid_spec=pltpu.PrefetchScalarGridSpec(
            num_scalar_prefetch=1,
            grid=(blocks,),
            in_specs=[
                kv_spec,
                once(groups, HEAD, span),
                once(qw, count),
                once(8, span),
                once(count, width),
                once(1, width),
                once(count, width),
                once(count, width),
                once(count, width),
                once(count, width),
                once(count, LANES),
                once(count, LANES),
            ]
            + weight_specs,
            out_specs=[
                fixed(count, qw),
                place_spec,
                fixed(count, width),
                fixed(count, width),
                fixed(1, width),
            ],
            scratch_shapes=[
                pltpu.VMEM((qw, width), BF16),
                pltpu.VMEM((groups, HEAD, span), BF16),
                pltpu.VMEM((8, span), F32),
                pltpu.VMEM((groups, HEAD, span), F32),
                pltpu.VMEM((2, 2, count, span), F32),
                pltpu.VMEM((qw, count), F32),
                pltpu.SemaphoreType.DMA((len(sizes),)),
            ],
        ),
        compiler_params=params(),
        cost_estimate=cost(
            10 * count * count * blocks * qw, 14e6, count * count * blocks * groups * per
        ),
        name="attend_back",
    )(
        ids,
        all_kv,
        q_cols,
        out_tall,
        log_total,
        mid,
        gain_two,
        cot,
        to_own,
        from_near,
        from_far,
        cosine,
        sine,
        *out_weights,
    )
    own_kv = scatter(after(grad_kv, down_sum).reshape(n_ctx, count, 2 * kvw))

    def stack(parts, breadth, name):
        height = sum(part.shape[0] * part.shape[1] for part in parts[::3]) // breadth
        if breadth % LANES:
            wide = jnp.concatenate(
                [add(parts[index : index + 3]) for index in range(0, len(parts), 3)], axis=1
            )
            wide = wide.astype(BF16).reshape(rows, -1, breadth)
            return wide.transpose(1, 0, 2).reshape(height, breadth)
        return call_once(stack_kernel, [((height, breadth), BF16)], parts, flops=1e6, name=name)[0]

    grad_blocks = call_once(
        weight_grads_kernel,
        [((rows, qw), BF16)] * n_shard + [((rows, width), BF16)] * n_shard,
        [hidden, grad_query, attended, branch],
        held=[ids],
        scratch=[pltpu.VMEM((width, qw), F32)],
        flops=4 * count * width * qw,
        limit=ALL_VMEM,
        name="weight_grads",
    )
    parts_query = reduce(grad_blocks[:n_shard])
    parts_out = reduce(grad_blocks[n_shard:])
    mixed = stack(parts_query + parts_out, tile, "stack_mixed")
    mixed_sum = scatter(after(mixed, own_kv).reshape(n_ctx, -1, tile))

    grad_kv_pre, *kv_blocks = call_once(
        functools.partial(kv_back_kernel, kvw=kvw),
        [((count, 2 * kvw), BF16)] + [((rows, 2 * kvw), BF16)] * n_shard,
        [own_kv, cosine, sine, hidden],
        held=[ids],
        scratch=[pltpu.VMEM((width, 2 * kvw), F32)],
        flops=4 * count * width * kvw,
        name="kv_back",
    )
    sum_kv = stack(reduce(kv_blocks), LANES, "stack_kv").reshape(n_ctx, -1, LANES)
    shares = jnp.concatenate([gate_up_sum, down_sum, jnp.zeros_like(mixed_sum)])
    shares = lax.dynamic_update_slice_in_dim(after(shares, sum_kv), mixed_sum, 3 * rows, 0)
    gathered = collect(shares[None])

    def exchange(value):
        return lax.all_to_all(value, "ctx", split_axis=0, concat_axis=0, tiled=True)

    own_sum = jnp.sum(exchange(sum_kv).astype(F32), axis=0, keepdims=True).astype(BF16)
    both = exchange(jnp.broadcast_to(own_sum, sum_kv.shape))
    both = both.reshape(2 * kvw // LANES, rows, LANES).transpose(1, 0, 2).reshape(rows, 2 * kvw)
    grad_w_key = both[:, :kvw].astype(F32)
    grad_w_value = both[:, kvw:].astype(F32)

    grad_x, gain_one_part = call_once(
        functools.partial(inputs_kernel, sizes=sizes),
        [((count, width), BF16), ((1, width), F32)],
        [grad_query, grad_kv_pre, x, gain_one, grad_mid],
        held=[ids],
        moved=[*query_weights, *kv_weights],
        scratch=[
            pltpu.VMEM((width, qw), BF16),
            pltpu.VMEM((width, 2 * kvw), BF16),
            fetch_sems,
            fetch_sems,
        ],
        flops=2 * count * width * (qw + 2 * kvw),
        name="grad_inputs",
    )

    gain_parts = jnp.concatenate([gain_one_part, gain_two_part], axis=0)
    for distance in [1 << bit for bit in range(n_shard.bit_length() - 1)]:
        gain_parts = gain_parts + hop(gain_parts, distance)
    for distance in [1 << bit for bit in range(n_ctx.bit_length() - 1)]:
        gain_parts = gain_parts + ctx_hop(gain_parts, distance)
    own_gains = lax.dynamic_slice_in_dim(gain_parts, shard * rows, rows, 1)

    if aligned:
        share = mixed_sum.shape[0]
        rolled = lambda step, where: (lax.rem(step + where[0], n_shard), 0, 0)
        band = ff_own // n_ctx
        grad_w_gate, grad_w_up, grad_w_down, grad_w_query, grad_w_out = pl.pallas_call(
            functools.partial(widen_kernel, rows=rows),
            out_shape=(
                jax.ShapeDtypeStruct((rows, ff), F32),
                jax.ShapeDtypeStruct((rows, ff), F32),
                jax.ShapeDtypeStruct((ff_own, width), F32),
                jax.ShapeDtypeStruct((rows, qw), F32),
                jax.ShapeDtypeStruct((rows, width), F32),
            ),
            grid_spec=pltpu.PrefetchScalarGridSpec(
                num_scalar_prefetch=1,
                grid=(n_shard,),
                in_specs=[
                    pl.BlockSpec((per_shard, 2 * rows, tile), rolled),
                    pl.BlockSpec((per_shard, rows, tile), lambda step, where: (step, 2, 0)),
                    pl.BlockSpec(
                        (per_shard, share, tile),
                        lambda step, where: (step, 3 * rows // share, 0),
                    ),
                ],
                out_specs=[
                    pl.BlockSpec((rows, ff_own), lambda step, where: (0, step)),
                    pl.BlockSpec((rows, ff_own), lambda step, where: (0, step)),
                    pl.BlockSpec((per_shard * band, width), lambda step, where: (step, 0)),
                    pl.BlockSpec((rows, qw), lambda step, where: (0, 0)),
                    pl.BlockSpec((rows, width), lambda step, where: (0, 0)),
                ],
                scratch_shapes=[pltpu.VMEM((n_ctx * share, tile), F32)],
            ),
            compiler_params=params(),
            cost_estimate=cost(1e6, 20e6),
            name="widen",
        )(ids, gathered, gathered, gathered)
    else:

        def untile(part):
            back = jnp.roll(part.reshape(n_shard, per_shard, rows, tile), -shard, axis=0)
            back = back.reshape(n_ctx, rows, tile).transpose(1, 0, 2)
            return back.reshape(rows, ff).astype(F32)

        grad_w_gate = untile(gathered[:, :rows])
        grad_w_up = untile(gathered[:, rows : 2 * rows])
        down = gathered[:, 2 * rows : 3 * rows].reshape(n_ctx, width // tile, -1, tile)
        grad_w_down = down.transpose(0, 2, 1, 3).reshape(ff_own, width).astype(F32)
        wide = gathered[:, 3 * rows :].reshape(2 * qw // tile, rows, tile).transpose(1, 0, 2)
        wide = wide.reshape(rows, 2 * qw).astype(F32)
        grad_w_query, grad_w_out = wide[:, :qw], wide[:, qw:]

    return (
        output,
        grad_x[None],
        own_gains[0],
        grad_w_query,
        grad_w_key,
        grad_w_value,
        grad_w_out,
        own_gains[1],
        grad_w_gate,
        grad_w_up,
        grad_w_down,
    )


def solution(mesh):
    tokens = P("shard", "ctx", None)
    split = P("shard", None)
    gain = P("shard")
    placed = (tokens, gain, split, split, split, split, gain, split, split, split, tokens)
    return jax.shard_map(
        functools.partial(on_device, n_ctx=mesh.shape["ctx"], n_shard=mesh.shape["shard"]),
        mesh=mesh,
        in_specs=placed,
        out_specs=(tokens, tokens, gain, split, split, split, split, gain, split, split, split),
        check_vma=False,
    )
```

```python
import functools
import math

import jax
import jax.numpy as jnp
from jax import lax
from jax.experimental import pallas as pl
from jax.experimental.pallas import tpu as pltpu
from jax.sharding import PartitionSpec as P

HEAD = 64
BLOCK = 256
EPSILON = 1e-05
LANES = 128
F32 = jnp.float32
BF16 = jnp.bfloat16
SCORE_SCALE = math.log2(math.e) * 0.125
NEGATIVE = -1e30
ALL_VMEM = 60 * 1024 * 1024
PART_VMEM = 32 * 1024 * 1024


def nn(left, right):
    return lax.dot_general(left, right, (((1,), (0,)), ((), ())), preferred_element_type=F32)


def nt(left, right):
    return lax.dot_general(left, right, (((1,), (1,)), ((), ())), preferred_element_type=F32)


def tn(left, right):
    return lax.dot_general(left, right, (((0,), (0,)), ((), ())), preferred_element_type=F32)


def ring_order(count):
    return list(range(0, count, 2)) + list(range(count - 1, 0, -2))


def ring_place(index, count):
    return jnp.where(index % 2 == 0, index // 2, count - 1 - index // 2)


def params(limit=ALL_VMEM):
    return pltpu.CompilerParams(vmem_limit_bytes=limit)


def cost(flops, moved, exps=0):
    return pl.CostEstimate(flops=int(flops), bytes_accessed=int(moved), transcendentals=int(exps))


HBM_SPEC = pl.BlockSpec(memory_space=pltpu.HBM)
SMEM_SPEC = pl.BlockSpec(memory_space=pltpu.SMEM)


def block(shape):
    return pl.BlockSpec(shape, lambda *_: (0,) * len(shape), pipeline_mode=pl.Buffered(1))


def call_once(
    kernel, outs, ins, held=(), moved=(), scratch=(), flops=0, limit=PART_VMEM, name=None
):
    return pl.pallas_call(
        kernel,
        out_shape=tuple(jax.ShapeDtypeStruct(shape, dtype) for shape, dtype in outs),
        grid=(1,),
        in_specs=[SMEM_SPEC] * len(held)
        + [block(array.shape) for array in ins]
        + [HBM_SPEC] * len(moved),
        out_specs=tuple(pl.BlockSpec(shape, lambda *_: (0,) * len(shape)) for shape, _ in outs),
        scratch_shapes=list(scratch),
        compiler_params=params(limit),
        cost_estimate=cost(flops, sum(2 * math.prod(shape) for shape, _ in outs) + 4e6),
        name=name,
    )(*held, *ins, *moved)


def swap_halves(tile):
    lane = lax.broadcasted_iota(jnp.int32, tile.shape, 1)
    ahead = pltpu.roll(tile, LANES - HEAD // 2, 1)
    behind = pltpu.roll(tile, HEAD // 2, 1)
    return jnp.where(lane % HEAD < HEAD // 2, ahead, behind)


def row_start(ids_ref, hop, rows):
    return pl.multiple_of((ids_ref[0] ^ hop) * rows, 16)


def fetches(ids_ref, pieces, whole, sems, sizes, column=0):
    copies = []
    for index, (piece, size) in enumerate(zip(pieces, sizes)):
        start = row_start(ids_ref, index, size)
        copies.append(
            pltpu.make_async_copy(
                piece.at[pl.ds(0, size), pl.ds(column, whole.shape[1])],
                whole.at[pl.ds(start, size), :],
                sems.at[index],
            )
        )
    return copies


def keys_kernel(ids_ref, x_ref, cos_ref, sin_ref, *rest, sizes, kvw):
    pieces = rest[: len(sizes)]
    hidden_ref, kv_ref, one_ref, two_ref, whole, bands, sems, band_sems = rest[len(sizes) :]
    copies = fetches(ids_ref, pieces, whole, sems, sizes)
    rows = sizes[0]
    for index, piece in enumerate(pieces):
        band = pltpu.make_async_copy(
            piece.at[pl.ds(rows, 16), :], bands.at[index], band_sems.at[index]
        )
        band.start()
        copies[index].start()
    x = x_ref[...].astype(F32)
    scale = lax.rsqrt(jnp.mean(x * x, axis=-1, keepdims=True) + EPSILON)
    width = x.shape[1]
    ones = jnp.zeros((8, width), F32)
    twos = jnp.zeros((8, width), F32)
    for index, piece in enumerate(pieces):
        pltpu.make_async_copy(
            piece.at[pl.ds(rows, 16), :], bands.at[index], band_sems.at[index]
        ).wait()
        band = bands[index].astype(F32)[:8, :]
        blank = jnp.zeros((8, width - rows), F32)
        first = jnp.concatenate([band[:, :rows], blank], axis=1)
        second = jnp.concatenate([band[:, rows : 2 * rows], blank], axis=1)
        ones = ones + pltpu.roll(first, (ids_ref[0] ^ index) * rows, 1)
        twos = twos + pltpu.roll(second, (ids_ref[0] ^ index) * rows, 1)
    one_ref[...] = ones[:1, :]
    two_ref[...] = twos[:1, :]
    hidden = (x * scale * ones[:1, :]).astype(BF16)
    hidden_ref[...] = hidden
    for copy in copies:
        copy.wait()
    pre = nn(hidden, whole[...])
    for start in range(0, kvw, LANES):
        tile = pre[:, start : start + LANES]
        turned = tile * cos_ref[...] + swap_halves(tile) * sin_ref[...]
        kv_ref[:, start : start + LANES] = turned.astype(BF16)
    kv_ref[:, kvw:] = pre[:, kvw:].astype(BF16)


def queries_kernel(ids_ref, hidden_ref, cos_ref, sin_ref, *rest, sizes):
    pieces = rest[: len(sizes)]
    query_ref, whole, sems = rest[len(sizes) :]
    copies = fetches(ids_ref, pieces, whole, sems, sizes)
    for copy in copies:
        copy.start()
    for copy in copies:
        copy.wait()
    pre = nn(hidden_ref[...], whole[...])
    for start in range(0, pre.shape[1], LANES):
        tile = pre[:, start : start + LANES]
        turned = tile * cos_ref[...] + swap_halves(tile) * sin_ref[...]
        query_ref[:, start : start + LANES] = turned.astype(BF16)


def attend_kernel(
    table_ref,
    q_ref,
    kv_ref,
    x_ref,
    gain_ref,
    *rest,
    sizes,
    column,
    groups,
    per,
    blocks,
):
    pieces = rest[:-13]
    (
        out_ref,
        attended_ref,
        log_ref,
        mid_ref,
        normed_ref,
        cols_ref,
        acc,
        top,
        total,
        whole,
        scores,
        tall,
        sems,
    ) = rest[-13:]
    step = pl.program_id(0)
    last = table_ref[1]
    count = q_ref.shape[0]
    kvw = groups * HEAD

    @pl.when(step == 0)
    def _():
        for copy in fetches(table_ref, pieces, whole, sems, sizes, column):
            copy.start()
        turned = q_ref[...].T
        for group in range(groups):
            for member in range(per):
                head = group * per + member
                cols_ref[group, :, member * count : (member + 1) * count] = turned[
                    head * HEAD : (head + 1) * HEAD, :
                ]
        acc[...] = jnp.zeros_like(acc)
        total[...] = jnp.zeros_like(total)
        top[...] = jnp.full_like(top, NEGATIVE)

    @pl.when(step <= last)
    def _():
        def score(group):
            key = kv_ref[:, group * HEAD : (group + 1) * HEAD]
            scores[group % 2] = nn(key, cols_ref[group])

        score(0)
        for group in range(groups):
            if group + 1 < groups:
                score(group + 1)
            value = kv_ref[:, kvw + group * HEAD : kvw + (group + 1) * HEAD]
            raw = scores[group % 2]
            old = top[group : group + 1, :]
            new = jnp.maximum(old, jnp.max(raw, axis=0, keepdims=True))
            shrink = jnp.exp2((old - new) * SCORE_SCALE)
            probs = jnp.exp2((raw - new) * SCORE_SCALE)
            top[group : group + 1, :] = new
            total[group : group + 1, :] = total[group : group + 1, :] * shrink + jnp.sum(
                probs, axis=0, keepdims=True
            )
            acc[group] = acc[group] * shrink + tn(value, probs.astype(BF16))

    @pl.when(step == blocks - 1)
    def _():
        for group in range(groups):
            sums = total[group : group + 1, :]
            log_ref[group : group + 1, :] = top[
                group : group + 1, :
            ] * SCORE_SCALE + jnp.log2(sums)
            rowed = acc[group] / sums
            for member in range(per):
                head = group * per + member
                tall[head * HEAD : (head + 1) * HEAD, :] = rowed[
                    :, member * count : (member + 1) * count
                ]
        out_ref[...] = tall[...]
        attended = tall[...].astype(BF16).T
        attended_ref[...] = attended
        for copy in fetches(table_ref, pieces, whole, sems, sizes, column):
            copy.wait()
        mid = x_ref[...].astype(F32) + nn(attended, whole[...])
        mid_ref[...] = mid
        scale = lax.rsqrt(jnp.mean(mid * mid, axis=-1, keepdims=True) + EPSILON)
        normed_ref[...] = (mid * scale * gain_ref[...]).astype(BF16)


def attend_back_kernel(
    table_ref,
    kv_ref,
    cols_ref,
    out_ref,
    log_ref,
    mid_ref,
    gain_ref,
    cot_ref,
    gn_own_ref,
    gn_near_ref,
    gn_far_ref,
    cos_ref,
    sin_ref,
    *rest,
    sizes,
    column,
    groups,
    per,
    blocks,
):
    pieces = rest[: len(sizes)]
    (
        gq_ref,
        gkv_ref,
        branch_ref,
        gmid_ref,
        ggain_ref,
        whole,
        d_cols,
        delta,
        acc,
        probs_all,
        tall,
        sems,
    ) = rest[len(sizes) :]
    step = pl.program_id(0)
    last = table_ref[1]
    count = kv_ref.shape[0]
    kvw = groups * HEAD

    @pl.when(step == 0)
    def _():
        copies = fetches(table_ref, pieces, whole, sems, sizes, column)
        for copy in copies:
            copy.start()
        mid = mid_ref[...]
        incoming = (
            gn_own_ref[...].astype(F32) + gn_near_ref[...].astype(F32)
        ) + gn_far_ref[...].astype(F32)
        gain = gain_ref[...]
        scale = lax.rsqrt(jnp.mean(mid * mid, axis=-1, keepdims=True) + EPSILON)
        weighted = incoming * gain
        inner = jnp.mean(weighted * mid, axis=-1, keepdims=True)
        ggain_ref[...] = jnp.sum(incoming * mid * scale, axis=0, keepdims=True)
        grad_mid = (
            cot_ref[...].astype(F32) + scale * weighted - mid * (scale * scale * scale * inner)
        )
        gmid_ref[...] = grad_mid
        branch = grad_mid.astype(BF16)
        branch_ref[...] = branch
        for copy in copies:
            copy.wait()
        grads = nt(branch, whole[...]).astype(BF16)
        turned = grads.T
        tall[...] = turned.astype(F32) * out_ref[...]
        for group in range(groups):
            for member in range(per):
                head = group * per + member
                span = slice(head * HEAD, (head + 1) * HEAD)
                cols = slice(member * count, (member + 1) * count)
                d_cols[group, :, cols] = turned[span, :]
                delta[group : group + 1, cols] = jnp.sum(tall[span, :], axis=0, keepdims=True)
        acc[...] = jnp.zeros_like(acc)

    @pl.when(step > last)
    def _():
        gkv_ref[...] = jnp.zeros_like(gkv_ref)

    @pl.when(step <= last)
    def _():
        def spans(group):
            return (
                slice(group * HEAD, (group + 1) * HEAD),
                slice(kvw + group * HEAD, kvw + (group + 1) * HEAD),
            )

        def score(group):
            key_span, value_span = spans(group)
            probs_all[group % 2, 0] = nn(kv_ref[:, key_span], cols_ref[group])
            probs_all[group % 2, 1] = nn(kv_ref[:, value_span], d_cols[group])

        score(0)
        for group in range(groups):
            if group + 1 < groups:
                score(group + 1)
            key_span, value_span = spans(group)
            probs = jnp.exp2(
                probs_all[group % 2, 0] * SCORE_SCALE - log_ref[group : group + 1, :]
            )
            grad_scores = (
                probs * (probs_all[group % 2, 1] - delta[group : group + 1, :])
            ).astype(BF16)
            gkv_ref[:, value_span] = nt(probs.astype(BF16), d_cols[group]).astype(BF16)
            gkv_ref[:, key_span] = (nt(grad_scores, cols_ref[group]) * 0.125).astype(BF16)
            acc[group] = acc[group] + tn(kv_ref[:, key_span], grad_scores)

    @pl.when(step == blocks - 1)
    def _():
        for group in range(groups):
            for member in range(per):
                head = group * per + member
                tall[head * HEAD : (head + 1) * HEAD, :] = (
                    acc[group, :, member * count : (member + 1) * count] * 0.125
                )
        for start in range(0, tall.shape[0], LANES):
            tile = tall[start : start + LANES, :].T
            turned = tile * cos_ref[...] - swap_halves(tile) * sin_ref[...]
            gq_ref[:, start : start + LANES] = turned.astype(BF16)


def columns_in_turn(left, right, full):
    breadth = full.shape[1] // 3

    def third(index, carry):
        span = pl.ds(pl.multiple_of(index * breadth, LANES), breadth)
        full[:, span] = tn(left[...], right[:, span])
        return carry

    lax.fori_loop(0, 3, third, 0)


def kv_back_kernel(ids_ref, grad_ref, cos_ref, sin_ref, hidden_ref, out_ref, *rest, kvw):
    outs, full = rest[:-1], rest[-1]
    for start in range(0, kvw, LANES):
        tile = grad_ref[:, start : start + LANES].astype(F32)
        turned = tile * cos_ref[...] - swap_halves(tile) * sin_ref[...]
        out_ref[:, start : start + LANES] = turned.astype(BF16)
    out_ref[:, kvw:] = grad_ref[:, kvw:]
    columns_in_turn(hidden_ref, out_ref, full)
    for index, out in enumerate(outs):
        start = row_start(ids_ref, index, out.shape[0])
        out[...] = full[pl.ds(start, out.shape[0]), :].astype(BF16)


def stack_kernel(*refs):
    parts, out_ref = refs[:-1], refs[-1]
    tile = out_ref.shape[1]
    row = 0
    for index in range(0, len(parts), 3):
        first, second, third = parts[index : index + 3]
        rows, columns = first.shape
        for start in range(0, columns, tile):
            span = slice(start, start + tile)
            total = (
                first[:, span].astype(F32) + second[:, span].astype(F32)
            ) + third[:, span].astype(F32)
            out_ref[row : row + rows, :] = total.astype(BF16)
            row += rows


def inputs_kernel(ids_ref, gq_ref, gkv_ref, x_ref, gain_ref, gmid_ref, *rest, sizes):
    hops = len(sizes)
    grad_ref, ggain_ref, whole_q, whole_kv, arriving, q_sems, kv_sems = rest[2 * hops :]
    copies = fetches(ids_ref, rest[:hops], whole_q, q_sems, sizes)
    copies += fetches(ids_ref, rest[hops : 2 * hops], whole_kv, kv_sems, sizes)
    for copy in copies:
        copy.start()
    for copy in copies:
        copy.wait()
    breadth = arriving.shape[1] // 3

    def third(index, carry):
        span = pl.ds(pl.multiple_of(index * breadth, LANES), breadth)
        arriving[:, span] = nt(gq_ref[...], whole_q[span, :]) + nt(gkv_ref[...], whole_kv[span, :])
        return carry

    lax.fori_loop(0, 3, third, 0)
    incoming = arriving[...]
    x = x_ref[...].astype(F32)
    scale = lax.rsqrt(jnp.mean(x * x, axis=-1, keepdims=True) + EPSILON)
    weighted = incoming * gain_ref[...]
    inner = jnp.mean(weighted * x, axis=-1, keepdims=True)
    ggain_ref[...] = jnp.sum(incoming * x * scale, axis=0, keepdims=True)
    grad = gmid_ref[...] + scale * weighted - x * (scale * scale * scale * inner)
    grad_ref[...] = grad.astype(BF16)


def weight_grads_kernel(ids_ref, hidden_ref, query_ref, attended_ref, branch_ref, *rest):
    outs, full = rest[:-1], rest[-1]
    hops = len(outs) // 2
    for index, (left, right) in enumerate(((hidden_ref, query_ref), (attended_ref, branch_ref))):
        full[...] = tn(left[...], right[...])
        for hop, out in enumerate(outs[index * hops : (index + 1) * hops]):
            start = row_start(ids_ref, hop, out.shape[0])
            out[...] = full[pl.ds(start, out.shape[0]), :].astype(BF16)


def units(normed, cot, gate_mat, up_mat, down_mat):
    gate = nn(normed, gate_mat)
    up = nn(normed, up_mat)
    grad = nt(cot, down_mat)
    sigmoid = 1.0 / (1.0 + jnp.exp(-gate))
    silu = gate * sigmoid
    return (
        (silu * up).astype(BF16),
        (grad * up * (sigmoid * (1.0 + gate * (1.0 - sigmoid)))).astype(BF16),
        (grad * silu).astype(BF16),
    )


def feed_near_kernel(
    ids_ref, own_gate_ref, own_up_ref, near_ref, far_ref, down_ref, *rest, half, lanes
):
    normed_refs, cot_refs = rest[:2], rest[2:4]
    gate_mat_out, up_mat_out, act_out, gate_out, up_out, back_out = rest[4:10]
    gate_mat, up_mat, down_mat, tokens, cots, act, grad_gate, grad_up, back = rest[10:19]
    mat_sems, token_sems, out_sems = rest[19:]
    rows = near_ref.shape[0]
    own = gate_mat.shape[1]
    mats = []

    def place(source, row, column, height, breadth):
        target = gate_mat if column < own else up_mat
        mats.append(
            pltpu.make_async_copy(
                source,
                target.at[pl.ds(row, height), pl.ds(column % own, breadth)],
                mat_sems.at[len(mats)],
            )
        )

    mine = pl.ds(pl.multiple_of(ids_ref[0] * own, LANES), own)
    for index, ref in enumerate((own_gate_ref, own_up_ref)):
        place(ref.at[:, mine], row_start(ids_ref, 0, rows), index * own, rows, own)
        place(
            near_ref.at[:, pl.ds(index * own, own)],
            row_start(ids_ref, 1, rows),
            index * own,
            rows,
            own,
        )
    for spot in range(far_ref.shape[0]):
        for index in range(2):
            place(
                far_ref.at[spot, pl.ds(index * half, half), :],
                pl.multiple_of(row_start(ids_ref, 2 + index, rows) + (spot % 2) * half, 16),
                (spot // 2) * lanes,
                half,
                lanes,
            )
    loads = [
        pltpu.make_async_copy(ref, target.at[index], token_sems.at[slot, index])
        for slot, (refs, target) in enumerate(((normed_refs, tokens), (cot_refs, cots)))
        for index, ref in enumerate(refs)
    ]
    loads.append(pltpu.make_async_copy(down_ref, down_mat, token_sems.at[2, 0]))
    for copy in mats + loads:
        copy.start()
    for copy in mats:
        copy.wait()
    outs = [
        pltpu.make_async_copy(source, target, out_sems.at[index])
        for index, (source, target) in enumerate(
            (
                (gate_mat, gate_mat_out),
                (up_mat, up_mat_out),
                (act, act_out),
                (grad_gate, gate_out),
                (grad_up, up_out),
                (back, back_out),
            )
        )
    ]
    for copy in outs[:2]:
        copy.start()
    for copy in loads:
        copy.wait()

    def token_block(index, carry):
        act[index], grad_gate[index], grad_up[index] = units(
            tokens[index], cots[index], gate_mat[...], up_mat[...], down_mat[...]
        )
        back[index] = (
            nt(grad_gate[index], gate_mat[...]) + nt(grad_up[index], up_mat[...])
        ).astype(BF16)
        return carry

    lax.fori_loop(0, 2, token_block, 0)
    for copy in outs[2:]:
        copy.start()
    for copy in outs:
        copy.wait()


def feed_far_kernel(
    ids_ref, gate_mat_ref, up_mat_ref, down_ref, act_in, gate_in, up_in, *rest, per_shard
):
    hops = 4
    normed_refs, cot_refs = rest[:hops], rest[hops : 2 * hops]
    tiles_out, act_out, gate_out, up_out = rest[2 * hops : 2 * hops + 4]
    gate_mat, up_mat, down_mat, tokens, cots, turned, act, grad_gate, grad_up, tiles = rest[
        2 * hops + 4 : 2 * hops + 14
    ]
    mat_sems, token_sems, cot_sems, unit_sems, out_sems, tile_sems = rest[2 * hops + 14 :]
    width, own = gate_mat.shape
    count = tokens.shape[1]
    places, height, tile = tiles.shape
    rows = height // 3
    mats = [
        pltpu.make_async_copy(source, target, mat_sems.at[index])
        for index, (source, target) in enumerate(
            ((gate_mat_ref, gate_mat), (up_mat_ref, up_mat), (down_ref, down_mat))
        )
    ]
    token_copies = [
        pltpu.make_async_copy(ref, tokens.at[index], token_sems.at[index])
        for index, ref in enumerate(normed_refs)
    ]
    cot_copies = [
        pltpu.make_async_copy(ref, cots.at[pl.ds(index * count, count), :], cot_sems.at[index])
        for index, ref in enumerate(cot_refs)
    ]
    unit_copies = [
        pltpu.make_async_copy(source.at[index], target.at[pl.ds(index * count, count), :],
                              unit_sems.at[slot, index])
        for slot, (source, target) in enumerate(
            ((act_in, act), (gate_in, grad_gate), (up_in, grad_up))
        )
        for index in range(2)
    ]
    for copy in mats + token_copies[2:] + cot_copies[2:]:
        copy.start()
    for copy in token_copies[:2] + cot_copies[:2] + unit_copies:
        copy.start()
    for copy in token_copies[:2]:
        copy.wait()
    for index in range(2):
        turned[:, index * count : (index + 1) * count] = tokens[index].T
    for copy in mats + token_copies[2:] + cot_copies[2:]:
        copy.wait()

    def token_block(index, carry):
        span = pl.ds(pl.multiple_of(index * count, count), count)
        normed = tokens[index]
        act[span, :], grad_gate[span, :], grad_up[span, :] = units(
            normed, cots[span, :], gate_mat[...], up_mat[...], down_mat[...]
        )
        turned[:, span] = normed.T
        return carry

    lax.fori_loop(2, hops, token_block, 0)
    late = pl.ds(2 * count, 2 * count)
    outs = [
        pltpu.make_async_copy(source.at[late, :], target, out_sems.at[index])
        for index, (source, target) in enumerate(
            ((act, act_out), (grad_gate, gate_out), (grad_up, up_out))
        )
    ]
    for copy in outs:
        copy.start()
    for copy in cot_copies[:2] + unit_copies:
        copy.wait()

    def tile_copy(spot, slot):
        low, high = ((0, 2 * rows), (2 * rows, 3 * rows))[slot]
        return pltpu.make_async_copy(
            tiles.at[spot, pl.ds(low, high - low), :],
            tiles_out.at[spot, pl.ds(low, high - low), :],
            tile_sems.at[slot, spot],
        )

    def row_block(index, carry):
        left = turned[pl.ds(pl.multiple_of(index * rows, 16), rows), :]
        spot = lax.rem(index + ids_ref[0], hops) * per_shard
        for slot, ref in ((0, grad_gate), (1, grad_up)):
            grad = nn(left, ref[...])
            for part in range(per_shard):
                tiles[spot + part, slot * rows : (slot + 1) * rows, :] = grad[
                    :, part * tile : (part + 1) * tile
                ].astype(BF16)
        for part in range(per_shard):
            tile_copy(spot + part, 0).start()
        return carry

    lax.fori_loop(0, hops, row_block, 0)
    band = own // places
    turned[:own, :] = act[...].T

    def down_block(index, carry):
        left = turned[pl.ds(pl.multiple_of(index * 2 * band, 16), 2 * band), :]
        grad = nn(left, cots[...])
        for part in range(2):
            for split in range(width // tile):
                start = 2 * rows + split * band
                tiles[2 * index + part, start : start + band, :] = grad[
                    part * band : (part + 1) * band, split * tile : (split + 1) * tile
                ].astype(BF16)
            tile_copy(2 * index + part, 1).start()
        return carry

    lax.fori_loop(0, places // 2, down_block, 0)
    for copy in outs:
        copy.wait()
    for spot in range(places):
        for slot in range(2):
            tile_copy(spot, slot).wait()


def normed_back_kernel(gate_ref, up_ref, gate_mat_ref, up_mat_ref, *outs):
    count = outs[0].shape[0]
    for index, out in enumerate(outs):
        span = slice(index * count, (index + 1) * count)
        out[...] = (
            nt(gate_ref[span, :], gate_mat_ref[...]) + nt(up_ref[span, :], up_mat_ref[...])
        ).astype(BF16)


def widen_kernel(
    ids_ref,
    gate_up_ref,
    down_in_ref,
    mixed_ref,
    gate_ref,
    up_ref,
    down_ref,
    query_ref,
    out_ref,
    stack,
    *,
    rows,
):
    step = pl.program_id(0)
    several, _, tile = gate_up_ref.shape
    band = down_ref.shape[0] // several
    share = mixed_ref.shape[1]
    for part in range(several):
        span = slice(part * tile, (part + 1) * tile)
        gate_ref[:, span] = gate_up_ref[part, :rows, :].astype(F32)
        up_ref[:, span] = gate_up_ref[part, rows:, :].astype(F32)
        for split in range(down_ref.shape[1] // tile):
            down_ref[part * band : (part + 1) * band, split * tile : (split + 1) * tile] = (
                down_in_ref[part, split * band : (split + 1) * band, :].astype(F32)
            )
        start = pl.multiple_of((step * several + part) * share, 8)
        stack[pl.ds(start, share), :] = mixed_ref[part].astype(F32)

    @pl.when(step == pl.num_programs(0) - 1)
    def _():
        cuts = query_ref.shape[1] // tile
        for cut in range(cuts):
            span = slice(cut * tile, (cut + 1) * tile)
            query_ref[:, span] = stack[cut * rows : (cut + 1) * rows, :]
            out_ref[:, span] = stack[(cuts + cut) * rows : (cuts + cut + 1) * rows, :]


def on_device(
    inputs,
    gain_attn,
    w_query,
    w_key,
    w_value,
    w_out,
    gain_mlp,
    w_gate,
    w_up,
    w_down,
    cotangent,
    *,
    n_ctx,
    n_shard,
):
    x = inputs[0]
    cot = cotangent[0]
    count, width = x.shape
    rows, qw = w_query.shape
    kvw = w_key.shape[1]
    ff_own = w_down.shape[0]
    ff = w_gate.shape[1]
    groups = kvw // HEAD
    per = qw // kvw
    blocks = n_ctx
    per_shard = n_ctx // n_shard
    tile = ff_own // per_shard
    assert count == BLOCK and n_shard == 4 and n_ctx % 2 == 0 and ff_own * n_shard == ff
    aligned = tile % LANES == 0
    order = ring_order(n_ctx)
    places = [order.index(index) for index in range(n_ctx)]
    shard = lax.axis_index("shard")
    ctx = lax.axis_index("ctx")

    def after(value, done):
        return lax.optimization_barrier((value, done))[0]

    def hop(value, distance):
        pairs = [(index, index ^ distance) for index in range(n_shard)]
        return lax.ppermute(value, "shard", pairs)

    def ctx_hop(value, distance):
        pairs = [(index, index ^ distance) for index in range(n_ctx)]
        return lax.ppermute(value, "ctx", pairs)

    def gather(value, done):
        far = hop(after(value, done), 2)
        return [value, hop(value, 1), far, hop(far, 1)]

    def halves(parts):
        third = hop(parts[3], 1)
        first = hop(parts[1], 1)
        across = (parts[2].astype(F32) + third.astype(F32)).astype(BF16)
        return parts[0], first, across

    def reduce(parts):
        own, first, across = halves(parts)
        return [own, first, hop(across, 2)]

    def add(parts):
        return sum(part.astype(F32) for part in parts)

    def scatter(value):
        return lax.psum_scatter(
            value, "ctx", scatter_dimension=0, axis_index_groups=[order], tiled=False
        )

    def collect(value):
        return lax.all_gather(value, "ctx", axis=0, axis_index_groups=[order], tiled=True)

    lane = jnp.arange(LANES, dtype=jnp.int32)
    frequency = jnp.exp((lane % (HEAD // 2)).astype(F32) * (-2.0 * math.log(10000.0) / HEAD))
    positions = (ctx * count + jnp.arange(count, dtype=jnp.int32)).astype(F32)
    angles = positions[:, None] * frequency[None, :]
    cosine = jnp.cos(angles)
    sine = jnp.where(lane % HEAD < HEAD // 2, -1.0, 1.0)[None, :] * jnp.sin(angles)

    gains = jnp.concatenate([gain_attn, gain_mlp])
    gain_rows = jnp.zeros((16, 2 * kvw), BF16).at[0, : 2 * rows].set(gains)
    kv_own = jnp.concatenate([jnp.concatenate([w_key, w_value], axis=1), gain_rows], axis=0)
    far = hop(kv_own, 2)
    kv_weights = [kv_own, hop(kv_own, 1), far, hop(far, 1)]
    ids = jnp.stack([shard, ctx]).astype(jnp.int32)
    sizes = (rows,) * n_shard


    half = rows // 2
    lanes = 4 * ff_own // n_ctx
    spot = ring_place(ctx, n_ctx)

    def columns(peer):
        start = peer * ff_own
        return jnp.concatenate(
            [
                lax.dynamic_slice_in_dim(w_gate, start, ff_own, 1),
                lax.dynamic_slice_in_dim(w_up, start, ff_own, 1),
            ],
            axis=1,
        )

    def far_columns(peer):
        column = peer * ff_own + lax.rem(spot // 2 * lanes, ff_own)
        cuts = [
            lax.dynamic_slice(mat, (spot % 2 * half, column), (half, lanes))
            for mat in (w_gate, w_up)
        ]
        return jnp.where(spot // 2 * lanes < ff_own, cuts[0], cuts[1])

    near_columns = columns(shard ^ 1)
    far_cut = jnp.concatenate([far_columns(shard ^ distance) for distance in (2, 3)], axis=0)
    query_own = jnp.concatenate([w_query, far_cut], axis=1)
    cosine, sine, ids, near_columns, query_own = lax.optimization_barrier(
        (cosine, sine, ids, near_columns, query_own)
    )
    query_weights = gather(query_own, far)
    out_far = hop(after(w_out, query_weights[2]), 2)
    fetch_sems = pltpu.SemaphoreType.DMA((n_shard,))
    hidden, kv, gain_one, gain_two = call_once(
        functools.partial(keys_kernel, sizes=sizes, kvw=kvw),
        [((count, width), BF16), ((count, 2 * kvw), BF16), ((1, width), F32), ((1, width), F32)],
        [x, cosine, sine],
        held=[ids],
        moved=kv_weights,
        scratch=[
            pltpu.VMEM((width, 2 * kvw), BF16),
            pltpu.VMEM((n_shard, 16, 2 * kvw), BF16),
            fetch_sems,
            fetch_sems,
        ],
        flops=4 * count * width * kvw,
        limit=ALL_VMEM,
        name="keys",
    )
    all_kv = collect(kv)

    (queries,) = call_once(
        functools.partial(queries_kernel, sizes=sizes),
        [((count, qw), BF16)],
        [hidden, cosine, sine],
        held=[ids],
        moved=query_weights,
        scratch=[pltpu.VMEM((width, qw), BF16), fetch_sems],
        flops=2 * count * width * qw,
        name="queries",
    )
    out_weights = [w_out, hop(w_out, 1), out_far, hop(after(out_far, queries), 1)]
    far_tile = jnp.concatenate(
        [query_weights[2][:half, qw:], query_weights[3][half:, qw:]], axis=0
    )
    far_rows = collect(after(far_tile, kv)[None])
    near_part = hop(near_columns, 1)
    cot_near = hop(cot, 1)
    cot_far = hop(after(cot, (out_weights[2], queries)), 2)

    shared = dict(sizes=sizes, column=0, groups=groups, per=per, blocks=blocks)
    fixed = lambda *shape: pl.BlockSpec(shape, lambda step, table: (0,) * len(shape))
    kv_spec = pl.BlockSpec(
        (count, 2 * kvw), lambda step, table: (ring_place(jnp.minimum(step, table[1]), blocks), 0)
    )
    once = lambda *shape: block(shape)
    weight_specs = [HBM_SPEC] * len(sizes)
    span = per * count
    out_tall, attended, log_total, mid, normed, q_cols = pl.pallas_call(
        functools.partial(attend_kernel, **shared),
        out_shape=(
            jax.ShapeDtypeStruct((qw, count), F32),
            jax.ShapeDtypeStruct((count, qw), BF16),
            jax.ShapeDtypeStruct((8, span), F32),
            jax.ShapeDtypeStruct((count, width), F32),
            jax.ShapeDtypeStruct((count, width), BF16),
            jax.ShapeDtypeStruct((groups, HEAD, span), BF16),
        ),
        grid_spec=pltpu.PrefetchScalarGridSpec(
            num_scalar_prefetch=1,
            grid=(blocks,),
            in_specs=[once(count, qw), kv_spec, once(count, width), once(1, width)]
            + weight_specs,
            out_specs=[
                fixed(qw, count),
                fixed(count, qw),
                fixed(8, span),
                fixed(count, width),
                fixed(count, width),
                fixed(groups, HEAD, span),
            ],
            scratch_shapes=[
                pltpu.VMEM((groups, HEAD, span), F32),
                pltpu.VMEM((8, span), F32),
                pltpu.VMEM((8, span), F32),
                pltpu.VMEM((qw, width), BF16),
                pltpu.VMEM((2, count, span), F32),
                pltpu.VMEM((qw, count), F32),
                pltpu.SemaphoreType.DMA((len(sizes),)),
            ],
        ),
        compiler_params=params(),
        cost_estimate=cost(
            4 * count * count * blocks * qw, 12e6, count * count * blocks * groups * per
        ),
        name="attend",
    )(ids, queries, all_kv, x, gain_two, *out_weights)

    normed_far = hop(normed, 2)
    normed_near = hop(normed, 1)
    cot_far = after(cot_far, normed)
    far_rows = after(far_rows, normed)
    all_count = n_shard * count
    if aligned:
        two = ((2, count, ff_own), BF16)
        mats = [((width, ff_own), BF16)] * 2
        pair = (2, count, width)
        gate_mat, up_mat, *near_units, back = pl.pallas_call(
            functools.partial(feed_near_kernel, half=half, lanes=lanes),
            out_shape=tuple(
                jax.ShapeDtypeStruct(*out) for out in [*mats, two, two, two, (pair, BF16)]
            ),
            in_specs=[SMEM_SPEC] + [HBM_SPEC] * 9,
            out_specs=(HBM_SPEC,) * 6,
            scratch_shapes=[
                pltpu.VMEM((width, ff_own), BF16),
                pltpu.VMEM((width, ff_own), BF16),
                pltpu.VMEM((ff_own, width), BF16),
                pltpu.VMEM(pair, BF16),
                pltpu.VMEM(pair, BF16),
                pltpu.VMEM(*two),
                pltpu.VMEM(*two),
                pltpu.VMEM(*two),
                pltpu.VMEM(pair, BF16),
                pltpu.SemaphoreType.DMA((4 + 2 * n_ctx,)),
                pltpu.SemaphoreType.DMA((3, 2)),
                pltpu.SemaphoreType.DMA((6,)),
            ],
            compiler_params=params(),
            cost_estimate=cost(10 * 2 * count * width * ff_own, 12e6),
            name="feed_near",
        )(
            ids,
            w_gate,
            w_up,
            near_part,
            far_rows,
            w_down,
            normed,
            normed_near,
            cot,
            cot_near,
        )
        normed_far, cot_far = lax.optimization_barrier((normed_far, cot_far, back))[:2]
        normed_pieces = [normed, normed_near, normed_far, hop(normed_far, 1)]
        cot_pieces = [cot, cot_near, cot_far, hop(cot_far, 1)]
        late = ((2 * count, ff_own), BF16)
        feed_tiles, *far_units = pl.pallas_call(
            functools.partial(feed_far_kernel, per_shard=per_shard),
            out_shape=tuple(
                jax.ShapeDtypeStruct(*out)
                for out in [((n_ctx, 3 * rows, tile), BF16), late, late, late]
            ),
            in_specs=[SMEM_SPEC] + [HBM_SPEC] * (6 + 2 * n_shard),
            out_specs=(HBM_SPEC,) * 4,
            scratch_shapes=[
                pltpu.VMEM((width, ff_own), BF16),
                pltpu.VMEM((width, ff_own), BF16),
                pltpu.VMEM((ff_own, width), BF16),
                pltpu.VMEM((n_shard, count, width), BF16),
                pltpu.VMEM((all_count, width), BF16),
                pltpu.VMEM((width, all_count), BF16),
                pltpu.VMEM((all_count, ff_own), BF16),
                pltpu.VMEM((all_count, ff_own), BF16),
                pltpu.VMEM((all_count, ff_own), BF16),
                pltpu.VMEM((n_ctx, 3 * rows, tile), BF16),
                pltpu.SemaphoreType.DMA((3,)),
                pltpu.SemaphoreType.DMA((n_shard,)),
                pltpu.SemaphoreType.DMA((n_shard,)),
                pltpu.SemaphoreType.DMA((3, 2)),
                pltpu.SemaphoreType.DMA((3,)),
                pltpu.SemaphoreType.DMA((2, n_ctx)),
            ],
            compiler_params=params(),
            cost_estimate=cost(9 * all_count * width * ff_own, 25e6),
            name="feed_far",
        )(
            ids, gate_mat, up_mat, w_down, *near_units, *normed_pieces, *cot_pieces
        )
        to_own, to_near = back[0], back[1]
        act_parts = [near_units[0].reshape(2 * count, ff_own), far_units[0]]
        grad_gate_far, grad_up_far = far_units[1:]
    else:
        normed_pieces = [normed, normed_near, normed_far, hop(normed_far, 1)]
        cot_pieces = [cot, cot_near, cot_far, hop(cot_far, 1)]
        tiles_of = far_rows.reshape(n_ctx // 2, 2, 2, half, lanes)
        tiles_of = tiles_of.transpose(2, 1, 3, 0, 4).reshape(2, rows, 2 * ff_own)
        gate_mat = jnp.zeros((width, ff_own), BF16)
        up_mat = jnp.zeros((width, ff_own), BF16)
        for part, start in zip(
            (columns(shard), near_part, tiles_of[0], tiles_of[1]),
            [(shard ^ k) * rows for k in range(n_shard)],
        ):
            gate_mat = lax.dynamic_update_slice_in_dim(gate_mat, part[:, :ff_own], start, 0)
            up_mat = lax.dynamic_update_slice_in_dim(up_mat, part[:, ff_own:], start, 0)
        all_cot = jnp.concatenate(cot_pieces, axis=0)
        all_normed = jnp.concatenate(normed_pieces, axis=0)
        gate = nn(all_normed, gate_mat)
        up = nn(all_normed, up_mat)
        grad_activated = nt(all_cot, w_down)
        sigmoid = jax.nn.sigmoid(gate)
        activated = (gate * sigmoid * up).astype(BF16)
        grad_gate = (grad_activated * up * (sigmoid * (1.0 + gate * (1.0 - sigmoid)))).astype(BF16)
        grad_up = (grad_activated * (gate * sigmoid)).astype(BF16)

        def tiles(grad):
            pieces = grad.astype(BF16).reshape(n_shard, rows, per_shard, tile)
            pieces = pieces.transpose(0, 2, 1, 3)
            return jnp.roll(pieces, shard, axis=0).reshape(n_ctx, rows, tile)

        down = tn(activated, all_cot).astype(BF16)
        down = down.reshape(n_ctx, ff_own // n_ctx, width // tile, tile).transpose(0, 2, 1, 3)
        feed_tiles = jnp.concatenate(
            [
                tiles(tn(all_normed, grad_gate)),
                tiles(tn(all_normed, grad_up)),
                down.reshape(n_ctx, rows, tile),
            ],
            axis=1,
        )
        grad_gate_far, grad_up_far = grad_gate[2 * count :], grad_up[2 * count :]
        back = nt(grad_gate[: 2 * count], gate_mat) + nt(grad_up[: 2 * count], up_mat)
        to_own, to_near = back[:count].astype(BF16), back[count:].astype(BF16)
        act_parts = [activated[: 2 * count], activated[2 * count :]]
    from_near = hop(to_near, 1)
    feed_sum = scatter(feed_tiles)
    down_sum = feed_sum[2 * rows :]
    pairs = []
    for index in range(n_ctx):
        for source in range(n_shard):
            target = (places[index] // per_shard - source) % n_shard
            pairs.append((index * n_shard + source, index * n_shard + target))
    gate_up_sum = lax.ppermute(feed_sum[: 2 * rows], ("ctx", "shard"), pairs)

    to_far, to_third = call_once(
        normed_back_kernel,
        [((count, width), BF16)] * 2,
        [grad_gate_far, grad_up_far, gate_mat, up_mat],
        flops=8 * count * width * ff_own,
        limit=ALL_VMEM,
        name="normed_back",
    )
    third = hop(to_third, 1)
    across = (to_far.astype(F32) + third.astype(F32)).astype(BF16)
    from_far = hop(across, 2)

    part_out = [after(nn(part, w_down).astype(BF16), from_far) for part in act_parts]
    part_out = [part[k * count : (k + 1) * count] for part in part_out for k in range(2)]
    output = (mid + add(reduce(part_out))).astype(BF16)[None]

    place_spec = pl.BlockSpec(
        (count, 2 * kvw), lambda step, table: (ring_place(step, blocks), 0)
    )
    grad_query, grad_kv, branch, grad_mid, gain_two_part = pl.pallas_call(
        functools.partial(attend_back_kernel, **shared),
        out_shape=(
            jax.ShapeDtypeStruct((count, qw), BF16),
            jax.ShapeDtypeStruct((blocks * count, 2 * kvw), BF16),
            jax.ShapeDtypeStruct((count, width), BF16),
            jax.ShapeDtypeStruct((count, width), F32),
            jax.ShapeDtypeStruct((1, width), F32),
        ),
        grid_spec=pltpu.PrefetchScalarGridSpec(
            num_scalar_prefetch=1,
            grid=(blocks,),
            in_specs=[
                kv_spec,
                once(groups, HEAD, span),
                once(qw, count),
                once(8, span),
                once(count, width),
                once(1, width),
                once(count, width),
                once(count, width),
                once(count, width),
                once(count, width),
                once(count, LANES),
                once(count, LANES),
            ]
            + weight_specs,
            out_specs=[
                fixed(count, qw),
                place_spec,
                fixed(count, width),
                fixed(count, width),
                fixed(1, width),
            ],
            scratch_shapes=[
                pltpu.VMEM((qw, width), BF16),
                pltpu.VMEM((groups, HEAD, span), BF16),
                pltpu.VMEM((8, span), F32),
                pltpu.VMEM((groups, HEAD, span), F32),
                pltpu.VMEM((2, 2, count, span), F32),
                pltpu.VMEM((qw, count), F32),
                pltpu.SemaphoreType.DMA((len(sizes),)),
            ],
        ),
        compiler_params=params(),
        cost_estimate=cost(
            10 * count * count * blocks * qw, 14e6, count * count * blocks * groups * per
        ),
        name="attend_back",
    )(
        ids,
        all_kv,
        q_cols,
        out_tall,
        log_total,
        mid,
        gain_two,
        cot,
        to_own,
        from_near,
        from_far,
        cosine,
        sine,
        *out_weights,
    )
    own_kv = scatter(after(grad_kv, down_sum).reshape(n_ctx, count, 2 * kvw))

    def stack(parts, breadth, name):
        height = sum(part.shape[0] * part.shape[1] for part in parts[::3]) // breadth
        if breadth % LANES:
            wide = jnp.concatenate(
                [add(parts[index : index + 3]) for index in range(0, len(parts), 3)], axis=1
            )
            wide = wide.astype(BF16).reshape(rows, -1, breadth)
            return wide.transpose(1, 0, 2).reshape(height, breadth)
        return call_once(stack_kernel, [((height, breadth), BF16)], parts, flops=1e6, name=name)[0]

    grad_blocks = call_once(
        weight_grads_kernel,
        [((rows, qw), BF16)] * n_shard + [((rows, width), BF16)] * n_shard,
        [hidden, grad_query, attended, branch],
        held=[ids],
        scratch=[pltpu.VMEM((width, qw), F32)],
        flops=4 * count * width * qw,
        limit=ALL_VMEM,
        name="weight_grads",
    )
    parts_query = reduce(grad_blocks[:n_shard])
    parts_out = reduce(grad_blocks[n_shard:])
    mixed = stack(parts_query + parts_out, tile, "stack_mixed")
    mixed_sum = scatter(after(mixed, own_kv).reshape(n_ctx, -1, tile))

    grad_kv_pre, *kv_blocks = call_once(
        functools.partial(kv_back_kernel, kvw=kvw),
        [((count, 2 * kvw), BF16)] + [((rows, 2 * kvw), BF16)] * n_shard,
        [own_kv, cosine, sine, hidden],
        held=[ids],
        scratch=[pltpu.VMEM((width, 2 * kvw), F32)],
        flops=4 * count * width * kvw,
        name="kv_back",
    )
    sum_kv = stack(reduce(kv_blocks), LANES, "stack_kv").reshape(n_ctx, -1, LANES)
    shares = jnp.concatenate([gate_up_sum, down_sum, jnp.zeros_like(mixed_sum)])
    shares = lax.dynamic_update_slice_in_dim(after(shares, sum_kv), mixed_sum, 3 * rows, 0)
    gathered = collect(shares[None])

    def exchange(value):
        return lax.all_to_all(value, "ctx", split_axis=0, concat_axis=0, tiled=True)

    own_sum = jnp.sum(exchange(sum_kv).astype(F32), axis=0, keepdims=True).astype(BF16)
    both = exchange(jnp.broadcast_to(own_sum, sum_kv.shape))
    both = both.reshape(2 * kvw // LANES, rows, LANES).transpose(1, 0, 2).reshape(rows, 2 * kvw)
    grad_w_key = both[:, :kvw].astype(F32)
    grad_w_value = both[:, kvw:].astype(F32)

    grad_x, gain_one_part = call_once(
        functools.partial(inputs_kernel, sizes=sizes),
        [((count, width), BF16), ((1, width), F32)],
        [grad_query, grad_kv_pre, x, gain_one, grad_mid],
        held=[ids],
        moved=[*query_weights, *kv_weights],
        scratch=[
            pltpu.VMEM((width, qw), BF16),
            pltpu.VMEM((width, 2 * kvw), BF16),
            pltpu.VMEM((count, width), F32),
            fetch_sems,
            fetch_sems,
        ],
        flops=2 * count * width * (qw + 2 * kvw),
        name="grad_inputs",
    )

    gain_parts = jnp.concatenate([gain_one_part, gain_two_part], axis=0)
    for distance in [1 << bit for bit in range(n_shard.bit_length() - 1)]:
        gain_parts = gain_parts + hop(gain_parts, distance)
    for distance in [1 << bit for bit in range(n_ctx.bit_length() - 1)]:
        gain_parts = gain_parts + ctx_hop(gain_parts, distance)
    own_gains = lax.dynamic_slice_in_dim(gain_parts, shard * rows, rows, 1)

    if aligned:
        share = mixed_sum.shape[0]
        rolled = lambda step, where: (lax.rem(step + where[0], n_shard), 0, 0)
        band = ff_own // n_ctx
        grad_w_gate, grad_w_up, grad_w_down, grad_w_query, grad_w_out = pl.pallas_call(
            functools.partial(widen_kernel, rows=rows),
            out_shape=(
                jax.ShapeDtypeStruct((rows, ff), F32),
                jax.ShapeDtypeStruct((rows, ff), F32),
                jax.ShapeDtypeStruct((ff_own, width), F32),
                jax.ShapeDtypeStruct((rows, qw), F32),
                jax.ShapeDtypeStruct((rows, width), F32),
            ),
            grid_spec=pltpu.PrefetchScalarGridSpec(
                num_scalar_prefetch=1,
                grid=(n_shard,),
                in_specs=[
                    pl.BlockSpec((per_shard, 2 * rows, tile), rolled),
                    pl.BlockSpec((per_shard, rows, tile), lambda step, where: (step, 2, 0)),
                    pl.BlockSpec(
                        (per_shard, share, tile),
                        lambda step, where: (step, 3 * rows // share, 0),
                    ),
                ],
                out_specs=[
                    pl.BlockSpec((rows, ff_own), lambda step, where: (0, step)),
                    pl.BlockSpec((rows, ff_own), lambda step, where: (0, step)),
                    pl.BlockSpec((per_shard * band, width), lambda step, where: (step, 0)),
                    pl.BlockSpec((rows, qw), lambda step, where: (0, 0)),
                    pl.BlockSpec((rows, width), lambda step, where: (0, 0)),
                ],
                scratch_shapes=[pltpu.VMEM((n_ctx * share, tile), F32)],
            ),
            compiler_params=params(),
            cost_estimate=cost(1e6, 20e6),
            name="widen",
        )(ids, gathered, gathered, gathered)
    else:

        def untile(part):
            back = jnp.roll(part.reshape(n_shard, per_shard, rows, tile), -shard, axis=0)
            back = back.reshape(n_ctx, rows, tile).transpose(1, 0, 2)
            return back.reshape(rows, ff).astype(F32)

        grad_w_gate = untile(gathered[:, :rows])
        grad_w_up = untile(gathered[:, rows : 2 * rows])
        down = gathered[:, 2 * rows : 3 * rows].reshape(n_ctx, width // tile, -1, tile)
        grad_w_down = down.transpose(0, 2, 1, 3).reshape(ff_own, width).astype(F32)
        wide = gathered[:, 3 * rows :].reshape(2 * qw // tile, rows, tile).transpose(1, 0, 2)
        wide = wide.reshape(rows, 2 * qw).astype(F32)
        grad_w_query, grad_w_out = wide[:, :qw], wide[:, qw:]

    return (
        output,
        grad_x[None],
        own_gains[0],
        grad_w_query,
        grad_w_key,
        grad_w_value,
        grad_w_out,
        own_gains[1],
        grad_w_gate,
        grad_w_up,
        grad_w_down,
    )


def solution(mesh):
    tokens = P("shard", "ctx", None)
    split = P("shard", None)
    gain = P("shard")
    placed = (tokens, gain, split, split, split, split, gain, split, split, split, tokens)
    return jax.shard_map(
        functools.partial(on_device, n_ctx=mesh.shape["ctx"], n_shard=mesh.shape["shard"]),
        mesh=mesh,
        in_specs=placed,
        out_specs=(tokens, tokens, gain, split, split, split, split, gain, split, split, split),
        check_vma=False,
    )
```

```python
import functools
import math

import jax
import jax.numpy as jnp
from jax import lax
from jax.experimental import pallas as pl
from jax.experimental.pallas import tpu as pltpu
from jax.sharding import PartitionSpec as P

HEAD = 64
BLOCK = 256
EPSILON = 1e-05
LANES = 128
F32 = jnp.float32
BF16 = jnp.bfloat16
SCORE_SCALE = math.log2(math.e) * 0.125
NEGATIVE = -1e30
ALL_VMEM = 60 * 1024 * 1024
PART_VMEM = 32 * 1024 * 1024


def nn(left, right):
    return lax.dot_general(left, right, (((1,), (0,)), ((), ())), preferred_element_type=F32)


def nt(left, right):
    return lax.dot_general(left, right, (((1,), (1,)), ((), ())), preferred_element_type=F32)


def tn(left, right):
    return lax.dot_general(left, right, (((0,), (0,)), ((), ())), preferred_element_type=F32)


def ring_order(count):
    return list(range(0, count, 2)) + list(range(count - 1, 0, -2))


def ring_place(index, count):
    return jnp.where(index % 2 == 0, index // 2, count - 1 - index // 2)


def params(limit=ALL_VMEM):
    return pltpu.CompilerParams(vmem_limit_bytes=limit)


def cost(flops, moved, exps=0):
    return pl.CostEstimate(flops=int(flops), bytes_accessed=int(moved), transcendentals=int(exps))


HBM_SPEC = pl.BlockSpec(memory_space=pltpu.HBM)
SMEM_SPEC = pl.BlockSpec(memory_space=pltpu.SMEM)


def block(shape):
    return pl.BlockSpec(shape, lambda *_: (0,) * len(shape), pipeline_mode=pl.Buffered(1))


def call_once(
    kernel, outs, ins, held=(), moved=(), scratch=(), flops=0, limit=PART_VMEM, name=None
):
    return pl.pallas_call(
        kernel,
        out_shape=tuple(jax.ShapeDtypeStruct(shape, dtype) for shape, dtype in outs),
        grid=(1,),
        in_specs=[SMEM_SPEC] * len(held)
        + [block(array.shape) for array in ins]
        + [HBM_SPEC] * len(moved),
        out_specs=tuple(pl.BlockSpec(shape, lambda *_: (0,) * len(shape)) for shape, _ in outs),
        scratch_shapes=list(scratch),
        compiler_params=params(limit),
        cost_estimate=cost(flops, sum(2 * math.prod(shape) for shape, _ in outs) + 4e6),
        name=name,
    )(*held, *ins, *moved)


def swap_halves(tile):
    lane = lax.broadcasted_iota(jnp.int32, tile.shape, 1)
    ahead = pltpu.roll(tile, LANES - HEAD // 2, 1)
    behind = pltpu.roll(tile, HEAD // 2, 1)
    return jnp.where(lane % HEAD < HEAD // 2, ahead, behind)


def row_start(ids_ref, hop, rows):
    return pl.multiple_of((ids_ref[0] ^ hop) * rows, 16)


def fetches(ids_ref, pieces, whole, sems, sizes, column=0):
    copies = []
    for index, (piece, size) in enumerate(zip(pieces, sizes)):
        start = row_start(ids_ref, index, size)
        copies.append(
            pltpu.make_async_copy(
                piece.at[pl.ds(0, size), pl.ds(column, whole.shape[1])],
                whole.at[pl.ds(start, size), :],
                sems.at[index],
            )
        )
    return copies


def keys_kernel(ids_ref, x_ref, cos_ref, sin_ref, *rest, sizes, kvw):
    pieces = rest[: len(sizes)]
    hidden_ref, kv_ref, one_ref, two_ref, whole, bands, sems, band_sems = rest[len(sizes) :]
    copies = fetches(ids_ref, pieces, whole, sems, sizes)
    rows = sizes[0]
    for index, piece in enumerate(pieces):
        band = pltpu.make_async_copy(
            piece.at[pl.ds(rows, 16), :], bands.at[index], band_sems.at[index]
        )
        band.start()
        copies[index].start()
    x = x_ref[...].astype(F32)
    scale = lax.rsqrt(jnp.mean(x * x, axis=-1, keepdims=True) + EPSILON)
    width = x.shape[1]
    ones = jnp.zeros((8, width), F32)
    twos = jnp.zeros((8, width), F32)
    for index, piece in enumerate(pieces):
        pltpu.make_async_copy(
            piece.at[pl.ds(rows, 16), :], bands.at[index], band_sems.at[index]
        ).wait()
        band = bands[index].astype(F32)[:8, :]
        blank = jnp.zeros((8, width - rows), F32)
        first = jnp.concatenate([band[:, :rows], blank], axis=1)
        second = jnp.concatenate([band[:, rows : 2 * rows], blank], axis=1)
        ones = ones + pltpu.roll(first, (ids_ref[0] ^ index) * rows, 1)
        twos = twos + pltpu.roll(second, (ids_ref[0] ^ index) * rows, 1)
    one_ref[...] = ones[:1, :]
    two_ref[...] = twos[:1, :]
    hidden = (x * scale * ones[:1, :]).astype(BF16)
    hidden_ref[...] = hidden
    for copy in copies:
        copy.wait()
    pre = nn(hidden, whole[...])
    for start in range(0, kvw, LANES):
        tile = pre[:, start : start + LANES]
        turned = tile * cos_ref[...] + swap_halves(tile) * sin_ref[...]
        kv_ref[:, start : start + LANES] = turned.astype(BF16)
    kv_ref[:, kvw:] = pre[:, kvw:].astype(BF16)


def queries_kernel(ids_ref, hidden_ref, cos_ref, sin_ref, *rest, sizes):
    pieces = rest[: len(sizes)]
    query_ref, whole, sems = rest[len(sizes) :]
    copies = fetches(ids_ref, pieces, whole, sems, sizes)
    for copy in copies:
        copy.start()
    for copy in copies:
        copy.wait()
    pre = nn(hidden_ref[...], whole[...])
    for start in range(0, pre.shape[1], LANES):
        tile = pre[:, start : start + LANES]
        turned = tile * cos_ref[...] + swap_halves(tile) * sin_ref[...]
        query_ref[:, start : start + LANES] = turned.astype(BF16)


def attend_kernel(
    table_ref,
    q_ref,
    kv_ref,
    x_ref,
    gain_ref,
    *rest,
    sizes,
    column,
    groups,
    per,
    blocks,
):
    pieces = rest[:-13]
    (
        out_ref,
        attended_ref,
        log_ref,
        mid_ref,
        normed_ref,
        cols_ref,
        acc,
        top,
        total,
        whole,
        scores,
        tall,
        sems,
    ) = rest[-13:]
    step = pl.program_id(0)
    last = table_ref[1]
    count = q_ref.shape[0]
    kvw = groups * HEAD

    @pl.when(step == 0)
    def _():
        for copy in fetches(table_ref, pieces, whole, sems, sizes, column):
            copy.start()
        turned = q_ref[...].T
        for group in range(groups):
            for member in range(per):
                head = group * per + member
                cols_ref[group, :, member * count : (member + 1) * count] = turned[
                    head * HEAD : (head + 1) * HEAD, :
                ]
        acc[...] = jnp.zeros_like(acc)
        total[...] = jnp.zeros_like(total)
        top[...] = jnp.full_like(top, NEGATIVE)

    @pl.when(step <= last)
    def _():
        def score(group):
            key = kv_ref[:, group * HEAD : (group + 1) * HEAD]
            scores[group % 2] = nn(key, cols_ref[group])

        score(0)
        for group in range(groups):
            if group + 1 < groups:
                score(group + 1)
            value = kv_ref[:, kvw + group * HEAD : kvw + (group + 1) * HEAD]
            raw = scores[group % 2]
            old = top[group : group + 1, :]
            new = jnp.maximum(old, jnp.max(raw, axis=0, keepdims=True))
            shrink = jnp.exp2((old - new) * SCORE_SCALE)
            probs = jnp.exp2((raw - new) * SCORE_SCALE)
            top[group : group + 1, :] = new
            total[group : group + 1, :] = total[group : group + 1, :] * shrink + jnp.sum(
                probs, axis=0, keepdims=True
            )
            acc[group] = acc[group] * shrink + tn(value, probs.astype(BF16))

    @pl.when(step == blocks - 1)
    def _():
        for group in range(groups):
            sums = total[group : group + 1, :]
            log_ref[group : group + 1, :] = top[
                group : group + 1, :
            ] * SCORE_SCALE + jnp.log2(sums)
            rowed = acc[group] / sums
            for member in range(per):
                head = group * per + member
                tall[head * HEAD : (head + 1) * HEAD, :] = rowed[
                    :, member * count : (member + 1) * count
                ]
        out_ref[...] = tall[...]
        attended = tall[...].astype(BF16).T
        attended_ref[...] = attended
        for copy in fetches(table_ref, pieces, whole, sems, sizes, column):
            copy.wait()
        mid = x_ref[...].astype(F32) + nn(attended, whole[...])
        mid_ref[...] = mid
        scale = lax.rsqrt(jnp.mean(mid * mid, axis=-1, keepdims=True) + EPSILON)
        normed_ref[...] = (mid * scale * gain_ref[...]).astype(BF16)


def attend_back_kernel(
    table_ref,
    kv_ref,
    cols_ref,
    out_ref,
    log_ref,
    mid_ref,
    gain_ref,
    cot_ref,
    gn_own_ref,
    gn_near_ref,
    gn_far_ref,
    cos_ref,
    sin_ref,
    *rest,
    sizes,
    column,
    groups,
    per,
    blocks,
):
    pieces = rest[: len(sizes)]
    (
        gq_ref,
        gkv_ref,
        branch_ref,
        gmid_ref,
        ggain_ref,
        whole,
        d_cols,
        delta,
        acc,
        probs_all,
        tall,
        sems,
    ) = rest[len(sizes) :]
    step = pl.program_id(0)
    last = table_ref[1]
    count = kv_ref.shape[0]
    kvw = groups * HEAD

    @pl.when(step == 0)
    def _():
        copies = fetches(table_ref, pieces, whole, sems, sizes, column)
        for copy in copies:
            copy.start()
        mid = mid_ref[...]
        incoming = (
            gn_own_ref[...].astype(F32) + gn_near_ref[...].astype(F32)
        ) + gn_far_ref[...].astype(F32)
        gain = gain_ref[...]
        scale = lax.rsqrt(jnp.mean(mid * mid, axis=-1, keepdims=True) + EPSILON)
        weighted = incoming * gain
        inner = jnp.mean(weighted * mid, axis=-1, keepdims=True)
        ggain_ref[...] = jnp.sum(incoming * mid * scale, axis=0, keepdims=True)
        grad_mid = (
            cot_ref[...].astype(F32) + scale * weighted - mid * (scale * scale * scale * inner)
        )
        gmid_ref[...] = grad_mid
        branch = grad_mid.astype(BF16)
        branch_ref[...] = branch
        for copy in copies:
            copy.wait()
        grads = nt(branch, whole[...]).astype(BF16)
        turned = grads.T
        tall[...] = turned.astype(F32) * out_ref[...]
        for group in range(groups):
            for member in range(per):
                head = group * per + member
                span = slice(head * HEAD, (head + 1) * HEAD)
                cols = slice(member * count, (member + 1) * count)
                d_cols[group, :, cols] = turned[span, :]
                delta[group : group + 1, cols] = jnp.sum(tall[span, :], axis=0, keepdims=True)
        acc[...] = jnp.zeros_like(acc)

    @pl.when(step > last)
    def _():
        gkv_ref[...] = jnp.zeros_like(gkv_ref)

    @pl.when(step <= last)
    def _():
        def spans(group):
            return (
                slice(group * HEAD, (group + 1) * HEAD),
                slice(kvw + group * HEAD, kvw + (group + 1) * HEAD),
            )

        def score(group):
            key_span, value_span = spans(group)
            probs_all[group % 2, 0] = nn(kv_ref[:, key_span], cols_ref[group])
            probs_all[group % 2, 1] = nn(kv_ref[:, value_span], d_cols[group])

        score(0)
        for group in range(groups):
            if group + 1 < groups:
                score(group + 1)
            key_span, value_span = spans(group)
            probs = jnp.exp2(
                probs_all[group % 2, 0] * SCORE_SCALE - log_ref[group : group + 1, :]
            )
            grad_scores = (
                probs * (probs_all[group % 2, 1] - delta[group : group + 1, :])
            ).astype(BF16)
            gkv_ref[:, value_span] = nt(probs.astype(BF16), d_cols[group]).astype(BF16)
            gkv_ref[:, key_span] = (nt(grad_scores, cols_ref[group]) * 0.125).astype(BF16)
            acc[group] = acc[group] + tn(kv_ref[:, key_span], grad_scores)

    @pl.when(step == blocks - 1)
    def _():
        for group in range(groups):
            for member in range(per):
                head = group * per + member
                tall[head * HEAD : (head + 1) * HEAD, :] = (
                    acc[group, :, member * count : (member + 1) * count] * 0.125
                )
        for start in range(0, tall.shape[0], LANES):
            tile = tall[start : start + LANES, :].T
            turned = tile * cos_ref[...] - swap_halves(tile) * sin_ref[...]
            gq_ref[:, start : start + LANES] = turned.astype(BF16)


def columns_in_turn(left, right, full):
    breadth = full.shape[1] // 3

    def third(index, carry):
        span = pl.ds(pl.multiple_of(index * breadth, LANES), breadth)
        full[:, span] = tn(left[...], right[:, span])
        return carry

    lax.fori_loop(0, 3, third, 0)


def kv_back_kernel(ids_ref, grad_ref, cos_ref, sin_ref, hidden_ref, out_ref, *rest, kvw):
    outs, full = rest[:-1], rest[-1]
    for start in range(0, kvw, LANES):
        tile = grad_ref[:, start : start + LANES].astype(F32)
        turned = tile * cos_ref[...] - swap_halves(tile) * sin_ref[...]
        out_ref[:, start : start + LANES] = turned.astype(BF16)
    out_ref[:, kvw:] = grad_ref[:, kvw:]
    columns_in_turn(hidden_ref, out_ref, full)
    for index, out in enumerate(outs):
        start = row_start(ids_ref, index, out.shape[0])
        out[...] = full[pl.ds(start, out.shape[0]), :].astype(BF16)


def stack_kernel(*refs):
    parts, out_ref = refs[:-1], refs[-1]
    tile = out_ref.shape[1]
    row = 0
    for index in range(0, len(parts), 3):
        first, second, third = parts[index : index + 3]
        rows, columns = first.shape
        for start in range(0, columns, tile):
            span = slice(start, start + tile)
            total = (
                first[:, span].astype(F32) + second[:, span].astype(F32)
            ) + third[:, span].astype(F32)
            out_ref[row : row + rows, :] = total.astype(BF16)
            row += rows


def inputs_kernel(ids_ref, gq_ref, gkv_ref, x_ref, gain_ref, gmid_ref, *rest, sizes):
    hops = len(sizes)
    grad_ref, ggain_ref, whole_q, whole_kv, arriving, q_sems, kv_sems = rest[2 * hops :]
    copies = fetches(ids_ref, rest[:hops], whole_q, q_sems, sizes)
    copies += fetches(ids_ref, rest[hops : 2 * hops], whole_kv, kv_sems, sizes)
    for copy in copies:
        copy.start()
    for copy in copies:
        copy.wait()
    breadth = arriving.shape[1] // 3

    def third(index, carry):
        span = pl.ds(pl.multiple_of(index * breadth, LANES), breadth)
        arriving[:, span] = nt(gq_ref[...], whole_q[span, :]) + nt(gkv_ref[...], whole_kv[span, :])
        return carry

    lax.fori_loop(0, 3, third, 0)
    incoming = arriving[...]
    x = x_ref[...].astype(F32)
    scale = lax.rsqrt(jnp.mean(x * x, axis=-1, keepdims=True) + EPSILON)
    weighted = incoming * gain_ref[...]
    inner = jnp.mean(weighted * x, axis=-1, keepdims=True)
    ggain_ref[...] = jnp.sum(incoming * x * scale, axis=0, keepdims=True)
    grad = gmid_ref[...] + scale * weighted - x * (scale * scale * scale * inner)
    grad_ref[...] = grad.astype(BF16)


def weight_grads_kernel(ids_ref, hidden_ref, query_ref, attended_ref, branch_ref, *rest):
    outs, full = rest[:-1], rest[-1]
    hops = len(outs) // 2
    for index, (left, right) in enumerate(((hidden_ref, query_ref), (attended_ref, branch_ref))):
        full[...] = tn(left[...], right[...])
        for hop, out in enumerate(outs[index * hops : (index + 1) * hops]):
            start = row_start(ids_ref, hop, out.shape[0])
            out[...] = full[pl.ds(start, out.shape[0]), :].astype(BF16)


def units(normed, cot, gate_mat, up_mat, down_mat):
    gate = nn(normed, gate_mat)
    up = nn(normed, up_mat)
    grad = nt(cot, down_mat)
    sigmoid = 1.0 / (1.0 + jnp.exp(-gate))
    silu = gate * sigmoid
    return (
        (silu * up).astype(BF16),
        (grad * up * (sigmoid * (1.0 + gate * (1.0 - sigmoid)))).astype(BF16),
        (grad * silu).astype(BF16),
    )


def feed_near_kernel(
    ids_ref, own_gate_ref, own_up_ref, near_ref, far_ref, down_ref, *rest, half, lanes
):
    normed_refs, cot_refs = rest[:2], rest[2:4]
    gate_mat_out, up_mat_out, act_out, gate_out, up_out, back_out = rest[4:10]
    gate_mat, up_mat, down_mat, tokens, cots, act, grad_gate, grad_up, back = rest[10:19]
    mat_sems, token_sems, out_sems = rest[19:]
    rows = near_ref.shape[0]
    own = gate_mat.shape[1]
    mats = []

    def place(source, row, column, height, breadth):
        target = gate_mat if column < own else up_mat
        mats.append(
            pltpu.make_async_copy(
                source,
                target.at[pl.ds(row, height), pl.ds(column % own, breadth)],
                mat_sems.at[len(mats)],
            )
        )

    mine = pl.ds(pl.multiple_of(ids_ref[0] * own, LANES), own)
    for index, ref in enumerate((own_gate_ref, own_up_ref)):
        place(ref.at[:, mine], row_start(ids_ref, 0, rows), index * own, rows, own)
        place(
            near_ref.at[:, pl.ds(index * own, own)],
            row_start(ids_ref, 1, rows),
            index * own,
            rows,
            own,
        )
    for spot in range(far_ref.shape[0]):
        for index in range(2):
            place(
                far_ref.at[spot, pl.ds(index * half, half), :],
                pl.multiple_of(row_start(ids_ref, 2 + index, rows) + (spot % 2) * half, 16),
                (spot // 2) * lanes,
                half,
                lanes,
            )
    loads = [
        pltpu.make_async_copy(ref, target.at[index], token_sems.at[slot, index])
        for slot, (refs, target) in enumerate(((normed_refs, tokens), (cot_refs, cots)))
        for index, ref in enumerate(refs)
    ]
    loads.append(pltpu.make_async_copy(down_ref, down_mat, token_sems.at[2, 0]))
    for copy in mats + loads:
        copy.start()
    for copy in mats:
        copy.wait()
    outs = [
        pltpu.make_async_copy(source, target, out_sems.at[index])
        for index, (source, target) in enumerate(
            (
                (gate_mat, gate_mat_out),
                (up_mat, up_mat_out),
                (act, act_out),
                (grad_gate, gate_out),
                (grad_up, up_out),
                (back, back_out),
            )
        )
    ]
    for copy in outs[:2]:
        copy.start()
    for copy in loads:
        copy.wait()

    def token_block(index, carry):
        act[index], grad_gate[index], grad_up[index] = units(
            tokens[index], cots[index], gate_mat[...], up_mat[...], down_mat[...]
        )
        back[index] = (
            nt(grad_gate[index], gate_mat[...]) + nt(grad_up[index], up_mat[...])
        ).astype(BF16)
        return carry

    lax.fori_loop(0, 2, token_block, 0)
    for copy in outs[2:]:
        copy.start()
    for copy in outs:
        copy.wait()


def feed_far_kernel(
    ids_ref, gate_mat_ref, up_mat_ref, down_ref, act_in, gate_in, up_in, *rest, per_shard
):
    hops = 4
    normed_refs, cot_refs = rest[:hops], rest[hops : 2 * hops]
    tiles_out, act_out, gate_out, up_out = rest[2 * hops : 2 * hops + 4]
    gate_mat, up_mat, down_mat, tokens, cots, turned, act, grad_gate, grad_up, tiles = rest[
        2 * hops + 4 : 2 * hops + 14
    ]
    mat_sems, token_sems, cot_sems, unit_sems, out_sems, tile_sems = rest[2 * hops + 14 :]
    width, own = gate_mat.shape
    count = tokens.shape[1]
    places, height, tile = tiles.shape
    rows = height // 3
    mats = [
        pltpu.make_async_copy(source, target, mat_sems.at[index])
        for index, (source, target) in enumerate(
            ((gate_mat_ref, gate_mat), (up_mat_ref, up_mat), (down_ref, down_mat))
        )
    ]
    token_copies = [
        pltpu.make_async_copy(ref, tokens.at[index], token_sems.at[index])
        for index, ref in enumerate(normed_refs)
    ]
    cot_copies = [
        pltpu.make_async_copy(ref, cots.at[pl.ds(index * count, count), :], cot_sems.at[index])
        for index, ref in enumerate(cot_refs)
    ]
    unit_copies = [
        pltpu.make_async_copy(source.at[index], target.at[pl.ds(index * count, count), :],
                              unit_sems.at[slot, index])
        for slot, (source, target) in enumerate(
            ((act_in, act), (gate_in, grad_gate), (up_in, grad_up))
        )
        for index in range(2)
    ]
    for copy in mats + token_copies[2:] + cot_copies[2:]:
        copy.start()
    for copy in token_copies[:2] + cot_copies[:2] + unit_copies:
        copy.start()
    for copy in token_copies[:2]:
        copy.wait()
    for index in range(2):
        turned[:, index * count : (index + 1) * count] = tokens[index].T
    for copy in mats + token_copies[2:] + cot_copies[2:]:
        copy.wait()

    def token_block(index, carry):
        span = pl.ds(pl.multiple_of(index * count, count), count)
        normed = tokens[index]
        act[span, :], grad_gate[span, :], grad_up[span, :] = units(
            normed, cots[span, :], gate_mat[...], up_mat[...], down_mat[...]
        )
        turned[:, span] = normed.T
        return carry

    lax.fori_loop(2, hops, token_block, 0)
    late = pl.ds(2 * count, 2 * count)
    outs = [
        pltpu.make_async_copy(source.at[late, :], target, out_sems.at[index])
        for index, (source, target) in enumerate(
            ((act, act_out), (grad_gate, gate_out), (grad_up, up_out))
        )
    ]
    for copy in outs:
        copy.start()
    for copy in cot_copies[:2] + unit_copies:
        copy.wait()

    def tile_copy(spot, slot):
        low, high = ((0, 2 * rows), (2 * rows, 3 * rows))[slot]
        return pltpu.make_async_copy(
            tiles.at[spot, pl.ds(low, high - low), :],
            tiles_out.at[spot, pl.ds(low, high - low), :],
            tile_sems.at[slot, spot],
        )

    def row_block(index, carry):
        left = turned[pl.ds(pl.multiple_of(index * rows, 16), rows), :]
        spot = lax.rem(index + ids_ref[0], hops) * per_shard
        for slot, ref in ((0, grad_gate), (1, grad_up)):
            grad = nn(left, ref[...])
            for part in range(per_shard):
                tiles[spot + part, slot * rows : (slot + 1) * rows, :] = grad[
                    :, part * tile : (part + 1) * tile
                ].astype(BF16)
        for part in range(per_shard):
            tile_copy(spot + part, 0).start()
        return carry

    lax.fori_loop(0, hops, row_block, 0)
    band = own // places
    turned[:own, :] = act[...].T

    def down_block(index, carry):
        left = turned[pl.ds(pl.multiple_of(index * 2 * band, 16), 2 * band), :]
        grad = nn(left, cots[...])
        for part in range(2):
            for split in range(width // tile):
                start = 2 * rows + split * band
                tiles[2 * index + part, start : start + band, :] = grad[
                    part * band : (part + 1) * band, split * tile : (split + 1) * tile
                ].astype(BF16)
            tile_copy(2 * index + part, 1).start()
        return carry

    lax.fori_loop(0, places // 2, down_block, 0)
    for copy in outs:
        copy.wait()
    for spot in range(places):
        for slot in range(2):
            tile_copy(spot, slot).wait()


def normed_back_kernel(gate_ref, up_ref, gate_mat_ref, up_mat_ref, *outs):
    count = outs[0].shape[0]
    for index, out in enumerate(outs):
        span = slice(index * count, (index + 1) * count)
        out[...] = (
            nt(gate_ref[span, :], gate_mat_ref[...]) + nt(up_ref[span, :], up_mat_ref[...])
        ).astype(BF16)


def widen_kernel(
    ids_ref,
    gate_up_ref,
    down_in_ref,
    mixed_ref,
    gate_ref,
    up_ref,
    down_ref,
    query_ref,
    out_ref,
    stack,
    *,
    rows,
):
    step = pl.program_id(0)
    several, _, tile = gate_up_ref.shape
    band = down_ref.shape[0] // several
    share = mixed_ref.shape[1]
    for part in range(several):
        span = slice(part * tile, (part + 1) * tile)
        gate_ref[:, span] = gate_up_ref[part, :rows, :].astype(F32)
        up_ref[:, span] = gate_up_ref[part, rows:, :].astype(F32)
        for split in range(down_ref.shape[1] // tile):
            down_ref[part * band : (part + 1) * band, split * tile : (split + 1) * tile] = (
                down_in_ref[part, split * band : (split + 1) * band, :].astype(F32)
            )
        start = pl.multiple_of((step * several + part) * share, 8)
        stack[pl.ds(start, share), :] = mixed_ref[part].astype(F32)

    @pl.when(step == pl.num_programs(0) - 1)
    def _():
        cuts = query_ref.shape[1] // tile
        for cut in range(cuts):
            span = slice(cut * tile, (cut + 1) * tile)
            query_ref[:, span] = stack[cut * rows : (cut + 1) * rows, :]
            out_ref[:, span] = stack[(cuts + cut) * rows : (cuts + cut + 1) * rows, :]


def on_device(
    inputs,
    gain_attn,
    w_query,
    w_key,
    w_value,
    w_out,
    gain_mlp,
    w_gate,
    w_up,
    w_down,
    cotangent,
    *,
    n_ctx,
    n_shard,
):
    x = inputs[0]
    cot = cotangent[0]
    count, width = x.shape
    rows, qw = w_query.shape
    kvw = w_key.shape[1]
    ff_own = w_down.shape[0]
    ff = w_gate.shape[1]
    groups = kvw // HEAD
    per = qw // kvw
    blocks = n_ctx
    per_shard = n_ctx // n_shard
    tile = ff_own // per_shard
    assert count == BLOCK and n_shard == 4 and n_ctx % 2 == 0 and ff_own * n_shard == ff
    aligned = tile % LANES == 0
    order = ring_order(n_ctx)
    places = [order.index(index) for index in range(n_ctx)]
    shard = lax.axis_index("shard")
    ctx = lax.axis_index("ctx")

    def after(value, done):
        return lax.optimization_barrier((value, done))[0]

    def hop(value, distance):
        pairs = [(index, index ^ distance) for index in range(n_shard)]
        return lax.ppermute(value, "shard", pairs)

    def ctx_hop(value, distance):
        pairs = [(index, index ^ distance) for index in range(n_ctx)]
        return lax.ppermute(value, "ctx", pairs)

    def gather(value, done):
        far = hop(after(value, done), 2)
        return [value, hop(value, 1), far, hop(far, 1)]

    def halves(parts):
        third = hop(parts[3], 1)
        first = hop(parts[1], 1)
        across = (parts[2].astype(F32) + third.astype(F32)).astype(BF16)
        return parts[0], first, across

    def reduce(parts):
        own, first, across = halves(parts)
        return [own, first, hop(across, 2)]

    def add(parts):
        return sum(part.astype(F32) for part in parts)

    def scatter(value):
        return lax.psum_scatter(
            value, "ctx", scatter_dimension=0, axis_index_groups=[order], tiled=False
        )

    def collect(value):
        return lax.all_gather(value, "ctx", axis=0, axis_index_groups=[order], tiled=True)

    lane = jnp.arange(LANES, dtype=jnp.int32)
    frequency = jnp.exp((lane % (HEAD // 2)).astype(F32) * (-2.0 * math.log(10000.0) / HEAD))
    positions = (ctx * count + jnp.arange(count, dtype=jnp.int32)).astype(F32)
    angles = positions[:, None] * frequency[None, :]
    cosine = jnp.cos(angles)
    sine = jnp.where(lane % HEAD < HEAD // 2, -1.0, 1.0)[None, :] * jnp.sin(angles)

    gains = jnp.concatenate([gain_attn, gain_mlp])
    gain_rows = jnp.zeros((16, 2 * kvw), BF16).at[0, : 2 * rows].set(gains)
    kv_own = jnp.concatenate([jnp.concatenate([w_key, w_value], axis=1), gain_rows], axis=0)
    far = hop(kv_own, 2)
    kv_weights = [kv_own, hop(kv_own, 1), far, hop(far, 1)]
    ids = jnp.stack([shard, ctx]).astype(jnp.int32)
    sizes = (rows,) * n_shard


    half = rows // 2
    lanes = 4 * ff_own // n_ctx
    spot = ring_place(ctx, n_ctx)

    def columns(peer):
        start = peer * ff_own
        return jnp.concatenate(
            [
                lax.dynamic_slice_in_dim(w_gate, start, ff_own, 1),
                lax.dynamic_slice_in_dim(w_up, start, ff_own, 1),
            ],
            axis=1,
        )

    def far_columns(peer):
        column = peer * ff_own + lax.rem(spot // 2 * lanes, ff_own)
        cuts = [
            lax.dynamic_slice(mat, (spot % 2 * half, column), (half, lanes))
            for mat in (w_gate, w_up)
        ]
        return jnp.where(spot // 2 * lanes < ff_own, cuts[0], cuts[1])

    near_columns = columns(shard ^ 1)
    far_cut = jnp.concatenate([far_columns(shard ^ distance) for distance in (2, 3)], axis=0)
    query_own = jnp.concatenate([w_query, far_cut], axis=1)
    cosine, sine, ids, near_columns, query_own = lax.optimization_barrier(
        (cosine, sine, ids, near_columns, query_own)
    )
    query_weights = gather(query_own, far)
    out_far = hop(after(w_out, query_weights[2]), 2)
    fetch_sems = pltpu.SemaphoreType.DMA((n_shard,))
    hidden, kv, gain_one, gain_two = call_once(
        functools.partial(keys_kernel, sizes=sizes, kvw=kvw),
        [((count, width), BF16), ((count, 2 * kvw), BF16), ((1, width), F32), ((1, width), F32)],
        [x, cosine, sine],
        held=[ids],
        moved=kv_weights,
        scratch=[
            pltpu.VMEM((width, 2 * kvw), BF16),
            pltpu.VMEM((n_shard, 16, 2 * kvw), BF16),
            fetch_sems,
            fetch_sems,
        ],
        flops=4 * count * width * kvw,
        limit=ALL_VMEM,
        name="keys",
    )
    all_kv = collect(kv)

    (queries,) = call_once(
        functools.partial(queries_kernel, sizes=sizes),
        [((count, qw), BF16)],
        [hidden, cosine, sine],
        held=[ids],
        moved=query_weights,
        scratch=[pltpu.VMEM((width, qw), BF16), fetch_sems],
        flops=2 * count * width * qw,
        name="queries",
    )
    out_weights = [w_out, hop(w_out, 1), out_far, hop(after(out_far, queries), 1)]
    far_tile = jnp.concatenate(
        [query_weights[2][:half, qw:], query_weights[3][half:, qw:]], axis=0
    )
    far_rows = collect(after(far_tile, kv)[None])
    near_part = hop(near_columns, 1)
    cot_near = hop(cot, 1)
    cot_far = hop(after(cot, (out_weights[2], queries)), 2)

    shared = dict(sizes=sizes, column=0, groups=groups, per=per, blocks=blocks)
    fixed = lambda *shape: pl.BlockSpec(shape, lambda step, table: (0,) * len(shape))
    kv_spec = pl.BlockSpec(
        (count, 2 * kvw), lambda step, table: (ring_place(jnp.minimum(step, table[1]), blocks), 0)
    )
    once = lambda *shape: block(shape)
    weight_specs = [HBM_SPEC] * len(sizes)
    span = per * count
    out_tall, attended, log_total, mid, normed, q_cols = pl.pallas_call(
        functools.partial(attend_kernel, **shared),
        out_shape=(
            jax.ShapeDtypeStruct((qw, count), F32),
            jax.ShapeDtypeStruct((count, qw), BF16),
            jax.ShapeDtypeStruct((8, span), F32),
            jax.ShapeDtypeStruct((count, width), F32),
            jax.ShapeDtypeStruct((count, width), BF16),
            jax.ShapeDtypeStruct((groups, HEAD, span), BF16),
        ),
        grid_spec=pltpu.PrefetchScalarGridSpec(
            num_scalar_prefetch=1,
            grid=(blocks,),
            in_specs=[once(count, qw), kv_spec, once(count, width), once(1, width)]
            + weight_specs,
            out_specs=[
                fixed(qw, count),
                fixed(count, qw),
                fixed(8, span),
                fixed(count, width),
                fixed(count, width),
                fixed(groups, HEAD, span),
            ],
            scratch_shapes=[
                pltpu.VMEM((groups, HEAD, span), F32),
                pltpu.VMEM((8, span), F32),
                pltpu.VMEM((8, span), F32),
                pltpu.VMEM((qw, width), BF16),
                pltpu.VMEM((2, count, span), F32),
                pltpu.VMEM((qw, count), F32),
                pltpu.SemaphoreType.DMA((len(sizes),)),
            ],
        ),
        compiler_params=params(),
        cost_estimate=cost(
            4 * count * count * blocks * qw, 12e6, count * count * blocks * groups * per
        ),
        name="attend",
    )(ids, queries, all_kv, x, gain_two, *out_weights)

    normed_far = hop(normed, 2)
    normed_near = hop(normed, 1)
    cot_far = after(cot_far, normed)
    far_rows = after(far_rows, normed)
    all_count = n_shard * count
    if aligned:
        two = ((2, count, ff_own), BF16)
        mats = [((width, ff_own), BF16)] * 2
        pair = (2, count, width)
        gate_mat, up_mat, *near_units, back = pl.pallas_call(
            functools.partial(feed_near_kernel, half=half, lanes=lanes),
            out_shape=tuple(
                jax.ShapeDtypeStruct(*out) for out in [*mats, two, two, two, (pair, BF16)]
            ),
            in_specs=[SMEM_SPEC] + [HBM_SPEC] * 9,
            out_specs=(HBM_SPEC,) * 6,
            scratch_shapes=[
                pltpu.VMEM((width, ff_own), BF16),
                pltpu.VMEM((width, ff_own), BF16),
                pltpu.VMEM((ff_own, width), BF16),
                pltpu.VMEM(pair, BF16),
                pltpu.VMEM(pair, BF16),
                pltpu.VMEM(*two),
                pltpu.VMEM(*two),
                pltpu.VMEM(*two),
                pltpu.VMEM(pair, BF16),
                pltpu.SemaphoreType.DMA((4 + 2 * n_ctx,)),
                pltpu.SemaphoreType.DMA((3, 2)),
                pltpu.SemaphoreType.DMA((6,)),
            ],
            compiler_params=params(),
            cost_estimate=cost(10 * 2 * count * width * ff_own, 12e6),
            name="feed_near",
        )(
            ids,
            w_gate,
            w_up,
            near_part,
            far_rows,
            w_down,
            normed,
            normed_near,
            cot,
            cot_near,
        )
        normed_far, cot_far = lax.optimization_barrier((normed_far, cot_far, back))[:2]
        normed_pieces = [normed, normed_near, normed_far, hop(normed_far, 1)]
        cot_pieces = [cot, cot_near, cot_far, hop(cot_far, 1)]
        late = ((2 * count, ff_own), BF16)
        feed_tiles, *far_units = pl.pallas_call(
            functools.partial(feed_far_kernel, per_shard=per_shard),
            out_shape=tuple(
                jax.ShapeDtypeStruct(*out)
                for out in [((n_ctx, 3 * rows, tile), BF16), late, late, late]
            ),
            in_specs=[SMEM_SPEC] + [HBM_SPEC] * (6 + 2 * n_shard),
            out_specs=(HBM_SPEC,) * 4,
            scratch_shapes=[
                pltpu.VMEM((width, ff_own), BF16),
                pltpu.VMEM((width, ff_own), BF16),
                pltpu.VMEM((ff_own, width), BF16),
                pltpu.VMEM((n_shard, count, width), BF16),
                pltpu.VMEM((all_count, width), BF16),
                pltpu.VMEM((width, all_count), BF16),
                pltpu.VMEM((all_count, ff_own), BF16),
                pltpu.VMEM((all_count, ff_own), BF16),
                pltpu.VMEM((all_count, ff_own), BF16),
                pltpu.VMEM((n_ctx, 3 * rows, tile), BF16),
                pltpu.SemaphoreType.DMA((3,)),
                pltpu.SemaphoreType.DMA((n_shard,)),
                pltpu.SemaphoreType.DMA((n_shard,)),
                pltpu.SemaphoreType.DMA((3, 2)),
                pltpu.SemaphoreType.DMA((3,)),
                pltpu.SemaphoreType.DMA((2, n_ctx)),
            ],
            compiler_params=params(),
            cost_estimate=cost(9 * all_count * width * ff_own, 25e6),
            name="feed_far",
        )(
            ids, gate_mat, up_mat, w_down, *near_units, *normed_pieces, *cot_pieces
        )
        to_own, to_near = back[0], back[1]
        act_parts = [near_units[0].reshape(2 * count, ff_own), far_units[0]]
        grad_gate_far, grad_up_far = far_units[1:]
    else:
        normed_pieces = [normed, normed_near, normed_far, hop(normed_far, 1)]
        cot_pieces = [cot, cot_near, cot_far, hop(cot_far, 1)]
        tiles_of = far_rows.reshape(n_ctx // 2, 2, 2, half, lanes)
        tiles_of = tiles_of.transpose(2, 1, 3, 0, 4).reshape(2, rows, 2 * ff_own)
        gate_mat = jnp.zeros((width, ff_own), BF16)
        up_mat = jnp.zeros((width, ff_own), BF16)
        for part, start in zip(
            (columns(shard), near_part, tiles_of[0], tiles_of[1]),
            [(shard ^ k) * rows for k in range(n_shard)],
        ):
            gate_mat = lax.dynamic_update_slice_in_dim(gate_mat, part[:, :ff_own], start, 0)
            up_mat = lax.dynamic_update_slice_in_dim(up_mat, part[:, ff_own:], start, 0)
        all_cot = jnp.concatenate(cot_pieces, axis=0)
        all_normed = jnp.concatenate(normed_pieces, axis=0)
        gate = nn(all_normed, gate_mat)
        up = nn(all_normed, up_mat)
        grad_activated = nt(all_cot, w_down)
        sigmoid = jax.nn.sigmoid(gate)
        activated = (gate * sigmoid * up).astype(BF16)
        grad_gate = (grad_activated * up * (sigmoid * (1.0 + gate * (1.0 - sigmoid)))).astype(BF16)
        grad_up = (grad_activated * (gate * sigmoid)).astype(BF16)

        def tiles(grad):
            pieces = grad.astype(BF16).reshape(n_shard, rows, per_shard, tile)
            pieces = pieces.transpose(0, 2, 1, 3)
            return jnp.roll(pieces, shard, axis=0).reshape(n_ctx, rows, tile)

        down = tn(activated, all_cot).astype(BF16)
        down = down.reshape(n_ctx, ff_own // n_ctx, width // tile, tile).transpose(0, 2, 1, 3)
        feed_tiles = jnp.concatenate(
            [
                tiles(tn(all_normed, grad_gate)),
                tiles(tn(all_normed, grad_up)),
                down.reshape(n_ctx, rows, tile),
            ],
            axis=1,
        )
        grad_gate_far, grad_up_far = grad_gate[2 * count :], grad_up[2 * count :]
        back = nt(grad_gate[: 2 * count], gate_mat) + nt(grad_up[: 2 * count], up_mat)
        to_own, to_near = back[:count].astype(BF16), back[count:].astype(BF16)
        act_parts = [activated[: 2 * count], activated[2 * count :]]
    from_near = hop(to_near, 1)
    feed_sum = scatter(feed_tiles)
    head_sum = feed_sum[2 * rows : 2 * rows + 16]
    pairs = []
    for index in range(n_ctx):
        for source in range(n_shard):
            target = (places[index] // per_shard - source) % n_shard
            pairs.append((index * n_shard + source, index * n_shard + target))
    gate_up_sum = lax.ppermute(feed_sum[: 2 * rows], ("ctx", "shard"), pairs)

    to_far, to_third = call_once(
        normed_back_kernel,
        [((count, width), BF16)] * 2,
        [grad_gate_far, grad_up_far, gate_mat, up_mat],
        flops=8 * count * width * ff_own,
        limit=ALL_VMEM,
        name="normed_back",
    )
    third = hop(to_third, 1)
    across = (to_far.astype(F32) + third.astype(F32)).astype(BF16)
    from_far = hop(across, 2)

    part_out = [after(nn(part, w_down).astype(BF16), from_far) for part in act_parts]
    part_out = [part[k * count : (k + 1) * count] for part in part_out for k in range(2)]
    output = (mid + add(reduce(part_out))).astype(BF16)[None]

    place_spec = pl.BlockSpec(
        (count, 2 * kvw), lambda step, table: (ring_place(step, blocks), 0)
    )
    grad_query, grad_kv, branch, grad_mid, gain_two_part = pl.pallas_call(
        functools.partial(attend_back_kernel, **shared),
        out_shape=(
            jax.ShapeDtypeStruct((count, qw), BF16),
            jax.ShapeDtypeStruct((blocks * count, 2 * kvw), BF16),
            jax.ShapeDtypeStruct((count, width), BF16),
            jax.ShapeDtypeStruct((count, width), F32),
            jax.ShapeDtypeStruct((1, width), F32),
        ),
        grid_spec=pltpu.PrefetchScalarGridSpec(
            num_scalar_prefetch=1,
            grid=(blocks,),
            in_specs=[
                kv_spec,
                once(groups, HEAD, span),
                once(qw, count),
                once(8, span),
                once(count, width),
                once(1, width),
                once(count, width),
                once(count, width),
                once(count, width),
                once(count, width),
                once(count, LANES),
                once(count, LANES),
            ]
            + weight_specs,
            out_specs=[
                fixed(count, qw),
                place_spec,
                fixed(count, width),
                fixed(count, width),
                fixed(1, width),
            ],
            scratch_shapes=[
                pltpu.VMEM((qw, width), BF16),
                pltpu.VMEM((groups, HEAD, span), BF16),
                pltpu.VMEM((8, span), F32),
                pltpu.VMEM((groups, HEAD, span), F32),
                pltpu.VMEM((2, 2, count, span), F32),
                pltpu.VMEM((qw, count), F32),
                pltpu.SemaphoreType.DMA((len(sizes),)),
            ],
        ),
        compiler_params=params(),
        cost_estimate=cost(
            10 * count * count * blocks * qw, 14e6, count * count * blocks * groups * per
        ),
        name="attend_back",
    )(
        ids,
        all_kv,
        q_cols,
        out_tall,
        log_total,
        mid,
        gain_two,
        cot,
        to_own,
        from_near,
        from_far,
        cosine,
        sine,
        *out_weights,
    )
    grad_kv, head_sum = lax.optimization_barrier((grad_kv, head_sum))
    own_kv = scatter(grad_kv.reshape(n_ctx, count, 2 * kvw))

    def stack(parts, breadth, name):
        height = sum(part.shape[0] * part.shape[1] for part in parts[::3]) // breadth
        if breadth % LANES:
            wide = jnp.concatenate(
                [add(parts[index : index + 3]) for index in range(0, len(parts), 3)], axis=1
            )
            wide = wide.astype(BF16).reshape(rows, -1, breadth)
            return wide.transpose(1, 0, 2).reshape(height, breadth)
        return call_once(stack_kernel, [((height, breadth), BF16)], parts, flops=1e6, name=name)[0]

    grad_blocks = call_once(
        weight_grads_kernel,
        [((rows, qw), BF16)] * n_shard + [((rows, width), BF16)] * n_shard,
        [hidden, grad_query, attended, branch],
        held=[ids],
        scratch=[pltpu.VMEM((width, qw), F32)],
        flops=4 * count * width * qw,
        limit=ALL_VMEM,
        name="weight_grads",
    )
    parts_query = reduce(grad_blocks[:n_shard])
    parts_out = reduce(grad_blocks[n_shard:])
    mixed = stack(parts_query + parts_out, tile, "stack_mixed")
    mixed_sum = scatter(after(mixed, own_kv).reshape(n_ctx, -1, tile))

    grad_kv_pre, *kv_blocks = call_once(
        functools.partial(kv_back_kernel, kvw=kvw),
        [((count, 2 * kvw), BF16)] + [((rows, 2 * kvw), BF16)] * n_shard,
        [own_kv, cosine, sine, hidden],
        held=[ids],
        scratch=[pltpu.VMEM((width, 2 * kvw), F32)],
        flops=4 * count * width * kvw,
        name="kv_back",
    )
    sum_kv = stack(reduce(kv_blocks), LANES, "stack_kv").reshape(n_ctx, -1, LANES)
    shares = jnp.concatenate(
        [gate_up_sum, head_sum, feed_sum[2 * rows + 16 :], jnp.zeros_like(mixed_sum)]
    )
    shares = lax.dynamic_update_slice_in_dim(after(shares, sum_kv), mixed_sum, 3 * rows, 0)
    gathered = collect(shares[None])

    def exchange(value):
        return lax.all_to_all(value, "ctx", split_axis=0, concat_axis=0, tiled=True)

    own_sum = jnp.sum(exchange(sum_kv).astype(F32), axis=0, keepdims=True).astype(BF16)
    both = exchange(jnp.broadcast_to(own_sum, sum_kv.shape))
    both = both.reshape(2 * kvw // LANES, rows, LANES).transpose(1, 0, 2).reshape(rows, 2 * kvw)
    grad_w_key = both[:, :kvw].astype(F32)
    grad_w_value = both[:, kvw:].astype(F32)

    grad_x, gain_one_part = call_once(
        functools.partial(inputs_kernel, sizes=sizes),
        [((count, width), BF16), ((1, width), F32)],
        [grad_query, grad_kv_pre, x, gain_one, grad_mid],
        held=[ids],
        moved=[*query_weights, *kv_weights],
        scratch=[
            pltpu.VMEM((width, qw), BF16),
            pltpu.VMEM((width, 2 * kvw), BF16),
            pltpu.VMEM((count, width), F32),
            fetch_sems,
            fetch_sems,
        ],
        flops=2 * count * width * (qw + 2 * kvw),
        name="grad_inputs",
    )

    gain_parts = jnp.concatenate([gain_one_part, gain_two_part], axis=0)
    for distance in [1 << bit for bit in range(n_shard.bit_length() - 1)]:
        gain_parts = gain_parts + hop(gain_parts, distance)
    for distance in [1 << bit for bit in range(n_ctx.bit_length() - 1)]:
        gain_parts = gain_parts + ctx_hop(gain_parts, distance)
    own_gains = lax.dynamic_slice_in_dim(gain_parts, shard * rows, rows, 1)

    if aligned:
        share = mixed_sum.shape[0]
        rolled = lambda step, where: (lax.rem(step + where[0], n_shard), 0, 0)
        band = ff_own // n_ctx
        grad_w_gate, grad_w_up, grad_w_down, grad_w_query, grad_w_out = pl.pallas_call(
            functools.partial(widen_kernel, rows=rows),
            out_shape=(
                jax.ShapeDtypeStruct((rows, ff), F32),
                jax.ShapeDtypeStruct((rows, ff), F32),
                jax.ShapeDtypeStruct((ff_own, width), F32),
                jax.ShapeDtypeStruct((rows, qw), F32),
                jax.ShapeDtypeStruct((rows, width), F32),
            ),
            grid_spec=pltpu.PrefetchScalarGridSpec(
                num_scalar_prefetch=1,
                grid=(n_shard,),
                in_specs=[
                    pl.BlockSpec((per_shard, 2 * rows, tile), rolled),
                    pl.BlockSpec((per_shard, rows, tile), lambda step, where: (step, 2, 0)),
                    pl.BlockSpec(
                        (per_shard, share, tile),
                        lambda step, where: (step, 3 * rows // share, 0),
                    ),
                ],
                out_specs=[
                    pl.BlockSpec((rows, ff_own), lambda step, where: (0, step)),
                    pl.BlockSpec((rows, ff_own), lambda step, where: (0, step)),
                    pl.BlockSpec((per_shard * band, width), lambda step, where: (step, 0)),
                    pl.BlockSpec((rows, qw), lambda step, where: (0, 0)),
                    pl.BlockSpec((rows, width), lambda step, where: (0, 0)),
                ],
                scratch_shapes=[pltpu.VMEM((n_ctx * share, tile), F32)],
            ),
            compiler_params=params(),
            cost_estimate=cost(1e6, 20e6),
            name="widen",
        )(ids, gathered, gathered, gathered)
    else:

        def untile(part):
            back = jnp.roll(part.reshape(n_shard, per_shard, rows, tile), -shard, axis=0)
            back = back.reshape(n_ctx, rows, tile).transpose(1, 0, 2)
            return back.reshape(rows, ff).astype(F32)

        grad_w_gate = untile(gathered[:, :rows])
        grad_w_up = untile(gathered[:, rows : 2 * rows])
        down = gathered[:, 2 * rows : 3 * rows].reshape(n_ctx, width // tile, -1, tile)
        grad_w_down = down.transpose(0, 2, 1, 3).reshape(ff_own, width).astype(F32)
        wide = gathered[:, 3 * rows :].reshape(2 * qw // tile, rows, tile).transpose(1, 0, 2)
        wide = wide.reshape(rows, 2 * qw).astype(F32)
        grad_w_query, grad_w_out = wide[:, :qw], wide[:, qw:]

    return (
        output,
        grad_x[None],
        own_gains[0],
        grad_w_query,
        grad_w_key,
        grad_w_value,
        grad_w_out,
        own_gains[1],
        grad_w_gate,
        grad_w_up,
        grad_w_down,
    )


def solution(mesh):
    tokens = P("shard", "ctx", None)
    split = P("shard", None)
    gain = P("shard")
    placed = (tokens, gain, split, split, split, split, gain, split, split, split, tokens)
    return jax.shard_map(
        functools.partial(on_device, n_ctx=mesh.shape["ctx"], n_shard=mesh.shape["shard"]),
        mesh=mesh,
        in_specs=placed,
        out_specs=(tokens, tokens, gain, split, split, split, split, gain, split, split, split),
        check_vma=False,
    )
```

```python
import functools
import math

import jax
import jax.numpy as jnp
from jax import lax
from jax.experimental import pallas as pl
from jax.experimental.pallas import tpu as pltpu
from jax.sharding import PartitionSpec as P

HEAD = 64
BLOCK = 256
EPSILON = 1e-05
LANES = 128
F32 = jnp.float32
BF16 = jnp.bfloat16
SCORE_SCALE = math.log2(math.e) * 0.125
NEGATIVE = -1e30
ALL_VMEM = 60 * 1024 * 1024
PART_VMEM = 32 * 1024 * 1024


def nn(left, right):
    return lax.dot_general(left, right, (((1,), (0,)), ((), ())), preferred_element_type=F32)


def nt(left, right):
    return lax.dot_general(left, right, (((1,), (1,)), ((), ())), preferred_element_type=F32)


def tn(left, right):
    return lax.dot_general(left, right, (((0,), (0,)), ((), ())), preferred_element_type=F32)


def ring_order(count):
    return list(range(0, count, 2)) + list(range(count - 1, 0, -2))


def ring_place(index, count):
    return jnp.where(index % 2 == 0, index // 2, count - 1 - index // 2)


def params(limit=ALL_VMEM):
    return pltpu.CompilerParams(vmem_limit_bytes=limit)


def cost(flops, moved, exps=0):
    return pl.CostEstimate(flops=int(flops), bytes_accessed=int(moved), transcendentals=int(exps))


HBM_SPEC = pl.BlockSpec(memory_space=pltpu.HBM)
SMEM_SPEC = pl.BlockSpec(memory_space=pltpu.SMEM)


def block(shape):
    return pl.BlockSpec(shape, lambda *_: (0,) * len(shape), pipeline_mode=pl.Buffered(1))


def call_once(
    kernel, outs, ins, held=(), moved=(), scratch=(), flops=0, limit=PART_VMEM, name=None
):
    return pl.pallas_call(
        kernel,
        out_shape=tuple(jax.ShapeDtypeStruct(shape, dtype) for shape, dtype in outs),
        grid=(1,),
        in_specs=[SMEM_SPEC] * len(held)
        + [block(array.shape) for array in ins]
        + [HBM_SPEC] * len(moved),
        out_specs=tuple(pl.BlockSpec(shape, lambda *_: (0,) * len(shape)) for shape, _ in outs),
        scratch_shapes=list(scratch),
        compiler_params=params(limit),
        cost_estimate=cost(flops, sum(2 * math.prod(shape) for shape, _ in outs) + 4e6),
        name=name,
    )(*held, *ins, *moved)


def swap_halves(tile):
    lane = lax.broadcasted_iota(jnp.int32, tile.shape, 1)
    ahead = pltpu.roll(tile, LANES - HEAD // 2, 1)
    behind = pltpu.roll(tile, HEAD // 2, 1)
    return jnp.where(lane % HEAD < HEAD // 2, ahead, behind)


def row_start(ids_ref, hop, rows):
    return pl.multiple_of((ids_ref[0] ^ hop) * rows, 16)


def fetches(ids_ref, pieces, whole, sems, sizes, column=0):
    copies = []
    for index, (piece, size) in enumerate(zip(pieces, sizes)):
        start = row_start(ids_ref, index, size)
        copies.append(
            pltpu.make_async_copy(
                piece.at[pl.ds(0, size), pl.ds(column, whole.shape[1])],
                whole.at[pl.ds(start, size), :],
                sems.at[index],
            )
        )
    return copies


def keys_kernel(ids_ref, x_ref, cos_ref, sin_ref, *rest, sizes, kvw):
    pieces = rest[: len(sizes)]
    hidden_ref, kv_ref, one_ref, two_ref, whole, bands, sems, band_sems = rest[len(sizes) :]
    copies = fetches(ids_ref, pieces, whole, sems, sizes)
    rows = sizes[0]
    for index, piece in enumerate(pieces):
        band = pltpu.make_async_copy(
            piece.at[pl.ds(rows, 16), :], bands.at[index], band_sems.at[index]
        )
        band.start()
        copies[index].start()
    x = x_ref[...].astype(F32)
    scale = lax.rsqrt(jnp.mean(x * x, axis=-1, keepdims=True) + EPSILON)
    width = x.shape[1]
    ones = jnp.zeros((8, width), F32)
    twos = jnp.zeros((8, width), F32)
    for index, piece in enumerate(pieces):
        pltpu.make_async_copy(
            piece.at[pl.ds(rows, 16), :], bands.at[index], band_sems.at[index]
        ).wait()
        band = bands[index].astype(F32)[:8, :]
        blank = jnp.zeros((8, width - rows), F32)
        first = jnp.concatenate([band[:, :rows], blank], axis=1)
        second = jnp.concatenate([band[:, rows : 2 * rows], blank], axis=1)
        ones = ones + pltpu.roll(first, (ids_ref[0] ^ index) * rows, 1)
        twos = twos + pltpu.roll(second, (ids_ref[0] ^ index) * rows, 1)
    one_ref[...] = ones[:1, :]
    two_ref[...] = twos[:1, :]
    hidden = (x * scale * ones[:1, :]).astype(BF16)
    hidden_ref[...] = hidden
    for copy in copies:
        copy.wait()
    pre = nn(hidden, whole[...])
    for start in range(0, kvw, LANES):
        tile = pre[:, start : start + LANES]
        turned = tile * cos_ref[...] + swap_halves(tile) * sin_ref[...]
        kv_ref[:, start : start + LANES] = turned.astype(BF16)
    kv_ref[:, kvw:] = pre[:, kvw:].astype(BF16)


def queries_kernel(ids_ref, hidden_ref, cos_ref, sin_ref, *rest, sizes):
    pieces = rest[: len(sizes)]
    query_ref, whole, sems = rest[len(sizes) :]
    copies = fetches(ids_ref, pieces, whole, sems, sizes)
    for copy in copies:
        copy.start()
    for copy in copies:
        copy.wait()
    pre = nn(hidden_ref[...], whole[...])
    for start in range(0, pre.shape[1], LANES):
        tile = pre[:, start : start + LANES]
        turned = tile * cos_ref[...] + swap_halves(tile) * sin_ref[...]
        query_ref[:, start : start + LANES] = turned.astype(BF16)


def attend_kernel(
    table_ref,
    q_ref,
    kv_ref,
    x_ref,
    gain_ref,
    *rest,
    sizes,
    column,
    groups,
    per,
    blocks,
):
    pieces = rest[:-13]
    (
        out_ref,
        attended_ref,
        log_ref,
        mid_ref,
        normed_ref,
        cols_ref,
        acc,
        top,
        total,
        whole,
        scores,
        tall,
        sems,
    ) = rest[-13:]
    step = pl.program_id(0)
    last = table_ref[1]
    count = q_ref.shape[0]
    kvw = groups * HEAD

    @pl.when(step == 0)
    def _():
        for copy in fetches(table_ref, pieces, whole, sems, sizes, column):
            copy.start()
        turned = q_ref[...].T
        for group in range(groups):
            for member in range(per):
                head = group * per + member
                cols_ref[group, :, member * count : (member + 1) * count] = turned[
                    head * HEAD : (head + 1) * HEAD, :
                ]
        acc[...] = jnp.zeros_like(acc)
        total[...] = jnp.zeros_like(total)
        top[...] = jnp.full_like(top, NEGATIVE)

    @pl.when(step <= last)
    def _():
        def score(group):
            key = kv_ref[:, group * HEAD : (group + 1) * HEAD]
            scores[group % 2] = nn(key, cols_ref[group])

        score(0)
        for group in range(groups):
            if group + 1 < groups:
                score(group + 1)
            value = kv_ref[:, kvw + group * HEAD : kvw + (group + 1) * HEAD]
            raw = scores[group % 2]
            old = top[group : group + 1, :]
            new = jnp.maximum(old, jnp.max(raw, axis=0, keepdims=True))
            shrink = jnp.exp2((old - new) * SCORE_SCALE)
            probs = jnp.exp2((raw - new) * SCORE_SCALE)
            top[group : group + 1, :] = new
            total[group : group + 1, :] = total[group : group + 1, :] * shrink + jnp.sum(
                probs, axis=0, keepdims=True
            )
            acc[group] = acc[group] * shrink + tn(value, probs.astype(BF16))

    @pl.when(step == blocks - 1)
    def _():
        for group in range(groups):
            sums = total[group : group + 1, :]
            log_ref[group : group + 1, :] = top[
                group : group + 1, :
            ] * SCORE_SCALE + jnp.log2(sums)
            rowed = acc[group] / sums
            for member in range(per):
                head = group * per + member
                tall[head * HEAD : (head + 1) * HEAD, :] = rowed[
                    :, member * count : (member + 1) * count
                ]
        out_ref[...] = tall[...]
        attended = tall[...].astype(BF16).T
        attended_ref[...] = attended
        for copy in fetches(table_ref, pieces, whole, sems, sizes, column):
            copy.wait()
        mid = x_ref[...].astype(F32) + nn(attended, whole[...])
        mid_ref[...] = mid
        scale = lax.rsqrt(jnp.mean(mid * mid, axis=-1, keepdims=True) + EPSILON)
        normed_ref[...] = (mid * scale * gain_ref[...]).astype(BF16)


def attend_back_kernel(
    table_ref,
    kv_ref,
    cols_ref,
    out_ref,
    log_ref,
    mid_ref,
    gain_ref,
    cot_ref,
    gn_own_ref,
    gn_near_ref,
    gn_far_ref,
    cos_ref,
    sin_ref,
    *rest,
    sizes,
    column,
    groups,
    per,
    blocks,
):
    pieces = rest[: len(sizes)]
    (
        gq_ref,
        gkv_ref,
        branch_ref,
        gmid_ref,
        ggain_ref,
        whole,
        d_cols,
        delta,
        acc,
        probs_all,
        tall,
        sems,
    ) = rest[len(sizes) :]
    step = pl.program_id(0)
    last = table_ref[1]
    count = kv_ref.shape[0]
    kvw = groups * HEAD

    @pl.when(step == 0)
    def _():
        copies = fetches(table_ref, pieces, whole, sems, sizes, column)
        for copy in copies:
            copy.start()
        mid = mid_ref[...]
        incoming = (
            gn_own_ref[...].astype(F32) + gn_near_ref[...].astype(F32)
        ) + gn_far_ref[...].astype(F32)
        gain = gain_ref[...]
        scale = lax.rsqrt(jnp.mean(mid * mid, axis=-1, keepdims=True) + EPSILON)
        weighted = incoming * gain
        inner = jnp.mean(weighted * mid, axis=-1, keepdims=True)
        ggain_ref[...] = jnp.sum(incoming * mid * scale, axis=0, keepdims=True)
        grad_mid = (
            cot_ref[...].astype(F32) + scale * weighted - mid * (scale * scale * scale * inner)
        )
        gmid_ref[...] = grad_mid
        branch = grad_mid.astype(BF16)
        branch_ref[...] = branch
        for copy in copies:
            copy.wait()
        grads = nt(branch, whole[...]).astype(BF16)
        turned = grads.T
        tall[...] = turned.astype(F32) * out_ref[...]
        for group in range(groups):
            for member in range(per):
                head = group * per + member
                span = slice(head * HEAD, (head + 1) * HEAD)
                cols = slice(member * count, (member + 1) * count)
                d_cols[group, :, cols] = turned[span, :]
                delta[group : group + 1, cols] = jnp.sum(tall[span, :], axis=0, keepdims=True)
        acc[...] = jnp.zeros_like(acc)

    @pl.when(step > last)
    def _():
        gkv_ref[...] = jnp.zeros_like(gkv_ref)

    @pl.when(step <= last)
    def _():
        def spans(group):
            return (
                slice(group * HEAD, (group + 1) * HEAD),
                slice(kvw + group * HEAD, kvw + (group + 1) * HEAD),
            )

        def score(group):
            key_span, value_span = spans(group)
            probs_all[group % 2, 0] = nn(kv_ref[:, key_span], cols_ref[group])
            probs_all[group % 2, 1] = nn(kv_ref[:, value_span], d_cols[group])

        score(0)
        for group in range(groups):
            if group + 1 < groups:
                score(group + 1)
            key_span, value_span = spans(group)
            probs = jnp.exp2(
                probs_all[group % 2, 0] * SCORE_SCALE - log_ref[group : group + 1, :]
            )
            grad_scores = (
                probs * (probs_all[group % 2, 1] - delta[group : group + 1, :])
            ).astype(BF16)
            gkv_ref[:, value_span] = nt(probs.astype(BF16), d_cols[group]).astype(BF16)
            gkv_ref[:, key_span] = (nt(grad_scores, cols_ref[group]) * 0.125).astype(BF16)
            acc[group] = acc[group] + tn(kv_ref[:, key_span], grad_scores)

    @pl.when(step == blocks - 1)
    def _():
        for group in range(groups):
            for member in range(per):
                head = group * per + member
                tall[head * HEAD : (head + 1) * HEAD, :] = (
                    acc[group, :, member * count : (member + 1) * count] * 0.125
                )
        for start in range(0, tall.shape[0], LANES):
            tile = tall[start : start + LANES, :].T
            turned = tile * cos_ref[...] - swap_halves(tile) * sin_ref[...]
            gq_ref[:, start : start + LANES] = turned.astype(BF16)


def columns_in_turn(left, right, full):
    breadth = full.shape[1] // 3

    def third(index, carry):
        span = pl.ds(pl.multiple_of(index * breadth, LANES), breadth)
        full[:, span] = tn(left[...], right[:, span])
        return carry

    lax.fori_loop(0, 3, third, 0)


def kv_back_kernel(ids_ref, grad_ref, cos_ref, sin_ref, hidden_ref, out_ref, *rest, kvw):
    outs, full = rest[:-1], rest[-1]
    for start in range(0, kvw, LANES):
        tile = grad_ref[:, start : start + LANES].astype(F32)
        turned = tile * cos_ref[...] - swap_halves(tile) * sin_ref[...]
        out_ref[:, start : start + LANES] = turned.astype(BF16)
    out_ref[:, kvw:] = grad_ref[:, kvw:]
    columns_in_turn(hidden_ref, out_ref, full)
    for index, out in enumerate(outs):
        start = row_start(ids_ref, index, out.shape[0])
        out[...] = full[pl.ds(start, out.shape[0]), :].astype(BF16)


def stack_kernel(*refs):
    parts, out_ref = refs[:-1], refs[-1]
    tile = out_ref.shape[1]
    row = 0
    for index in range(0, len(parts), 3):
        first, second, third = parts[index : index + 3]
        rows, columns = first.shape
        for start in range(0, columns, tile):
            span = slice(start, start + tile)
            total = (
                first[:, span].astype(F32) + second[:, span].astype(F32)
            ) + third[:, span].astype(F32)
            out_ref[row : row + rows, :] = total.astype(BF16)
            row += rows


def inputs_kernel(ids_ref, gq_ref, gkv_ref, x_ref, gain_ref, gmid_ref, *rest, sizes):
    hops = len(sizes)
    grad_ref, ggain_ref, whole_q, whole_kv, arriving, q_sems, kv_sems = rest[2 * hops :]
    copies = fetches(ids_ref, rest[:hops], whole_q, q_sems, sizes)
    copies += fetches(ids_ref, rest[hops : 2 * hops], whole_kv, kv_sems, sizes)
    for copy in copies:
        copy.start()
    for copy in copies:
        copy.wait()
    breadth = arriving.shape[1] // 3

    def third(index, carry):
        span = pl.ds(pl.multiple_of(index * breadth, LANES), breadth)
        arriving[:, span] = nt(gq_ref[...], whole_q[span, :]) + nt(gkv_ref[...], whole_kv[span, :])
        return carry

    lax.fori_loop(0, 3, third, 0)
    incoming = arriving[...]
    x = x_ref[...].astype(F32)
    scale = lax.rsqrt(jnp.mean(x * x, axis=-1, keepdims=True) + EPSILON)
    weighted = incoming * gain_ref[...]
    inner = jnp.mean(weighted * x, axis=-1, keepdims=True)
    ggain_ref[...] = jnp.sum(incoming * x * scale, axis=0, keepdims=True)
    grad = gmid_ref[...] + scale * weighted - x * (scale * scale * scale * inner)
    grad_ref[...] = grad.astype(BF16)


def weight_grads_kernel(ids_ref, hidden_ref, query_ref, attended_ref, branch_ref, *rest):
    outs, full = rest[:-1], rest[-1]
    hops = len(outs) // 2
    for index, (left, right) in enumerate(((hidden_ref, query_ref), (attended_ref, branch_ref))):
        full[...] = tn(left[...], right[...])
        for hop, out in enumerate(outs[index * hops : (index + 1) * hops]):
            start = row_start(ids_ref, hop, out.shape[0])
            out[...] = full[pl.ds(start, out.shape[0]), :].astype(BF16)


def units(normed, cot, gate_mat, up_mat, down_mat):
    gate = nn(normed, gate_mat)
    up = nn(normed, up_mat)
    grad = nt(cot, down_mat)
    sigmoid = 1.0 / (1.0 + jnp.exp(-gate))
    silu = gate * sigmoid
    return (
        (silu * up).astype(BF16),
        (grad * up * (sigmoid * (1.0 + gate * (1.0 - sigmoid)))).astype(BF16),
        (grad * silu).astype(BF16),
    )


def feed_near_kernel(
    ids_ref, own_gate_ref, own_up_ref, near_ref, far_ref, down_ref, *rest, half, lanes
):
    normed_refs, cot_refs = rest[:2], rest[2:4]
    gate_mat_out, up_mat_out, act_out, gate_out, up_out, back_out = rest[4:10]
    gate_mat, up_mat, down_mat, tokens, cots, act, grad_gate, grad_up, back = rest[10:19]
    mat_sems, token_sems, out_sems = rest[19:]
    rows = near_ref.shape[0]
    own = gate_mat.shape[1]
    mats = []

    def place(source, row, column, height, breadth):
        target = gate_mat if column < own else up_mat
        mats.append(
            pltpu.make_async_copy(
                source,
                target.at[pl.ds(row, height), pl.ds(column % own, breadth)],
                mat_sems.at[len(mats)],
            )
        )

    mine = pl.ds(pl.multiple_of(ids_ref[0] * own, LANES), own)
    for index, ref in enumerate((own_gate_ref, own_up_ref)):
        place(ref.at[:, mine], row_start(ids_ref, 0, rows), index * own, rows, own)
        place(
            near_ref.at[:, pl.ds(index * own, own)],
            row_start(ids_ref, 1, rows),
            index * own,
            rows,
            own,
        )
    for spot in range(far_ref.shape[0]):
        for index in range(2):
            place(
                far_ref.at[spot, pl.ds(index * half, half), :],
                pl.multiple_of(row_start(ids_ref, 2 + index, rows) + (spot % 2) * half, 16),
                (spot // 2) * lanes,
                half,
                lanes,
            )
    loads = [
        pltpu.make_async_copy(ref, target.at[index], token_sems.at[slot, index])
        for slot, (refs, target) in enumerate(((normed_refs, tokens), (cot_refs, cots)))
        for index, ref in enumerate(refs)
    ]
    loads.append(pltpu.make_async_copy(down_ref, down_mat, token_sems.at[2, 0]))
    for copy in mats + loads:
        copy.start()
    for copy in mats:
        copy.wait()
    outs = [
        pltpu.make_async_copy(source, target, out_sems.at[index])
        for index, (source, target) in enumerate(
            (
                (gate_mat, gate_mat_out),
                (up_mat, up_mat_out),
                (act, act_out),
                (grad_gate, gate_out),
                (grad_up, up_out),
                (back, back_out),
            )
        )
    ]
    for copy in outs[:2]:
        copy.start()
    for copy in loads:
        copy.wait()

    def token_block(index, carry):
        act[index], grad_gate[index], grad_up[index] = units(
            tokens[index], cots[index], gate_mat[...], up_mat[...], down_mat[...]
        )
        back[index] = (
            nt(grad_gate[index], gate_mat[...]) + nt(grad_up[index], up_mat[...])
        ).astype(BF16)
        return carry

    lax.fori_loop(0, 2, token_block, 0)
    for copy in outs[2:]:
        copy.start()
    for copy in outs:
        copy.wait()


def feed_far_kernel(
    ids_ref, gate_mat_ref, up_mat_ref, down_ref, act_in, gate_in, up_in, *rest, per_shard
):
    hops = 4
    normed_refs, cot_refs = rest[:hops], rest[hops : 2 * hops]
    tiles_out, act_out, gate_out, up_out = rest[2 * hops : 2 * hops + 4]
    gate_mat, up_mat, down_mat, tokens, cots, turned, act, grad_gate, grad_up, tiles = rest[
        2 * hops + 4 : 2 * hops + 14
    ]
    mat_sems, token_sems, cot_sems, unit_sems, out_sems, tile_sems = rest[2 * hops + 14 :]
    width, own = gate_mat.shape
    count = tokens.shape[1]
    places, height, tile = tiles.shape
    rows = height // 3
    mats = [
        pltpu.make_async_copy(source, target, mat_sems.at[index])
        for index, (source, target) in enumerate(
            ((gate_mat_ref, gate_mat), (up_mat_ref, up_mat), (down_ref, down_mat))
        )
    ]
    token_copies = [
        pltpu.make_async_copy(ref, tokens.at[index], token_sems.at[index])
        for index, ref in enumerate(normed_refs)
    ]
    cot_copies = [
        pltpu.make_async_copy(ref, cots.at[pl.ds(index * count, count), :], cot_sems.at[index])
        for index, ref in enumerate(cot_refs)
    ]
    unit_copies = [
        pltpu.make_async_copy(source.at[index], target.at[pl.ds(index * count, count), :],
                              unit_sems.at[slot, index])
        for slot, (source, target) in enumerate(
            ((act_in, act), (gate_in, grad_gate), (up_in, grad_up))
        )
        for index in range(2)
    ]
    for copy in mats + token_copies[2:] + cot_copies[2:]:
        copy.start()
    for copy in token_copies[:2] + cot_copies[:2] + unit_copies:
        copy.start()
    for copy in token_copies[:2]:
        copy.wait()
    for index in range(2):
        turned[:, index * count : (index + 1) * count] = tokens[index].T
    for copy in mats + token_copies[2:] + cot_copies[2:]:
        copy.wait()

    def token_block(index, carry):
        span = pl.ds(pl.multiple_of(index * count, count), count)
        normed = tokens[index]
        act[span, :], grad_gate[span, :], grad_up[span, :] = units(
            normed, cots[span, :], gate_mat[...], up_mat[...], down_mat[...]
        )
        turned[:, span] = normed.T
        return carry

    lax.fori_loop(2, hops, token_block, 0)
    late = pl.ds(2 * count, 2 * count)
    outs = [
        pltpu.make_async_copy(source.at[late, :], target, out_sems.at[index])
        for index, (source, target) in enumerate(
            ((act, act_out), (grad_gate, gate_out), (grad_up, up_out))
        )
    ]
    for copy in outs:
        copy.start()
    for copy in cot_copies[:2] + unit_copies:
        copy.wait()

    def tile_copy(spot, slot):
        low, high = ((0, 2 * rows), (2 * rows, 3 * rows))[slot]
        return pltpu.make_async_copy(
            tiles.at[spot, pl.ds(low, high - low), :],
            tiles_out.at[spot, pl.ds(low, high - low), :],
            tile_sems.at[slot, spot],
        )

    def row_block(index, carry):
        left = turned[pl.ds(pl.multiple_of(index * rows, 16), rows), :]
        spot = lax.rem(index + ids_ref[0], hops) * per_shard
        for slot, ref in ((0, grad_gate), (1, grad_up)):
            grad = nn(left, ref[...])
            for part in range(per_shard):
                tiles[spot + part, slot * rows : (slot + 1) * rows, :] = grad[
                    :, part * tile : (part + 1) * tile
                ].astype(BF16)
        for part in range(per_shard):
            tile_copy(spot + part, 0).start()
        return carry

    lax.fori_loop(0, hops, row_block, 0)
    band = own // places
    turned[:own, :] = act[...].T

    def down_block(index, carry):
        left = turned[pl.ds(pl.multiple_of(index * 4 * band, 16), 4 * band), :]
        grad = nn(left, cots[...])
        for part in range(4):
            for split in range(width // tile):
                start = 2 * rows + split * band
                tiles[4 * index + part, start : start + band, :] = grad[
                    part * band : (part + 1) * band, split * tile : (split + 1) * tile
                ].astype(BF16)
            tile_copy(4 * index + part, 1).start()
        return carry

    lax.fori_loop(0, places // 4, down_block, 0)
    for copy in outs:
        copy.wait()
    for spot in range(places):
        for slot in range(2):
            tile_copy(spot, slot).wait()


def normed_back_kernel(gate_ref, up_ref, gate_mat_ref, up_mat_ref, *outs):
    count = outs[0].shape[0]
    for index, out in enumerate(outs):
        span = slice(index * count, (index + 1) * count)
        out[...] = (
            nt(gate_ref[span, :], gate_mat_ref[...]) + nt(up_ref[span, :], up_mat_ref[...])
        ).astype(BF16)


def widen_kernel(
    ids_ref,
    gate_up_ref,
    down_in_ref,
    mixed_ref,
    gate_ref,
    up_ref,
    down_ref,
    query_ref,
    out_ref,
    stack,
    *,
    rows,
):
    step = pl.program_id(0)
    several, _, tile = gate_up_ref.shape
    band = down_ref.shape[0] // several
    share = mixed_ref.shape[1]
    for part in range(several):
        span = slice(part * tile, (part + 1) * tile)
        gate_ref[:, span] = gate_up_ref[part, :rows, :].astype(F32)
        up_ref[:, span] = gate_up_ref[part, rows:, :].astype(F32)
        for split in range(down_ref.shape[1] // tile):
            down_ref[part * band : (part + 1) * band, split * tile : (split + 1) * tile] = (
                down_in_ref[part, split * band : (split + 1) * band, :].astype(F32)
            )
        start = pl.multiple_of((step * several + part) * share, 8)
        stack[pl.ds(start, share), :] = mixed_ref[part].astype(F32)

    @pl.when(step == pl.num_programs(0) - 1)
    def _():
        cuts = query_ref.shape[1] // tile
        for cut in range(cuts):
            span = slice(cut * tile, (cut + 1) * tile)
            query_ref[:, span] = stack[cut * rows : (cut + 1) * rows, :]
            out_ref[:, span] = stack[(cuts + cut) * rows : (cuts + cut + 1) * rows, :]


def on_device(
    inputs,
    gain_attn,
    w_query,
    w_key,
    w_value,
    w_out,
    gain_mlp,
    w_gate,
    w_up,
    w_down,
    cotangent,
    *,
    n_ctx,
    n_shard,
):
    x = inputs[0]
    cot = cotangent[0]
    count, width = x.shape
    rows, qw = w_query.shape
    kvw = w_key.shape[1]
    ff_own = w_down.shape[0]
    ff = w_gate.shape[1]
    groups = kvw // HEAD
    per = qw // kvw
    blocks = n_ctx
    per_shard = n_ctx // n_shard
    tile = ff_own // per_shard
    assert count == BLOCK and n_shard == 4 and n_ctx % 2 == 0 and ff_own * n_shard == ff
    aligned = tile % LANES == 0
    order = ring_order(n_ctx)
    places = [order.index(index) for index in range(n_ctx)]
    shard = lax.axis_index("shard")
    ctx = lax.axis_index("ctx")

    def after(value, done):
        return lax.optimization_barrier((value, done))[0]

    def hop(value, distance):
        pairs = [(index, index ^ distance) for index in range(n_shard)]
        return lax.ppermute(value, "shard", pairs)

    def ctx_hop(value, distance):
        pairs = [(index, index ^ distance) for index in range(n_ctx)]
        return lax.ppermute(value, "ctx", pairs)

    def gather(value, done):
        far = hop(after(value, done), 2)
        return [value, hop(value, 1), far, hop(far, 1)]

    def halves(parts):
        third = hop(parts[3], 1)
        first = hop(parts[1], 1)
        across = (parts[2].astype(F32) + third.astype(F32)).astype(BF16)
        return parts[0], first, across

    def reduce(parts):
        own, first, across = halves(parts)
        return [own, first, hop(across, 2)]

    def add(parts):
        return sum(part.astype(F32) for part in parts)

    def scatter(value):
        return lax.psum_scatter(
            value, "ctx", scatter_dimension=0, axis_index_groups=[order], tiled=False
        )

    def collect(value):
        return lax.all_gather(value, "ctx", axis=0, axis_index_groups=[order], tiled=True)

    lane = jnp.arange(LANES, dtype=jnp.int32)
    frequency = jnp.exp((lane % (HEAD // 2)).astype(F32) * (-2.0 * math.log(10000.0) / HEAD))
    positions = (ctx * count + jnp.arange(count, dtype=jnp.int32)).astype(F32)
    angles = positions[:, None] * frequency[None, :]
    cosine = jnp.cos(angles)
    sine = jnp.where(lane % HEAD < HEAD // 2, -1.0, 1.0)[None, :] * jnp.sin(angles)

    gains = jnp.concatenate([gain_attn, gain_mlp])
    gain_rows = jnp.zeros((16, 2 * kvw), BF16).at[0, : 2 * rows].set(gains)
    kv_own = jnp.concatenate([jnp.concatenate([w_key, w_value], axis=1), gain_rows], axis=0)
    far = hop(kv_own, 2)
    kv_weights = [kv_own, hop(kv_own, 1), far, hop(far, 1)]
    ids = jnp.stack([shard, ctx]).astype(jnp.int32)
    sizes = (rows,) * n_shard


    half = rows // 2
    lanes = 4 * ff_own // n_ctx
    spot = ring_place(ctx, n_ctx)

    def columns(peer):
        start = peer * ff_own
        return jnp.concatenate(
            [
                lax.dynamic_slice_in_dim(w_gate, start, ff_own, 1),
                lax.dynamic_slice_in_dim(w_up, start, ff_own, 1),
            ],
            axis=1,
        )

    def far_columns(peer):
        column = peer * ff_own + lax.rem(spot // 2 * lanes, ff_own)
        cuts = [
            lax.dynamic_slice(mat, (spot % 2 * half, column), (half, lanes))
            for mat in (w_gate, w_up)
        ]
        return jnp.where(spot // 2 * lanes < ff_own, cuts[0], cuts[1])

    near_columns = columns(shard ^ 1)
    far_cut = jnp.concatenate([far_columns(shard ^ distance) for distance in (2, 3)], axis=0)
    query_own = jnp.concatenate([w_query, far_cut], axis=1)
    cosine, sine, ids, near_columns, query_own = lax.optimization_barrier(
        (cosine, sine, ids, near_columns, query_own)
    )
    query_weights = gather(query_own, far)
    out_far = hop(after(w_out, query_weights[2]), 2)
    fetch_sems = pltpu.SemaphoreType.DMA((n_shard,))
    hidden, kv, gain_one, gain_two = call_once(
        functools.partial(keys_kernel, sizes=sizes, kvw=kvw),
        [((count, width), BF16), ((count, 2 * kvw), BF16), ((1, width), F32), ((1, width), F32)],
        [x, cosine, sine],
        held=[ids],
        moved=kv_weights,
        scratch=[
            pltpu.VMEM((width, 2 * kvw), BF16),
            pltpu.VMEM((n_shard, 16, 2 * kvw), BF16),
            fetch_sems,
            fetch_sems,
        ],
        flops=4 * count * width * kvw,
        limit=ALL_VMEM,
        name="keys",
    )
    all_kv = collect(kv)

    (queries,) = call_once(
        functools.partial(queries_kernel, sizes=sizes),
        [((count, qw), BF16)],
        [hidden, cosine, sine],
        held=[ids],
        moved=query_weights,
        scratch=[pltpu.VMEM((width, qw), BF16), fetch_sems],
        flops=2 * count * width * qw,
        name="queries",
    )
    out_weights = [w_out, hop(w_out, 1), out_far, hop(after(out_far, queries), 1)]
    far_tile = jnp.concatenate(
        [query_weights[2][:half, qw:], query_weights[3][half:, qw:]], axis=0
    )
    far_rows = collect(after(far_tile, kv)[None])
    near_part = hop(near_columns, 1)
    cot_near = hop(cot, 1)
    cot_far = hop(after(cot, (out_weights[2], queries)), 2)

    shared = dict(sizes=sizes, column=0, groups=groups, per=per, blocks=blocks)
    fixed = lambda *shape: pl.BlockSpec(shape, lambda step, table: (0,) * len(shape))
    kv_spec = pl.BlockSpec(
        (count, 2 * kvw), lambda step, table: (ring_place(jnp.minimum(step, table[1]), blocks), 0)
    )
    once = lambda *shape: block(shape)
    weight_specs = [HBM_SPEC] * len(sizes)
    span = per * count
    out_tall, attended, log_total, mid, normed, q_cols = pl.pallas_call(
        functools.partial(attend_kernel, **shared),
        out_shape=(
            jax.ShapeDtypeStruct((qw, count), F32),
            jax.ShapeDtypeStruct((count, qw), BF16),
            jax.ShapeDtypeStruct((8, span), F32),
            jax.ShapeDtypeStruct((count, width), F32),
            jax.ShapeDtypeStruct((count, width), BF16),
            jax.ShapeDtypeStruct((groups, HEAD, span), BF16),
        ),
        grid_spec=pltpu.PrefetchScalarGridSpec(
            num_scalar_prefetch=1,
            grid=(blocks,),
            in_specs=[once(count, qw), kv_spec, once(count, width), once(1, width)]
            + weight_specs,
            out_specs=[
                fixed(qw, count),
                fixed(count, qw),
                fixed(8, span),
                fixed(count, width),
                fixed(count, width),
                fixed(groups, HEAD, span),
            ],
            scratch_shapes=[
                pltpu.VMEM((groups, HEAD, span), F32),
                pltpu.VMEM((8, span), F32),
                pltpu.VMEM((8, span), F32),
                pltpu.VMEM((qw, width), BF16),
                pltpu.VMEM((2, count, span), F32),
                pltpu.VMEM((qw, count), F32),
                pltpu.SemaphoreType.DMA((len(sizes),)),
            ],
        ),
        compiler_params=params(),
        cost_estimate=cost(
            4 * count * count * blocks * qw, 12e6, count * count * blocks * groups * per
        ),
        name="attend",
    )(ids, queries, all_kv, x, gain_two, *out_weights)

    normed_far = hop(normed, 2)
    normed_near = hop(normed, 1)
    cot_far = after(cot_far, normed)
    far_rows = after(far_rows, normed)
    all_count = n_shard * count
    if aligned:
        two = ((2, count, ff_own), BF16)
        mats = [((width, ff_own), BF16)] * 2
        pair = (2, count, width)
        gate_mat, up_mat, *near_units, back = pl.pallas_call(
            functools.partial(feed_near_kernel, half=half, lanes=lanes),
            out_shape=tuple(
                jax.ShapeDtypeStruct(*out) for out in [*mats, two, two, two, (pair, BF16)]
            ),
            in_specs=[SMEM_SPEC] + [HBM_SPEC] * 9,
            out_specs=(HBM_SPEC,) * 6,
            scratch_shapes=[
                pltpu.VMEM((width, ff_own), BF16),
                pltpu.VMEM((width, ff_own), BF16),
                pltpu.VMEM((ff_own, width), BF16),
                pltpu.VMEM(pair, BF16),
                pltpu.VMEM(pair, BF16),
                pltpu.VMEM(*two),
                pltpu.VMEM(*two),
                pltpu.VMEM(*two),
                pltpu.VMEM(pair, BF16),
                pltpu.SemaphoreType.DMA((4 + 2 * n_ctx,)),
                pltpu.SemaphoreType.DMA((3, 2)),
                pltpu.SemaphoreType.DMA((6,)),
            ],
            compiler_params=params(),
            cost_estimate=cost(10 * 2 * count * width * ff_own, 12e6),
            name="feed_near",
        )(
            ids,
            w_gate,
            w_up,
            near_part,
            far_rows,
            w_down,
            normed,
            normed_near,
            cot,
            cot_near,
        )
        normed_far, cot_far = lax.optimization_barrier((normed_far, cot_far, back))[:2]
        normed_pieces = [normed, normed_near, normed_far, hop(normed_far, 1)]
        cot_pieces = [cot, cot_near, cot_far, hop(cot_far, 1)]
        late = ((2 * count, ff_own), BF16)
        feed_tiles, *far_units = pl.pallas_call(
            functools.partial(feed_far_kernel, per_shard=per_shard),
            out_shape=tuple(
                jax.ShapeDtypeStruct(*out)
                for out in [((n_ctx, 3 * rows, tile), BF16), late, late, late]
            ),
            in_specs=[SMEM_SPEC] + [HBM_SPEC] * (6 + 2 * n_shard),
            out_specs=(HBM_SPEC,) * 4,
            scratch_shapes=[
                pltpu.VMEM((width, ff_own), BF16),
                pltpu.VMEM((width, ff_own), BF16),
                pltpu.VMEM((ff_own, width), BF16),
                pltpu.VMEM((n_shard, count, width), BF16),
                pltpu.VMEM((all_count, width), BF16),
                pltpu.VMEM((width, all_count), BF16),
                pltpu.VMEM((all_count, ff_own), BF16),
                pltpu.VMEM((all_count, ff_own), BF16),
                pltpu.VMEM((all_count, ff_own), BF16),
                pltpu.VMEM((n_ctx, 3 * rows, tile), BF16),
                pltpu.SemaphoreType.DMA((3,)),
                pltpu.SemaphoreType.DMA((n_shard,)),
                pltpu.SemaphoreType.DMA((n_shard,)),
                pltpu.SemaphoreType.DMA((3, 2)),
                pltpu.SemaphoreType.DMA((3,)),
                pltpu.SemaphoreType.DMA((2, n_ctx)),
            ],
            compiler_params=params(),
            cost_estimate=cost(9 * all_count * width * ff_own, 25e6),
            name="feed_far",
        )(
            ids, gate_mat, up_mat, w_down, *near_units, *normed_pieces, *cot_pieces
        )
        to_own, to_near = back[0], back[1]
        act_parts = [near_units[0].reshape(2 * count, ff_own), far_units[0]]
        grad_gate_far, grad_up_far = far_units[1:]
    else:
        normed_pieces = [normed, normed_near, normed_far, hop(normed_far, 1)]
        cot_pieces = [cot, cot_near, cot_far, hop(cot_far, 1)]
        tiles_of = far_rows.reshape(n_ctx // 2, 2, 2, half, lanes)
        tiles_of = tiles_of.transpose(2, 1, 3, 0, 4).reshape(2, rows, 2 * ff_own)
        gate_mat = jnp.zeros((width, ff_own), BF16)
        up_mat = jnp.zeros((width, ff_own), BF16)
        for part, start in zip(
            (columns(shard), near_part, tiles_of[0], tiles_of[1]),
            [(shard ^ k) * rows for k in range(n_shard)],
        ):
            gate_mat = lax.dynamic_update_slice_in_dim(gate_mat, part[:, :ff_own], start, 0)
            up_mat = lax.dynamic_update_slice_in_dim(up_mat, part[:, ff_own:], start, 0)
        all_cot = jnp.concatenate(cot_pieces, axis=0)
        all_normed = jnp.concatenate(normed_pieces, axis=0)
        gate = nn(all_normed, gate_mat)
        up = nn(all_normed, up_mat)
        grad_activated = nt(all_cot, w_down)
        sigmoid = jax.nn.sigmoid(gate)
        activated = (gate * sigmoid * up).astype(BF16)
        grad_gate = (grad_activated * up * (sigmoid * (1.0 + gate * (1.0 - sigmoid)))).astype(BF16)
        grad_up = (grad_activated * (gate * sigmoid)).astype(BF16)

        def tiles(grad):
            pieces = grad.astype(BF16).reshape(n_shard, rows, per_shard, tile)
            pieces = pieces.transpose(0, 2, 1, 3)
            return jnp.roll(pieces, shard, axis=0).reshape(n_ctx, rows, tile)

        down = tn(activated, all_cot).astype(BF16)
        down = down.reshape(n_ctx, ff_own // n_ctx, width // tile, tile).transpose(0, 2, 1, 3)
        feed_tiles = jnp.concatenate(
            [
                tiles(tn(all_normed, grad_gate)),
                tiles(tn(all_normed, grad_up)),
                down.reshape(n_ctx, rows, tile),
            ],
            axis=1,
        )
        grad_gate_far, grad_up_far = grad_gate[2 * count :], grad_up[2 * count :]
        back = nt(grad_gate[: 2 * count], gate_mat) + nt(grad_up[: 2 * count], up_mat)
        to_own, to_near = back[:count].astype(BF16), back[count:].astype(BF16)
        act_parts = [activated[: 2 * count], activated[2 * count :]]
    from_near = hop(to_near, 1)
    feed_sum = scatter(feed_tiles)
    head_sum = feed_sum[2 * rows : 2 * rows + 16]
    pairs = []
    for index in range(n_ctx):
        for source in range(n_shard):
            target = (places[index] // per_shard - source) % n_shard
            pairs.append((index * n_shard + source, index * n_shard + target))
    gate_up_sum = lax.ppermute(feed_sum[: 2 * rows], ("ctx", "shard"), pairs)

    to_far, to_third = call_once(
        normed_back_kernel,
        [((count, width), BF16)] * 2,
        [grad_gate_far, grad_up_far, gate_mat, up_mat],
        flops=8 * count * width * ff_own,
        limit=ALL_VMEM,
        name="normed_back",
    )
    third = hop(to_third, 1)
    across = (to_far.astype(F32) + third.astype(F32)).astype(BF16)
    from_far = hop(across, 2)

    part_out = [after(nn(part, w_down).astype(BF16), from_far) for part in act_parts]
    part_out = [part[k * count : (k + 1) * count] for part in part_out for k in range(2)]
    output = (mid + add(reduce(part_out))).astype(BF16)[None]

    place_spec = pl.BlockSpec(
        (count, 2 * kvw), lambda step, table: (ring_place(step, blocks), 0)
    )
    grad_query, grad_kv, branch, grad_mid, gain_two_part = pl.pallas_call(
        functools.partial(attend_back_kernel, **shared),
        out_shape=(
            jax.ShapeDtypeStruct((count, qw), BF16),
            jax.ShapeDtypeStruct((blocks * count, 2 * kvw), BF16),
            jax.ShapeDtypeStruct((count, width), BF16),
            jax.ShapeDtypeStruct((count, width), F32),
            jax.ShapeDtypeStruct((1, width), F32),
        ),
        grid_spec=pltpu.PrefetchScalarGridSpec(
            num_scalar_prefetch=1,
            grid=(blocks,),
            in_specs=[
                kv_spec,
                once(groups, HEAD, span),
                once(qw, count),
                once(8, span),
                once(count, width),
                once(1, width),
                once(count, width),
                once(count, width),
                once(count, width),
                once(count, width),
                once(count, LANES),
                once(count, LANES),
            ]
            + weight_specs,
            out_specs=[
                fixed(count, qw),
                place_spec,
                fixed(count, width),
                fixed(count, width),
                fixed(1, width),
            ],
            scratch_shapes=[
                pltpu.VMEM((qw, width), BF16),
                pltpu.VMEM((groups, HEAD, span), BF16),
                pltpu.VMEM((8, span), F32),
                pltpu.VMEM((groups, HEAD, span), F32),
                pltpu.VMEM((2, 2, count, span), F32),
                pltpu.VMEM((qw, count), F32),
                pltpu.SemaphoreType.DMA((len(sizes),)),
            ],
        ),
        compiler_params=params(),
        cost_estimate=cost(
            10 * count * count * blocks * qw, 14e6, count * count * blocks * groups * per
        ),
        name="attend_back",
    )(
        ids,
        all_kv,
        q_cols,
        out_tall,
        log_total,
        mid,
        gain_two,
        cot,
        to_own,
        from_near,
        from_far,
        cosine,
        sine,
        *out_weights,
    )
    grad_kv, head_sum = lax.optimization_barrier((grad_kv, head_sum))
    own_kv = scatter(grad_kv.reshape(n_ctx, count, 2 * kvw))

    def stack(parts, breadth, name):
        height = sum(part.shape[0] * part.shape[1] for part in parts[::3]) // breadth
        if breadth % LANES:
            wide = jnp.concatenate(
                [add(parts[index : index + 3]) for index in range(0, len(parts), 3)], axis=1
            )
            wide = wide.astype(BF16).reshape(rows, -1, breadth)
            return wide.transpose(1, 0, 2).reshape(height, breadth)
        return call_once(stack_kernel, [((height, breadth), BF16)], parts, flops=1e6, name=name)[0]

    grad_blocks = call_once(
        weight_grads_kernel,
        [((rows, qw), BF16)] * n_shard + [((rows, width), BF16)] * n_shard,
        [hidden, grad_query, attended, branch],
        held=[ids],
        scratch=[pltpu.VMEM((width, qw), F32)],
        flops=4 * count * width * qw,
        limit=ALL_VMEM,
        name="weight_grads",
    )
    parts_query = reduce(grad_blocks[:n_shard])
    parts_out = reduce(grad_blocks[n_shard:])
    mixed = stack(parts_query + parts_out, tile, "stack_mixed")
    mixed_sum = scatter(after(mixed, own_kv).reshape(n_ctx, -1, tile))

    grad_kv_pre, *kv_blocks = call_once(
        functools.partial(kv_back_kernel, kvw=kvw),
        [((count, 2 * kvw), BF16)] + [((rows, 2 * kvw), BF16)] * n_shard,
        [own_kv, cosine, sine, hidden],
        held=[ids],
        scratch=[pltpu.VMEM((width, 2 * kvw), F32)],
        flops=4 * count * width * kvw,
        name="kv_back",
    )
    sum_kv = stack(reduce(kv_blocks), LANES, "stack_kv").reshape(n_ctx, -1, LANES)
    shares = jnp.concatenate(
        [gate_up_sum, head_sum, feed_sum[2 * rows + 16 :], jnp.zeros_like(mixed_sum)]
    )
    shares = lax.dynamic_update_slice_in_dim(after(shares, sum_kv), mixed_sum, 3 * rows, 0)
    gathered = collect(shares[None])

    def exchange(value):
        return lax.all_to_all(value, "ctx", split_axis=0, concat_axis=0, tiled=True)

    own_sum = jnp.sum(exchange(sum_kv).astype(F32), axis=0, keepdims=True).astype(BF16)
    both = exchange(jnp.broadcast_to(own_sum, sum_kv.shape))
    both = both.reshape(2 * kvw // LANES, rows, LANES).transpose(1, 0, 2).reshape(rows, 2 * kvw)
    grad_w_key = both[:, :kvw].astype(F32)
    grad_w_value = both[:, kvw:].astype(F32)

    grad_x, gain_one_part = call_once(
        functools.partial(inputs_kernel, sizes=sizes),
        [((count, width), BF16), ((1, width), F32)],
        [grad_query, grad_kv_pre, x, gain_one, grad_mid],
        held=[ids],
        moved=[*query_weights, *kv_weights],
        scratch=[
            pltpu.VMEM((width, qw), BF16),
            pltpu.VMEM((width, 2 * kvw), BF16),
            pltpu.VMEM((count, width), F32),
            fetch_sems,
            fetch_sems,
        ],
        flops=2 * count * width * (qw + 2 * kvw),
        name="grad_inputs",
    )

    gain_parts = jnp.concatenate([gain_one_part, gain_two_part], axis=0)
    for distance in [1 << bit for bit in range(n_shard.bit_length() - 1)]:
        gain_parts = gain_parts + hop(gain_parts, distance)
    for distance in [1 << bit for bit in range(n_ctx.bit_length() - 1)]:
        gain_parts = gain_parts + ctx_hop(gain_parts, distance)
    own_gains = lax.dynamic_slice_in_dim(gain_parts, shard * rows, rows, 1)

    if aligned:
        share = mixed_sum.shape[0]
        rolled = lambda step, where: (lax.rem(step + where[0], n_shard), 0, 0)
        band = ff_own // n_ctx
        grad_w_gate, grad_w_up, grad_w_down, grad_w_query, grad_w_out = pl.pallas_call(
            functools.partial(widen_kernel, rows=rows),
            out_shape=(
                jax.ShapeDtypeStruct((rows, ff), F32),
                jax.ShapeDtypeStruct((rows, ff), F32),
                jax.ShapeDtypeStruct((ff_own, width), F32),
                jax.ShapeDtypeStruct((rows, qw), F32),
                jax.ShapeDtypeStruct((rows, width), F32),
            ),
            grid_spec=pltpu.PrefetchScalarGridSpec(
                num_scalar_prefetch=1,
                grid=(n_shard,),
                in_specs=[
                    pl.BlockSpec((per_shard, 2 * rows, tile), rolled),
                    pl.BlockSpec((per_shard, rows, tile), lambda step, where: (step, 2, 0)),
                    pl.BlockSpec(
                        (per_shard, share, tile),
                        lambda step, where: (step, 3 * rows // share, 0),
                    ),
                ],
                out_specs=[
                    pl.BlockSpec((rows, ff_own), lambda step, where: (0, step)),
                    pl.BlockSpec((rows, ff_own), lambda step, where: (0, step)),
                    pl.BlockSpec((per_shard * band, width), lambda step, where: (step, 0)),
                    pl.BlockSpec((rows, qw), lambda step, where: (0, 0)),
                    pl.BlockSpec((rows, width), lambda step, where: (0, 0)),
                ],
                scratch_shapes=[pltpu.VMEM((n_ctx * share, tile), F32)],
            ),
            compiler_params=params(),
            cost_estimate=cost(1e6, 20e6),
            name="widen",
        )(ids, gathered, gathered, gathered)
    else:

        def untile(part):
            back = jnp.roll(part.reshape(n_shard, per_shard, rows, tile), -shard, axis=0)
            back = back.reshape(n_ctx, rows, tile).transpose(1, 0, 2)
            return back.reshape(rows, ff).astype(F32)

        grad_w_gate = untile(gathered[:, :rows])
        grad_w_up = untile(gathered[:, rows : 2 * rows])
        down = gathered[:, 2 * rows : 3 * rows].reshape(n_ctx, width // tile, -1, tile)
        grad_w_down = down.transpose(0, 2, 1, 3).reshape(ff_own, width).astype(F32)
        wide = gathered[:, 3 * rows :].reshape(2 * qw // tile, rows, tile).transpose(1, 0, 2)
        wide = wide.reshape(rows, 2 * qw).astype(F32)
        grad_w_query, grad_w_out = wide[:, :qw], wide[:, qw:]

    return (
        output,
        grad_x[None],
        own_gains[0],
        grad_w_query,
        grad_w_key,
        grad_w_value,
        grad_w_out,
        own_gains[1],
        grad_w_gate,
        grad_w_up,
        grad_w_down,
    )


def solution(mesh):
    tokens = P("shard", "ctx", None)
    split = P("shard", None)
    gain = P("shard")
    placed = (tokens, gain, split, split, split, split, gain, split, split, split, tokens)
    return jax.shard_map(
        functools.partial(on_device, n_ctx=mesh.shape["ctx"], n_shard=mesh.shape["shard"]),
        mesh=mesh,
        in_specs=placed,
        out_specs=(tokens, tokens, gain, split, split, split, split, gain, split, split, split),
        check_vma=False,
    )
```
